32 devices in a mesh: dp: 8 (over z, x), narrow: 4 (over y, core).
Axes of the slice: x: 2, y: 2, z: 4, core: 2. Of those that a mesh axis runs over, the one named last changes fastest.
Arguments:
- wave: float32 [1313280], P(('dp', 'narrow')), may hold values from -6 to 6
- clip_ids: int32 [4096], P(('dp', 'narrow')), may hold values from 0 to 95, never falling along the last dimension, each value on 1 to 128 neighbouring positions
- span_starts: int32 [4096], P(('dp', 'narrow')), may hold values 0 or 1
- step_count: int32 [1], replicated, may hold values from 2 to 20
- conv_small: float32 [12, 512], replicated, as said below
- conv_stack: float32 [8192, 512], P(('dp', 'narrow')), may hold values from -0.25 to 0.25
- side: float32 [768, 2192], P('dp', 'narrow'), may hold values from -0.21875 to 0.21875
- vectors: float32 [10, 768], replicated, as said below
- block: float32 [3, 768, 3072], P(None, 'dp', 'narrow')
- teacher_block: float32 [3, 768, 3072], P(None, 'dp', 'narrow')
- teacher_vectors: float32 [10, 768], replicated, as said below
- small_mean: float32 [12, 512], replicated, may hold values from -4.4428212e-05 to 4.4428212e-05
- small_square: float32 [12, 512], replicated, may hold values from 1.2336662e-10 to 4.934665e-10
- stack_mean: float32 [8192, 512], P(('dp', 'narrow')), may hold values from -1.1107053e-05 to 1.1107053e-05
- stack_square: float32 [8192, 512], P(('dp', 'narrow')), may hold values from 7.710414e-12 to 3.0841656e-11
- side_mean: float32 [768, 2192], P('dp', 'narrow'), may hold values from -1.1107053e-05 to 1.1107053e-05
- side_square: float32 [768, 2192], P('dp', 'narrow'), may hold values from 7.710414e-12 to 3.0841656e-11
- vector_mean: float32 [10, 768], replicated, may hold values from -4.4428212e-05 to 4.4428212e-05
- vector_square: float32 [10, 768], replicated, may hold values from 1.2336662e-10 to 4.934665e-10
- block_momentum: float32 [3, 768, 3072], P(None, 'dp', 'narrow'), may hold values from -1.1107053e-05 to 1.1107053e-05
Outputs:
- loss: float32 [], replicated
- grad_norm: float32 [], replicated
- conv_small_next: float32 [12, 512], replicated
- small_mean_next: float32 [12, 512], replicated
- small_square_next: float32 [12, 512], replicated
- conv_stack_next: float32 [8192, 512], P(('dp', 'narrow'))
- stack_mean_next: float32 [8192, 512], P(('dp', 'narrow'))
- stack_square_next: float32 [8192, 512], P(('dp', 'narrow'))
- side_next: float32 [768, 2192], P('dp', 'narrow')
- side_mean_next: float32 [768, 2192], P('dp', 'narrow')
- side_square_next: float32 [768, 2192], P('dp', 'narrow')
- vectors_next: float32 [10, 768], replicated
- vector_mean_next: float32 [10, 768], replicated
- vector_square_next: float32 [10, 768], replicated
- block_next: float32 [3, 768, 3072], P(None, 'dp', 'narrow')
- momentum_next: float32 [3, 768, 3072], P(None, 'dp', 'narrow')
- teacher_block_next: float32 [3, 768, 3072], P(None, 'dp', 'narrow')
- teacher_vectors_next: float32 [10, 768], replicated
- block_copy: bfloat16 [3, 768, 3072], P(None, 'dp', 'narrow')
The draws below stay inside these ranges and needn't reach their ends.
Inputs may be any that keep to these rules, and one draw needn't show every extreme that they name: `clip_ids`: clip numbers never fall along the frames; a clip has 1 to 128 frames, and some clip has exactly 128. `conv_small`: rows 10 are positive gains. `vectors`: rows 0, 2, 4 are positive gains. `teacher_vectors`: rows 0, 2, 4 are positive gains.
All inputs are finite; a program needn't handle non-finite values. No bound on the sum of `span_starts` on one device may be relied on, other than what follows from the above.
Results may differ from the reference program's by a relative error of at most 0.0025.
The reference program's roundings to bfloat16 on the way count: a program that leaves them out, or rounds other values in their place, can miss the bound.
Values may be sent and summed in bfloat16 or wider, within the bound.
No kernel may reach another device: no remote copies, remote signals or barrier semaphores. Data moves between devices by JAX's collectives and lax.ppermute only.
A program may use at most 448 MiB of HBM per device.

```python
import math
import jax
import jax.numpy as jnp
import numpy as np
from jax import lax

D = 768
HEADS = 12
HEAD_DIM = 64
FF = 3072
CH = 512
GROUPS = 16
POS_K = 19
SPAN = 10
F_DEV = 128
SAMP = 41040
FRAMES = 4096
WAVE = 1313280
CLIPS = 96
STACK = 8192
SIDE_COLS = 2192
PARAMS = 12969472
N_DP = 8
DEVICES = 32


def gains_and_biases(key):
    gain_rows = jnp.exp(jax.random.uniform(jax.random.fold_in(key, 1), (10, D), jnp.float32, -0.7, 0.7))
    bias_rows = 0.3 * jax.random.normal(jax.random.fold_in(key, 2), (10, D), jnp.float32)
    mask_rows = jax.random.normal(jax.random.fold_in(key, 3), (10, D), jnp.float32)
    row_index = jnp.arange(10)[:, None]
    is_gain = (row_index == 0) | (row_index == 2) | (row_index == 4)
    return jnp.where(is_gain, gain_rows, jnp.where(row_index == 9, mask_rows, bias_rows))


def draw_vectors(key, part):
    return gains_and_biases(jax.random.fold_in(key, 11))


def draw_teacher_vectors(key, part):
    return gains_and_biases(jax.random.fold_in(key, 12))


def block_like(key):
    values = jax.random.normal(key, (3, D, FF), jnp.float32)
    columns = jnp.arange(FF)[None, None, :]
    matrix_index = jnp.arange(3)[:, None, None]
    scales = jnp.where(matrix_index == 2, FF ** (-0.5), jnp.where((matrix_index == 0) & (columns >= 3 * D), 4.0 * D ** (-0.5), D ** (-0.5)))
    return values * scales


def draw_block(key, part):
    return block_like(jax.random.fold_in(key, 21))


def draw_teacher_block(key, part):
    return block_like(jax.random.fold_in(key, 22))


def draw_conv_small(key, part):
    tap_rows = jax.random.normal(jax.random.fold_in(key, 31), (10, CH), jnp.float32) * 10.0 ** (-0.5)
    gain_row = jnp.exp(jax.random.uniform(jax.random.fold_in(key, 32), (1, CH), jnp.float32, -0.7, 0.7))
    shift_row = 0.3 * jax.random.normal(jax.random.fold_in(key, 33), (1, CH), jnp.float32)
    return jnp.concatenate([tap_rows, gain_row, shift_row], axis=0)


def set_ends(array, own_key, smallest, largest):
    shape = array.shape
    place = [jax.random.randint(jax.random.fold_in(own_key, axis), (), 0, shape[axis]) for axis in range(len(shape))]
    array = array.at[tuple(place)].set(smallest)
    longest = shape.index(max(shape))
    place[longest] = (place[longest] + 1) % shape[longest]
    return array.at[tuple(place)].set(largest)


def levels(rng, extent, pieces, low, high):
    factor_of = 1.0
    for dim, blocks in pieces:
        steps = jax.random.uniform(jax.random.fold_in(jax.random.fold_in(rng, 6), dim), (blocks,), jnp.float32, low / len(pieces), high / len(pieces))
        factor_of = factor_of * jnp.repeat(jnp.exp(steps), extent[dim] // blocks).reshape((-1,) + (1,) * (len(extent) - 1 - dim))
    return factor_of


def profile(count, total, most, lean):
    weights = [(1 << 20) // math.isqrt(grade ** lean) + 1 for grade in range(2, count + 1)]
    rest, holding = total - most - (count - 1), [1] * (count - 1)
    while rest > 0:
        movable = [i for i in range(count - 1) if holding[i] < most]
        mass, budget = sum([weights[i] for i in movable]), rest
        for i in movable:
            addition = min(most - holding[i], max(1, budget * weights[i] // mass), rest)
            holding[i] = holding[i] + addition
            rest = rest - addition
    return np.array([most] + holding)


def uneven(own_key, number_of, total, bound, skew):
    if number_of == 2:
        one = jax.random.randint(own_key, (), max(1, total - bound), min(bound, total - 1) + 1)
        return jnp.stack([one, total - one])
    tallies = jnp.asarray(profile(number_of, total, bound, skew), jnp.int32)
    twos = (number_of - 1) // 2
    donor, receiver = tallies[1:1 + 2 * twos:2], tallies[2:2 + 2 * twos:2]
    slack = jnp.minimum(donor - 1, bound - receiver)
    passed = jax.random.randint(jax.random.fold_in(own_key, 1), (twos,), 0, 1 << 20) % (slack + 1)
    tallies = tallies.at[1:1 + 2 * twos:2].set(donor - passed).at[2:2 + 2 * twos:2].set(receiver + passed)
    return tallies[jax.random.permutation(jax.random.fold_in(own_key, 2), number_of)]


def noise(key, shape, scale, most, shards=(), held_as=jnp.bfloat16):
    entries = jax.random.normal(key, shape, jnp.float32) * scale
    if len(shards) > 0:
        entries = levels(key, shape, shards, -0.22, 0.18) * entries
    return jnp.clip(entries, min=-most, max=most).astype(held_as)


def setup_inputs(seed: int = 0) -> dict:
    streams_of = jax.random.split(jax.random.key(seed), 21)
    return {
        "wave": noise(streams_of[0], (WAVE,), 1.0, 6.0, ((0, 32),), jnp.float32),
        "clip_ids": jnp.searchsorted(jnp.cumsum(uneven(streams_of[1], CLIPS, FRAMES, F_DEV, 2)), jnp.arange(FRAMES), side="right").astype(jnp.int32),
        "span_starts": set_ends((jax.random.randint(streams_of[2], (FRAMES,), 0, 200) < 13).astype(jnp.int32), jax.random.fold_in(streams_of[2], 1), 0, 1),
        "step_count": jax.random.randint(streams_of[3], (1,), 2, 21).astype(jnp.int32),
        "conv_small": draw_conv_small(jax.random.fold_in(streams_of[20], 71), 0),
        "conv_stack": noise(streams_of[5], (STACK, CH), CH ** -0.5, 0.25, ((0, 32),), jnp.float32),
        "side": noise(streams_of[6], (D, SIDE_COLS), D ** -0.5, 0.21875, ((0, 8), (1, 4)), jnp.float32),
        "vectors": draw_vectors(jax.random.fold_in(streams_of[20], 71), 0),
        "block": draw_block(jax.random.fold_in(streams_of[20], 71), 0),
        "teacher_block": draw_teacher_block(jax.random.fold_in(streams_of[20], 71), 0),
        "teacher_vectors": draw_teacher_vectors(jax.random.fold_in(streams_of[20], 71), 0),
        "small_mean": noise(streams_of[11], (12, CH), (0.04 * PARAMS ** -0.5), 4.442821227712557e-05, (), jnp.float32),
        "small_square": jnp.clip(jnp.exp(jax.random.uniform(streams_of[12], (12, CH), jnp.float32, math.log(1.2336662247314223e-10), math.log(4.934664898925689e-10))), 1.2336662247314223e-10, 4.934664898925689e-10),
        "stack_mean": noise(streams_of[13], (STACK, CH), (0.01 * PARAMS ** -0.5), 1.1107053069281392e-05, ((0, 32),), jnp.float32),
        "stack_square": jnp.clip(jnp.exp(math.log(3.084165561828556e-11) - 1.3862944 * jax.random.uniform(streams_of[14], (STACK, CH), jnp.float32) ** levels(streams_of[14], (STACK, CH), ((0, 32),), -0.2, 0.2)), 7.71041390457139e-12, 3.084165561828556e-11),
        "side_mean": noise(streams_of[15], (D, SIDE_COLS), (0.01 * PARAMS ** -0.5), 1.1107053069281392e-05, ((0, 8), (1, 4)), jnp.float32),
        "side_square": jnp.clip(jnp.exp(math.log(3.084165561828556e-11) - 1.3862944 * jax.random.uniform(streams_of[16], (D, SIDE_COLS), jnp.float32) ** levels(streams_of[16], (D, SIDE_COLS), ((0, 8), (1, 4)), -0.2, 0.2)), 7.71041390457139e-12, 3.084165561828556e-11),
        "vector_mean": noise(streams_of[17], (10, D), (0.04 * PARAMS ** -0.5), 4.442821227712557e-05, (), jnp.float32),
        "vector_square": jnp.clip(jnp.exp(jax.random.uniform(streams_of[18], (10, D), jnp.float32, math.log(1.2336662247314223e-10), math.log(4.934664898925689e-10))), 1.2336662247314223e-10, 4.934664898925689e-10),
        "block_momentum": noise(streams_of[19], (3, D, FF), (0.01 * PARAMS ** -0.5), 1.1107053069281392e-05, ((1, 8), (2, 4)), jnp.float32),
    }


EPS = 1e-05
VAR_FLOOR = 0.1
CLIP_LIMIT = 0.01
LR_ADAM = 0.03
LR_MUON = 2.0
DECAY = 0.5
WEIGHT_DECAY = 0.01
EMA_RATE = 0.5
KERNELS = (3, 3, 3, 3, 2, 2)
COEFF_A = 3.4445
COEFF_B = -4.775
COEFF_C = 2.0315
HIGHEST = lax.Precision.HIGHEST

@jax.custom_vjp
def low(v):
    return lax.optimization_barrier(v.astype(jnp.bfloat16)).astype(jnp.float32)

@jax.custom_vjp
def low_back(v):
    return v

def low_keep(v):
    return (low(v), None)

def low_pass(kept, grad):
    return (grad,)

def back_keep(v):
    return (v, None)

def back_low(kept, grad):
    return (low(grad),)
low.defvjp(low_keep, low_pass)
low_back.defvjp(back_keep, back_low)

def bprod(left_side, right_side):
    return low_back(jnp.einsum('bmk,bkn->bmn', left_side, right_side, precision=HIGHEST))

def matmul(left_side, right_side):
    return bprod(left_side[None], right_side[None])[0]

def layer_norm(values, gain, shift):
    center = values - lax.optimization_barrier(jnp.mean(values, axis=-1, keepdims=True))
    spread = lax.optimization_barrier(jnp.mean(center * center, axis=-1, keepdims=True))
    return center * lax.rsqrt(spread + EPS) * gain + shift

def strided_taps(values, kernel, stride, rows_out):
    return jnp.concatenate([lax.slice_in_dim(values, offset, offset + stride * (rows_out - 1) + 1, stride, 0) for offset in range(kernel)], axis=1)

def encode(conv_small, conv_stack, side, vectors, wave):
    frames = (wave.shape[0] - 80) // 320
    length = 64 * frames + 15
    hidden = strided_taps(low(wave)[:, None], 10, 5, length)
    hidden = low(jax.nn.gelu(matmul(hidden, conv_small[:10]), approximate=False))
    row_offset = 0
    for kernel in KERNELS:
        length = (length - kernel) // 2 + 1
        tap_rows = strided_taps(hidden, kernel, 2, length)
        hidden = jax.nn.gelu(matmul(tap_rows, conv_stack[row_offset:row_offset + kernel * CH]), approximate=False)
        row_offset = row_offset + kernel * CH
        if row_offset < conv_stack.shape[0]:
            hidden = low(hidden)
    normed = low(layer_norm(hidden, conv_small[10], conv_small[11]))
    return matmul(normed, side[:, :CH].T) + vectors[6]

def neighbours(segment):
    frames = segment.shape[0]
    reach = POS_K // 2
    padded = jnp.pad(segment, (reach, reach), constant_values=-1)
    return jnp.stack([padded[offset:offset + frames] == segment for offset in range(POS_K)], 0).astype(jnp.float32)[:, :, None]

def masked_of(starts):
    frames = starts.shape[0]
    padded = jnp.pad(starts, (SPAN - 1, 0))
    return lax.optimization_barrier(jnp.max(jnp.stack([padded[offset:offset + frames] for offset in range(SPAN)], 0), axis=0)) > 0

def position(values, side, pos_bias, nearby):
    frames = values.shape[0]
    group_width = D // GROUPS
    reach = POS_K // 2
    padded = jnp.pad(low(values), ((reach, reach), (0, 0)))
    tap_rows = jnp.stack([padded[offset:offset + frames] for offset in range(POS_K)], 0) * nearby
    tap_rows = tap_rows.reshape(POS_K, frames, GROUPS, group_width).transpose(2, 1, 0, 3).reshape(GROUPS, frames, POS_K * group_width)
    kernel = side[:, CH:CH + POS_K * group_width].reshape(GROUPS, group_width, POS_K, group_width)
    kernel = kernel.transpose(0, 2, 1, 3).reshape(GROUPS, POS_K * group_width, group_width)
    mixed = bprod(tap_rows, kernel).transpose(1, 0, 2).reshape(frames, D)
    return jax.nn.gelu(mixed + pos_bias, approximate=False)

def transform(values, side, block, vectors, nearby, attend):
    frames = values.shape[0]
    hidden = layer_norm(values + position(values, side, vectors[7], nearby), vectors[0], vectors[1])
    triple = low(matmul(low(hidden), block[0][:, :3 * D]))
    heads = triple.reshape(frames, 3, HEADS, HEAD_DIM).transpose(1, 2, 0, 3)
    scores = bprod(heads[0], heads[1].transpose(0, 2, 1)) / math.sqrt(HEAD_DIM)
    scores = jnp.where(attend[None], scores, -1e+30)
    weights = low(jax.nn.softmax(scores, axis=-1))
    mixed = bprod(weights, heads[2]).transpose(1, 0, 2).reshape(frames, D)
    hidden = layer_norm(hidden + matmul(low(mixed), block[0][:, 3 * D:]), vectors[2], vectors[3])
    inner = low(jax.nn.gelu(matmul(low(hidden), block[1]), approximate=False))
    return layer_norm(hidden + matmul(inner, block[2].T), vectors[4], vectors[5])

def target_of(feats, side, teacher_block, teacher_vectors, nearby, attend):
    output = transform(feats, side, teacher_block, teacher_vectors, nearby, attend)
    member = attend.astype(jnp.float32)
    clip_size = lax.optimization_barrier(jnp.sum(member, axis=1, keepdims=True))
    average = jnp.dot(member, output, precision=HIGHEST) / clip_size
    center = output - average
    spread = jnp.dot(member, center * center, precision=HIGHEST) / clip_size
    return center * lax.rsqrt(jnp.maximum(spread, VAR_FLOOR))

def student_loss(feats, side, block, vectors, nearby, attend, masked, target, total):
    chosen = masked[:, None]
    values = jnp.where(chosen, vectors[9], feats)
    hidden = transform(values, side, block, vectors, nearby, attend)
    predict = matmul(low(hidden), side[:, CH + POS_K * (D // GROUPS):]) + vectors[8]
    error = jnp.where(chosen, predict - target, 0.0)
    return jnp.sum(error * error) / (total * math.sqrt(D))

def local_step(wave, segment, starts, conv_small, conv_stack, side, vectors, block, teacher_block, teacher_vectors, total):
    nearby = neighbours(segment)
    attend = segment[:, None] == segment[None, :]
    masked = masked_of(starts)
    feats, encode_back = jax.vjp(lambda small_part, stack_part, side_part, vector_part: encode(low(small_part), low(stack_part), low(side_part), low(vector_part), wave), conv_small, conv_stack, side, vectors)
    target = target_of(feats, low(side), low(teacher_block), low(teacher_vectors), nearby, attend)
    loss_part, student_back = jax.vjp(lambda feat_part, side_part, block_part, vector_part: student_loss(feat_part, low(side_part), low(block_part), low(vector_part), nearby, attend, masked, target, total), feats, side, block, vectors)
    feat_grad, side_two, block_grad, vector_two = student_back(jnp.ones_like(loss_part))
    small_grad, stack_grad, side_one, vector_one = encode_back(feat_grad)
    return (loss_part, small_grad, stack_grad, side_one + side_two, block_grad, vector_one + vector_two)

def adamw(weight, grad, first, second, power):
    first = DECAY * first + (1.0 - DECAY) * grad
    second = DECAY * second + (1.0 - DECAY) * grad * grad
    unbias = 1.0 - power
    step_size = first / unbias / (jnp.sqrt(second / unbias) + 1e-08)
    return (weight - LR_ADAM * (step_size + WEIGHT_DECAY * weight), first, second)

def orthogonal(matrix, row_blocks, gram_total):
    blocks = matrix.reshape(matrix.shape[0] * row_blocks, matrix.shape[1] // row_blocks, matrix.shape[2])
    for iteration in range(5):
        gram_matrix = gram_total(jnp.einsum('brc,bsc->brs', blocks, blocks, precision=HIGHEST))
        if iteration == 0:
            scales = 1.0 / (jnp.sqrt(jnp.trace(gram_matrix, axis1=1, axis2=2)) + 1e-07)
            blocks = blocks * scales[:, None, None]
            gram_matrix = gram_matrix * (scales * scales)[:, None, None]
        polynom = COEFF_B * gram_matrix + COEFF_C * jnp.einsum('brs,bst->brt', gram_matrix, gram_matrix, precision=HIGHEST)
        blocks = COEFF_A * blocks + jnp.einsum('brs,bsc->brc', polynom, blocks, precision=HIGHEST)
    return blocks.reshape(matrix.shape)

def apply_updates(factor, power, weights, grads, states, row_blocks, gram_total):
    small_weight, stack_weight, side_weight, vector_weight, block_weight, teacher_weight, teacher_vector = weights
    small_grad, stack_grad, side_grad, block_grad, vector_grad = grads
    small_next = adamw(small_weight, factor * small_grad, states[0], states[1], power)
    stack_next = adamw(stack_weight, factor * stack_grad, states[2], states[3], power)
    side_next = adamw(side_weight, factor * side_grad, states[4], states[5], power)
    vector_next = adamw(vector_weight, factor * vector_grad, states[6], states[7], power)
    momentum = DECAY * states[8] + factor * block_grad
    block_next = block_weight * (1.0 - LR_MUON * WEIGHT_DECAY) - LR_MUON * orthogonal(momentum, row_blocks, gram_total)
    teacher_next = EMA_RATE * teacher_weight + (1.0 - EMA_RATE) * block_next
    teacher_vec_next = EMA_RATE * teacher_vector + (1.0 - EMA_RATE) * vector_next[0]
    return small_next + stack_next + side_next + vector_next + (block_next, momentum, teacher_next, teacher_vec_next, block_next.astype(jnp.bfloat16))

def plain_total(gram_matrix):
    return gram_matrix

def reference(wave, clip_ids, span_starts, step_count, conv_small, conv_stack, side, vectors, block, teacher_block, teacher_vectors, small_mean, small_square, stack_mean, stack_square, side_mean, side_square, vector_mean, vector_square, block_momentum):
    waves = wave.reshape(DEVICES, SAMP)
    segments = clip_ids.reshape(DEVICES, F_DEV)
    starts = span_starts.reshape(DEVICES, F_DEV)
    total = jnp.maximum(jnp.sum(jax.vmap(masked_of)(starts).astype(jnp.float32)), 1.0)

    def visit(carry, item):
        outcome = local_step(item[0], item[1], item[2], conv_small, conv_stack, side, vectors, block, teacher_block, teacher_vectors, total)
        return (jax.tree.map(jnp.add, carry, outcome), None)
    zeros = (jnp.zeros((), jnp.float32), jnp.zeros_like(conv_small), jnp.zeros_like(conv_stack), jnp.zeros_like(side), jnp.zeros_like(block), jnp.zeros_like(vectors))
    sums, unused_out = lax.scan(visit, zeros, (waves, segments, starts))
    loss_value = sums[0]
    grads = sums[1:]
    grad_norm = jnp.sqrt(sum((jnp.sum(member * member) for member in grads)))
    factor = jnp.minimum(1.0, CLIP_LIMIT / (grad_norm + 1e-06))
    power = jnp.power(DECAY, step_count[0].astype(jnp.float32))
    updates = apply_updates(factor, power, (conv_small, conv_stack, side, vectors, block, teacher_block, teacher_vectors), grads, (small_mean, small_square, stack_mean, stack_square, side_mean, side_square, vector_mean, vector_square, block_momentum), N_DP, plain_total)
    return (loss_value, grad_norm, updates[0], updates[1], updates[2], updates[3], updates[4], updates[5], updates[6], updates[7], updates[8], updates[9], updates[10], updates[11], updates[12], updates[13], updates[14], updates[15], updates[16])
```

```python
import math

import jax
import jax.numpy as jnp
import numpy as np
from jax import lax
from jax.sharding import Mesh
from jax.sharding import PartitionSpec as P

D = 768
HEADS = 12
HEAD_DIM = 64
CH = 512
GROUPS = 16
WIDTH = D // GROUPS
POS_K = 19
REACH = POS_K // 2
SPAN = 10
TAIL = 16

EPS = 1e-05
VAR_FLOOR = 0.1
CLIP_LIMIT = 0.01
LR_ADAM = 0.03
LR_MUON = 2.0
DECAY = 0.5
WEIGHT_DECAY = 0.01
EMA_RATE = 0.5
KERNELS = (3, 3, 3, 3, 2, 2)
COEFF_A = 3.4445
COEFF_B = -4.775
COEFF_C = 2.0315
HIGHEST = lax.Precision.HIGHEST
F32 = jnp.float32
BF16 = jnp.bfloat16
ROOT_HALF = math.sqrt(0.5)
ROOT_TAU = 1.0 / math.sqrt(2.0 * math.pi)


def bf(values):
    return values.astype(BF16)


def low(values):
    return lax.optimization_barrier(values.astype(BF16)).astype(F32)


def dot(left, right, contract, batch=((), ())):
    return lax.dot_general(left, right, (contract, batch), preferred_element_type=F32)


def mm(left, right):
    return dot(left, right, ((1,), (0,)))


def mm_t(left, right):
    return dot(left, right, ((1,), (1,)))


def t_mm(left, right):
    return dot(left, right, ((0,), (0,)))


def gelu(values):
    return 0.5 * values * (1.0 + lax.erf(values * ROOT_HALF))


def gelu_slope(values):
    return 0.5 * (1.0 + lax.erf(values * ROOT_HALF)) + values * (
        ROOT_TAU * jnp.exp(-0.5 * values * values)
    )


def norm_fwd(values, gain, shift):
    center = values - jnp.mean(values, axis=-1, keepdims=True)
    scale = lax.rsqrt(jnp.mean(center * center, axis=-1, keepdims=True) + EPS)
    unit = center * scale
    return unit * gain + shift, (unit, scale)


def norm_bwd(kept, gain, grad):
    unit, scale = kept
    inner = grad * gain
    back = scale * (
        inner
        - jnp.mean(inner, axis=-1, keepdims=True)
        - unit * jnp.mean(inner * unit, axis=-1, keepdims=True)
    )
    return back, jnp.sum(grad * unit, axis=0), jnp.sum(grad, axis=0)


def wave_taps(wave, frames):
    padded = jnp.pad(bf(wave), (0, 320 * (frames + 2) - wave.shape[0])).reshape(frames + 2, 320)
    rows = jnp.concatenate([padded[: frames + 1], padded[1:, :5]], axis=1)
    pick = np.zeros((325, 640), np.float32)
    for phase in range(64):
        for tap in range(10):
            pick[5 * phase + tap, 10 * phase + tap] = 1.0
    taps = bf(mm(rows, jnp.asarray(pick, BF16)))
    taps = taps.reshape(frames + 1, 64, 10).transpose(1, 0, 2)
    return jnp.concatenate(
        [taps[:, :frames].reshape(64 * frames, 10), taps[:TAIL, frames]], axis=0
    )


def tap_rows(hidden, kernel, frames):
    tail = hidden[-TAIL:]
    main = hidden[:-TAIL].reshape(-1, 2, frames, CH)
    half = main.shape[0]
    even, odd = main[:, 0], main[:, 1]
    pieces = [even.reshape(half * frames, CH), odd.reshape(half * frames, CH)]
    pad = jnp.zeros((TAIL // 2, CH), hidden.dtype)
    ends = [jnp.concatenate([tail[0::2], pad]), jnp.concatenate([tail[1::2], pad])]
    if kernel == 3:
        wrap = jnp.concatenate([even[0, 1:], tail[:1]], axis=0)
        pieces.append(jnp.concatenate([even[1:], wrap[None]], axis=0).reshape(half * frames, CH))
        ends.append(jnp.concatenate([tail[2::2], pad, pad[:1]]))
    return jnp.concatenate(
        [jnp.concatenate(pieces, axis=1), jnp.concatenate(ends, axis=1)], axis=0
    )


def tap_rows_back(grad, kernel, frames):
    main, tail = grad[:-TAIL], grad[-TAIL:]
    half = main.shape[0] // frames
    even = main[:, :CH].reshape(half, frames, CH)
    odd = main[:, CH : 2 * CH].reshape(half, frames, CH)
    tail_even = tail[: TAIL // 2, :CH]
    tail_odd = tail[: TAIL // 2, CH : 2 * CH]
    if kernel == 3:
        next_even = main[:, 2 * CH :].reshape(half, frames, CH)
        wrap = next_even[-1]
        first = jnp.concatenate([jnp.zeros((1, CH), F32), wrap[:-1]], axis=0)
        even = even + jnp.concatenate([first[None], next_even[:-1]], axis=0)
        tail_even = tail_even + jnp.concatenate(
            [wrap[-1:], tail[: TAIL // 2 - 1, 2 * CH :]], axis=0
        )
    main = jnp.stack([even, odd], axis=1).reshape(2 * half * frames, CH)
    tail = jnp.stack([tail_even, tail_odd], axis=1).reshape(TAIL, CH)
    return jnp.concatenate([main, tail], axis=0)


def encode_fwd(small, stack, taps, frames):
    first = mm(taps, bf(small[:10]))
    hidden = bf(gelu(first))
    kept = []
    offset = 0
    for kernel in KERNELS:
        rows = tap_rows(hidden, kernel, frames)
        values = mm(rows, stack[offset : offset + kernel * CH])
        kept.append((rows, values))
        offset += kernel * CH
        activated = gelu(values)
        hidden = bf(activated)
    encoded = activated[:frames]
    normed, norm_kept = norm_fwd(encoded, small[10], small[11])
    return bf(normed), (first, kept, norm_kept)


def encode_bwd(saved, small, stack, taps, frames, grad):
    first, kept, norm_kept = saved
    grad, gain_grad, shift_grad = norm_bwd(norm_kept, small[10], grad)
    grad = jnp.concatenate([grad, jnp.zeros((TAIL, CH), F32)], axis=0)
    offset = stack.shape[0]
    pieces = []
    for kernel, (rows, values) in zip(KERNELS[::-1], kept[::-1]):
        offset -= kernel * CH
        product_grad = bf(grad * gelu_slope(values))
        pieces.append(t_mm(rows, product_grad))
        grad = tap_rows_back(
            mm_t(product_grad, stack[offset : offset + kernel * CH]), kernel, frames
        )
    product_grad = bf(grad * gelu_slope(first))
    tap_grad = t_mm(taps, product_grad)
    small_grad = jnp.concatenate([tap_grad, gain_grad[None], shift_grad[None]], axis=0)
    return small_grad, jnp.concatenate(pieces[::-1], axis=0)


def neighbours(segment):
    frames = segment.shape[0]
    padded = jnp.pad(segment, (REACH, REACH), constant_values=-1)
    return jnp.stack([padded[offset : offset + frames] == segment for offset in range(POS_K)], 0)


def masked_of(starts):
    frames = starts.shape[0]
    padded = jnp.pad(starts, (SPAN - 1, 0))
    return (
        jnp.max(jnp.stack([padded[offset : offset + frames] for offset in range(SPAN)], 0), axis=0)
        > 0
    )


def group_taps(values, nearby):
    frames = values.shape[0]
    padded = jnp.pad(values, ((REACH, REACH), (0, 0)))
    rows = jnp.stack([padded[offset : offset + frames] for offset in range(POS_K)], 0)
    rows = jnp.where(nearby[:, :, None], rows, jnp.zeros((), BF16))
    return (
        rows.reshape(POS_K, frames, GROUPS, WIDTH)
        .transpose(2, 1, 0, 3)
        .reshape(GROUPS, frames, POS_K * WIDTH)
    )


def batch_mm(left, right):
    return dot(left, right, ((2,), (1,)), ((0,), (0,)))


def batch_mm_t(left, right):
    return dot(left, right, ((2,), (2,)), ((0,), (0,)))


def batch_t_mm(left, right):
    return dot(left, right, ((1,), (1,)), ((0,), (0,)))


def block_fwd(values, kernel, weights, vectors, nearby, attend):
    frames = values.shape[0]
    taps = group_taps(bf(values), nearby)
    mixed = batch_mm(taps, kernel).transpose(1, 0, 2).reshape(frames, D) + vectors[7]
    hidden, norm_one = norm_fwd(values + gelu(mixed), vectors[0], vectors[1])
    hidden_low = bf(hidden)
    triple = bf(mm(hidden_low, weights[0][:, : 3 * D]))
    heads = triple.reshape(frames, 3, HEADS, HEAD_DIM).transpose(1, 2, 0, 3)
    scores = batch_mm_t(heads[0], heads[1]) * (1.0 / math.sqrt(HEAD_DIM))
    scores = jnp.where(attend[None], scores, -1e30)
    chances = jax.nn.softmax(scores, axis=-1)
    chances_low = bf(chances)
    outs = bf(batch_mm(chances_low, heads[2]).transpose(1, 0, 2).reshape(frames, D))
    second, norm_two = norm_fwd(
        hidden + mm(outs, weights[0][:, 3 * D :]), vectors[2], vectors[3]
    )
    second_low = bf(second)
    wide = mm(second_low, weights[1])
    inner = bf(gelu(wide))
    result, norm_three = norm_fwd(second + mm_t(inner, weights[2]), vectors[4], vectors[5])
    return result, (
        taps,
        mixed,
        norm_one,
        hidden_low,
        heads,
        chances,
        chances_low,
        outs,
        norm_two,
        second_low,
        wide,
        inner,
        norm_three,
    )


def block_bwd(saved, kernel_back, weights, vectors, nearby, grad):
    (
        taps,
        mixed,
        norm_one,
        hidden_low,
        heads,
        chances,
        chances_low,
        outs,
        norm_two,
        second_low,
        wide,
        inner,
        norm_three,
    ) = saved
    frames = grad.shape[0]
    grad, gain_three, shift_three = norm_bwd(norm_three, vectors[4], grad)
    down = bf(grad)
    out_grad = t_mm(down, inner)
    wide_grad = bf(mm(down, weights[2]) * gelu_slope(wide))
    in_grad = t_mm(second_low, wide_grad)
    grad = grad + mm_t(wide_grad, weights[1])
    grad, gain_two, shift_two = norm_bwd(norm_two, vectors[2], grad)
    down = bf(grad)
    mix_grad = t_mm(outs, down)
    outs_grad = bf(mm_t(down, weights[0][:, 3 * D :]))
    outs_grad = outs_grad.reshape(frames, HEADS, HEAD_DIM).transpose(1, 0, 2)
    chance_grad = batch_mm_t(outs_grad, heads[2])
    value_grad = batch_t_mm(chances_low, outs_grad)
    score_grad = chances * (
        chance_grad - jnp.sum(chance_grad * chances, axis=-1, keepdims=True)
    )
    score_grad = bf(score_grad * (1.0 / math.sqrt(HEAD_DIM)))
    query_grad = batch_mm(score_grad, heads[1])
    key_grad = batch_t_mm(score_grad, heads[0])
    triple_grad = bf(
        jnp.stack([query_grad, key_grad, value_grad], 0)
        .transpose(2, 0, 1, 3)
        .reshape(frames, 3 * D)
    )
    triple_weight_grad = t_mm(hidden_low, triple_grad)
    grad = grad + mm_t(triple_grad, weights[0][:, : 3 * D])
    grad, gain_one, shift_one = norm_bwd(norm_one, vectors[0], grad)
    mixed_grad = grad * gelu_slope(mixed)
    bias_grad = jnp.sum(mixed_grad, axis=0)
    mixed_low = bf(mixed_grad)
    kernel_grad = batch_t_mm(
        taps, mixed_low.reshape(frames, GROUPS, WIDTH).transpose(1, 0, 2)
    )
    back_taps = group_taps(mixed_low, nearby)
    grad = grad + batch_mm(back_taps, kernel_back).transpose(1, 0, 2).reshape(frames, D)
    block_grad = jnp.stack(
        [jnp.concatenate([triple_weight_grad, mix_grad], axis=1), in_grad, out_grad], 0
    )
    kernel_grad = (
        kernel_grad.reshape(GROUPS, POS_K, WIDTH, WIDTH)
        .transpose(0, 2, 1, 3)
        .reshape(D, POS_K * WIDTH)
    )
    vector_grad = (gain_one, shift_one, gain_two, shift_two, gain_three, shift_three, bias_grad)
    return grad, block_grad, kernel_grad, vector_grad


def clip_normal(output, attend):
    member = attend.astype(F32)
    clip_size = jnp.sum(member, axis=1, keepdims=True)
    average = jnp.dot(member, output, precision=HIGHEST) / clip_size
    center = output - average
    spread = jnp.dot(member, center * center, precision=HIGHEST) / clip_size
    return center * lax.rsqrt(jnp.maximum(spread, VAR_FLOOR))


def adamw(weight, grad, first, second, power):
    first = DECAY * first + (1.0 - DECAY) * grad
    second = DECAY * second + (1.0 - DECAY) * grad * grad
    unbias = 1.0 - power
    step_size = first / unbias / (jnp.sqrt(second / unbias) + 1e-08)
    return (weight - LR_ADAM * (step_size + WEIGHT_DECAY * weight), first, second)


def exact(left, right):
    return jnp.einsum("brs,bst->brt", left, right, precision=HIGHEST)


def orthogonal(blocks, gram_total):
    gram = gram_total(jnp.einsum("brc,bsc->brs", blocks, blocks, precision=HIGHEST))
    scales = 1.0 / (jnp.sqrt(jnp.trace(gram, axis1=1, axis2=2)) + 1e-07)
    gram = gram * (scales * scales)[:, None, None]
    eye = jnp.eye(gram.shape[1], dtype=F32)[None]
    whole = None
    for iteration in range(5):
        square = exact(gram, gram)
        step = COEFF_A * eye + COEFF_B * gram + COEFF_C * square
        whole = step if whole is None else exact(step, whole)
        if iteration < 4:
            gram = exact(exact(step, gram), step)
            gram = 0.5 * (gram + gram.transpose(0, 2, 1))
    return exact(whole * scales[:, None, None], blocks)


def per_device(
    wave,
    clip_ids,
    span_starts,
    step_count,
    conv_small,
    conv_stack,
    side,
    vectors,
    block,
    teacher_block,
    teacher_vectors,
    small_mean,
    small_square,
    stack_mean,
    stack_square,
    side_mean,
    side_square,
    vector_mean,
    vector_square,
    block_momentum,
    n_dp,
    n_narrow,
):
    everyone = ("dp", "narrow")
    frames = clip_ids.shape[0]
    rows_here, cols_here = block.shape[1:]
    side_rows, side_cols = side.shape
    stack = lax.all_gather(bf(conv_stack), everyone, axis=0, tiled=True)
    masked = masked_of(span_starts)
    total = jnp.maximum(lax.psum(jnp.sum(masked.astype(F32)), everyone), 1.0)
    send = jnp.concatenate(
        [
            bf(block).reshape(3 * rows_here, cols_here),
            bf(teacher_block).reshape(3 * rows_here, cols_here),
            jnp.pad(bf(side), ((0, 0), (0, cols_here - side_cols))),
        ],
        axis=0,
    )
    whole = lax.all_gather(send, everyone, axis=0, tiled=False)
    whole = whole.reshape(n_dp, n_narrow, 7, rows_here, cols_here)
    weights = whole[:, :, :6].transpose(2, 0, 3, 1, 4).reshape(6, D, n_narrow * cols_here)
    whole_side = (
        whole[:, :, 6, :, :side_cols]
        .transpose(0, 2, 1, 3)
        .reshape(n_dp * side_rows, n_narrow * side_cols)
    )
    project = whole_side[:, :CH]
    kernel = whole_side[:, CH : CH + POS_K * WIDTH].reshape(GROUPS, WIDTH, POS_K, WIDTH)
    head = whole_side[:, CH + POS_K * WIDTH :]
    kernel_fwd = kernel.transpose(0, 2, 1, 3).reshape(GROUPS, POS_K * WIDTH, WIDTH)
    kernel_back = kernel[:, :, ::-1].transpose(0, 2, 3, 1).reshape(GROUPS, POS_K * WIDTH, WIDTH)

    nearby = neighbours(clip_ids)
    attend = clip_ids[:, None] == clip_ids[None, :]
    small_low = low(conv_small)
    vector_low = low(vectors)
    taps = wave_taps(wave, frames)
    normed, encode_saved = encode_fwd(small_low, stack, taps, frames)
    feats = mm_t(normed, project) + vector_low[6]
    teacher_out, unused = block_fwd(
        feats, kernel_fwd, weights[3:], low(teacher_vectors), nearby, attend
    )
    target = clip_normal(teacher_out, attend)
    chosen = masked[:, None]
    values = jnp.where(chosen, vector_low[9], feats)
    student_out, block_saved = block_fwd(
        values, kernel_fwd, weights[:3], vector_low, nearby, attend
    )
    student_low = bf(student_out)
    error = jnp.where(chosen, mm(student_low, head) + vector_low[8] - target, 0.0)
    weight = 1.0 / (total * math.sqrt(D))
    loss_part = jnp.sum(error * error) * weight

    predict_grad = error * (2.0 * weight)
    head_bias_grad = jnp.sum(predict_grad, axis=0)
    predict_low = bf(predict_grad)
    head_grad = t_mm(student_low, predict_low)
    grad, block_grad, kernel_grad, vector_parts = block_bwd(
        block_saved, kernel_back, weights[:3], vector_low, nearby, mm_t(predict_low, head)
    )
    mask_grad = jnp.sum(jnp.where(chosen, grad, 0.0), axis=0)
    feat_grad = jnp.where(chosen, 0.0, grad)
    project_bias_grad = jnp.sum(feat_grad, axis=0)
    feat_low = bf(feat_grad)
    project_grad = t_mm(feat_low, normed)
    vector_grad = jnp.stack(
        vector_parts[:6] + (project_bias_grad, vector_parts[6], head_bias_grad, mask_grad), 0
    )
    side_grad = jnp.concatenate([project_grad, kernel_grad, head_grad], axis=1)

    block_send = block_grad.reshape(3, n_dp, rows_here, n_narrow, cols_here).transpose(
        1, 3, 0, 2, 4
    )
    block_piece = lax.psum_scatter(
        block_send.reshape(n_dp * n_narrow * 3 * rows_here, cols_here),
        everyone,
        scatter_dimension=0,
        tiled=True,
    ).reshape(3, rows_here, cols_here)
    side_send = side_grad.reshape(n_dp, side_rows, n_narrow, side_cols).transpose(0, 2, 1, 3)
    side_piece = lax.psum_scatter(
        side_send.reshape(n_dp * n_narrow * side_rows, side_cols),
        everyone,
        scatter_dimension=0,
        tiled=True,
    )
    small_grad, stack_grad = encode_bwd(
        encode_saved, small_low, stack, taps, frames, mm(feat_low, project)
    )
    stack_piece = lax.psum_scatter(stack_grad, everyone, scatter_dimension=0, tiled=True)
    small_total, vector_total, loss_value = lax.psum(
        (small_grad, vector_grad, loss_part), everyone
    )
    shard_squares = (
        jnp.sum(block_piece * block_piece)
        + jnp.sum(side_piece * side_piece)
        + jnp.sum(stack_piece * stack_piece)
    )
    grad_norm = jnp.sqrt(
        lax.psum(shard_squares, everyone)
        + jnp.sum(small_total * small_total)
        + jnp.sum(vector_total * vector_total)
    )
    factor = jnp.minimum(1.0, CLIP_LIMIT / (grad_norm + 1e-06))
    power = jnp.power(DECAY, step_count[0].astype(F32))
    small_next = adamw(conv_small, factor * small_total, small_mean, small_square, power)
    stack_next = adamw(conv_stack, factor * stack_piece, stack_mean, stack_square, power)
    side_next = adamw(side, factor * side_piece, side_mean, side_square, power)
    vector_next = adamw(vectors, factor * vector_total, vector_mean, vector_square, power)
    momentum = DECAY * block_momentum + factor * block_piece
    ortho = orthogonal(momentum, lambda gram: lax.psum(gram, "narrow"))
    block_next = block * (1.0 - LR_MUON * WEIGHT_DECAY) - LR_MUON * ortho
    teacher_next = EMA_RATE * teacher_block + (1.0 - EMA_RATE) * block_next
    teacher_vec_next = EMA_RATE * teacher_vectors + (1.0 - EMA_RATE) * vector_next[0]
    return (
        (loss_value, grad_norm)
        + small_next
        + stack_next
        + side_next
        + vector_next
        + (block_next, momentum, teacher_next, teacher_vec_next, bf(block_next))
    )


def solution(mesh):
    n_dp, n_narrow = mesh.shape["dp"], mesh.shape["narrow"]

    def step(*arguments):
        return per_device(*arguments, n_dp, n_narrow)

    rows = P(("dp", "narrow"), None)
    flat = P(("dp", "narrow"))
    grid = P("dp", "narrow")
    cube = P(None, "dp", "narrow")
    one = P()
    in_specs = (
        (flat, flat, flat, one, one, rows, grid, one, cube, cube, one, one, one)
        + (rows, rows, grid, grid, one, one, cube)
    )
    out_specs = (
        (one, one, one, one, one, rows, rows, rows, grid, grid, grid, one, one, one)
        + (cube, cube, cube, one, cube)
    )
    return jax.shard_map(
        step, mesh=mesh, in_specs=in_specs, out_specs=out_specs, check_vma=False
    )
```

```python
import math

import jax
import jax.numpy as jnp
import numpy as np
from jax import lax
from jax.experimental import pallas as pl
from jax.experimental.pallas import tpu as pltpu
from jax.sharding import Mesh
from jax.sharding import PartitionSpec as P

D = 768
HEADS = 12
HEAD_DIM = 64
CH = 512
GROUPS = 16
WIDTH = D // GROUPS
POS_K = 19
REACH = POS_K // 2
SPAN = 10
TAIL = 16

EPS = 1e-05
VAR_FLOOR = 0.1
CLIP_LIMIT = 0.01
LR_ADAM = 0.03
LR_MUON = 2.0
DECAY = 0.5
WEIGHT_DECAY = 0.01
EMA_RATE = 0.5
KERNELS = (3, 3, 3, 3, 2, 2)
COEFF_A = 3.4445
COEFF_B = -4.775
COEFF_C = 2.0315
HIGHEST = lax.Precision.HIGHEST
F32 = jnp.float32
BF16 = jnp.bfloat16
LIMIT = 60 * 1024 * 1024
ROOT_HALF = math.sqrt(0.5)
ROOT_TAU = 1.0 / math.sqrt(2.0 * math.pi)


VMEM = pl.BlockSpec(memory_space=pltpu.VMEM)
ANY = pl.BlockSpec(memory_space=pl.ANY)
SMEM = pl.BlockSpec(memory_space=pltpu.SMEM)


def bf(values):
    return values.astype(BF16)


def low(values):
    return lax.optimization_barrier(values.astype(BF16)).astype(F32)


def dot(left, right, contract, batch=((), ())):
    return lax.dot_general(left, right, (contract, batch), preferred_element_type=F32)


def mm(left, right):
    return dot(left, right, ((1,), (0,)))


def mm_t(left, right):
    return dot(left, right, ((1,), (1,)))


def t_mm(left, right):
    return dot(left, right, ((0,), (0,)))


def gelu(values):
    return 0.5 * values * (1.0 + lax.erf(values * ROOT_HALF))


def gelu_slope(values):
    return 0.5 * (1.0 + lax.erf(values * ROOT_HALF)) + values * (
        ROOT_TAU * jnp.exp(-0.5 * values * values)
    )


def norm_fwd(values, gain, shift):
    center = values - jnp.mean(values, axis=-1, keepdims=True)
    scale = lax.rsqrt(jnp.mean(center * center, axis=-1, keepdims=True) + EPS)
    unit = center * scale
    return unit * gain + shift, (unit, scale)


def norm_bwd(kept, gain, grad):
    unit, scale = kept
    inner = grad * gain
    back = scale * (
        inner
        - jnp.mean(inner, axis=-1, keepdims=True)
        - unit * jnp.mean(inner * unit, axis=-1, keepdims=True)
    )
    return back, jnp.sum(grad * unit, axis=0), jnp.sum(grad, axis=0)


def first_taps(wave, frames):
    padded = jnp.pad(bf(wave), (0, 320 * (frames + 2) - wave.shape[0])).reshape(frames + 2, 320)
    rows = jnp.concatenate([padded[: frames + 1], padded[1:, :16]], axis=1)
    pick = np.zeros((336, 65 * 16), np.float32)
    for phase in range(64):
        for tap in range(10):
            pick[5 * phase + tap, 16 * phase + tap] = 1.0
    taps = bf(mm(rows, jnp.asarray(pick[:, : 64 * 16], BF16)))
    taps = taps.reshape(frames + 1, 64, 16).transpose(1, 0, 2)
    main = jnp.concatenate(
        [taps[:, :frames], taps[:1, 1:], jnp.zeros((1, frames, 16), BF16)], axis=0
    )
    return main, taps[:TAIL, frames]


def chooser(delta, rows_last=True):
    rows = lax.broadcasted_iota(jnp.int32, (TAIL, TAIL), 0)
    cols = lax.broadcasted_iota(jnp.int32, (TAIL, TAIL), 1)
    hit = cols == 2 * rows + delta if rows_last else rows == 2 * cols + delta
    return jnp.where(hit, 1.0, 0.0)


def stack_rows(ref, tap, taps=sum(KERNELS)):
    count = ref.shape[0] // taps
    rows = CH // count
    return ref[tap * count : (tap + 1) * count, :rows, :].reshape(CH, CH)


def first_kernel(taps_ref, weight_ref, out_ref):
    frames = taps_ref.shape[1]
    rows = taps_ref[...].reshape(2 * frames, taps_ref.shape[2])
    out_ref[...] = bf(gelu(mm(rows, weight_ref[...]))).reshape(out_ref.shape)


def encode_kernel(hidden_ref, tail_ref, stack_ref, small_ref, *refs):
    value_refs, hidden_refs = refs[:6], (hidden_ref,) + refs[6:11]
    value_tail_ref, hidden_tail_ref, normed_ref, unit_ref, scale_ref = refs[11:]
    frames = hidden_ref.shape[2]
    offset = 0
    tail = tail_ref[...]
    for layer, kernel in enumerate(KERNELS):
        source, values = hidden_refs[layer], value_refs[layer]
        count = values.shape[0]
        size = min(4, count)
        target = hidden_refs[layer + 1] if layer < 5 else None

        def product(index, offset=offset, kernel=kernel, source=source, size=size):
            total = None
            for tap in range(kernel):
                piece = source[pl.ds(index * size + tap // 2, size), tap % 2]
                part = mm(
                    piece.reshape(size * frames, CH),
                    stack_rows(stack_ref, offset // CH + tap),
                )
                total = part if total is None else total + part
            return total

        def step(index, carry, values=values, target=target, size=size, product=product):
            total = product(index)
            values[pl.ds(index * size, size)] = total.reshape(size, frames, CH)
            active = bf(gelu(total))
            target[pl.ds(index * (size // 2), size // 2)] = active.reshape(
                size // 2, 2, frames, CH
            )
            return carry

        if layer < 5:
            if count == size:
                step(0, 0)
            else:
                lax.fori_loop(0, count // size, step, 0)
        else:
            total = product(0)
            values[...] = total.reshape(values.shape)
            encoded = gelu(total)
            normed, kept = norm_fwd(encoded, small_ref[10:11, :], small_ref[11:12, :])
            normed_ref[...] = bf(normed)
            unit_ref[...] = kept[0]
            scale_ref[...] = jnp.broadcast_to(kept[1], scale_ref.shape)
        if layer < 3:
            total = None
            for tap in range(kernel):
                part = mm(
                    bf(mm(bf(chooser(tap)), tail)),
                    stack_rows(stack_ref, offset // CH + tap),
                )
                total = part if total is None else total + part
            value_tail_ref[layer] = total
            active = gelu(total)
            tail = bf(active)
            hidden_tail_ref[layer] = tail
            head = target[0, 0].astype(F32)
            rows = lax.broadcasted_iota(jnp.int32, (frames, CH), 0)
            moved = jnp.where(
                rows == frames - 1, active[0:1].astype(BF16).astype(F32),
                pltpu.roll(head, frames - 1, 0),
            )
            target[count // 2, 0] = bf(moved)
            target[count // 2, 1] = jnp.zeros((frames, CH), BF16)
        offset += kernel * CH


def layer_dw(grad_ref, source_ref, tail_grad, source_tail, kernel, out_ref):
    count, frames = grad_ref.shape[:2]
    size = min(8, count)
    for tap in range(kernel):
        rows = slice(tap * CH, (tap + 1) * CH)
        if tail_grad is None:
            out_ref[rows, :] = jnp.zeros((CH, CH), F32)
        else:
            out_ref[rows, :] = t_mm(bf(mm(bf(chooser(tap)), source_tail)), tail_grad)

        def step(index, carry, tap=tap, rows=rows):
            piece = source_ref[pl.ds(index * size + tap // 2, size), tap % 2]
            grad = grad_ref[pl.ds(index * size, size)]
            out_ref[rows, :] += t_mm(
                piece.reshape(size * frames, CH), grad.reshape(size * frames, CH)
            )
            return carry

        if count == size:
            step(0, 0)
        else:
            lax.fori_loop(0, count // size, step, 0)


def layer_dx(grad_ref, tail_grad, kernel, weight_of, slope, write, carry_ref, head_ref):
    count, frames = grad_ref.shape[:2]
    size = min(4, count)
    carry_ref[...] = jnp.zeros((frames, CH), F32)

    def step(index, unused):
        grad = grad_ref[pl.ds(index * size, size)].reshape(size * frames, CH)
        even = mm_t(grad, weight_of(0)).reshape(size, frames, CH)
        odd = mm_t(grad, weight_of(1)).reshape(size, frames, CH)
        if kernel == 3:
            late = mm_t(grad, weight_of(2)).reshape(size, frames, CH)
            before = carry_ref[...][None]
            if size > 1:
                before = jnp.concatenate([before, late[:-1]], axis=0)
            even = even + before
            carry_ref[...] = late[-1]
        write(index, size, even, odd)
        return unused

    if count == size:
        step(0, 0)
    else:
        lax.fori_loop(0, count // size, step, 0)
    if kernel != 3:
        return None
    wrap = carry_ref[...]
    rows = lax.broadcasted_iota(jnp.int32, (frames, CH), 0)
    head_ref[...] = jnp.where(rows == 0, 0.0, pltpu.roll(wrap, 1, 0))
    first = lax.broadcasted_iota(jnp.int32, (TAIL, CH), 0) == 0
    back = jnp.where(first, wrap[frames - 1 : frames, :], 0.0)
    if tail_grad is not None:
        for tap in range(3):
            back = back + jnp.dot(
                chooser(tap, False), mm_t(tail_grad, weight_of(tap)),
                precision=HIGHEST, preferred_element_type=F32,
            )
    return back


def copy_halves(core_ref, held, send_ref, keep_ref, first, taps, sem):
    half = CH // 2
    core = core_ref[0]
    copies = []
    for tap in range(taps):
        for target, index in ((send_ref, 1 - core), (keep_ref, core)):
            start = pl.multiple_of(tap * CH + index * half, half)
            copies.append(
                pltpu.make_async_copy(held.at[pl.ds(start, half)], target.at[first + tap], sem)
            )
            copies[-1].start()
    return copies


def encode_back_kernel(core_ref, grad_ref, unit_ref, scale_ref, small_ref, stack_ref, *refs):
    value_refs, hidden_refs = refs[:6], refs[6:11]
    value_tail_ref, hidden_tail_ref = refs[11:13]
    send_ref, keep_ref, second_ref, second_tail_ref, norm_ref = refs[13:18]
    grad_refs = (second_ref,) + refs[18:23]
    buffer_ref, carry_ref, head_ref, even_ref, sems = refs[23:]
    frames = grad_ref.shape[0]
    grad, gain, shift = norm_bwd(
        (unit_ref[...], scale_ref[:, :1]), small_ref[10:11, :], grad_ref[...]
    )
    norm_ref[0:1, :] = gain[None]
    norm_ref[1:2, :] = shift[None]
    grad_refs[5][0] = bf(grad * gelu_slope(value_refs[5][0]))
    tail_grad = None
    offset = sum(KERNELS) * CH
    copies = [[], []]
    for layer in range(5, 0, -1):
        kernel = KERNELS[layer]
        offset -= kernel * CH
        slot = layer % 2
        for copy in copies[slot]:
            copy.wait()
        held = buffer_ref.at[slot, 0 : kernel * CH]
        tail_source = None if tail_grad is None else hidden_tail_ref[layer - 1]
        layer_dw(grad_refs[layer], hidden_refs[layer - 1], tail_grad, tail_source, kernel, held)
        copies[slot] = copy_halves(
            core_ref, held, send_ref, keep_ref, offset // CH, kernel, sems.at[slot]
        )
        values, target = value_refs[layer - 1], grad_refs[layer - 1]

        def weight_of(tap, offset=offset):
            return stack_rows(stack_ref, offset // CH + tap)

        def write(index, size, even, odd, values=values, target=target, kernel=kernel):
            if kernel == 3:
                if not isinstance(index, int):
                    @pl.when(index == 0)
                    def _():
                        even_ref[...] = even[0]
                else:
                    even_ref[...] = even[0]
            for item in range(size):
                place = 2 * (index * size + item)
                target[place] = bf(even[item] * gelu_slope(values[place]))
                target[place + 1] = bf(odd[item] * gelu_slope(values[place + 1]))

        back = layer_dx(grad_refs[layer], tail_grad, kernel, weight_of, None, write,
                        carry_ref, head_ref)
        tail_grad = None
        if kernel == 3:
            target[0] = bf((even_ref[...] + head_ref[...]) * gelu_slope(values[0]))
            tail_grad = bf(back * gelu_slope(value_tail_ref[layer - 1]))
    second_tail_ref[...] = tail_grad
    for copy in copies[0] + copies[1]:
        copy.wait()


def second_dw_kernel(core_ref, grad_ref, tail_grad_ref, hidden_ref, tail_ref, old_send_ref,
                     old_keep_ref, send_ref, keep_ref, buffer_ref, sem):
    layer_dw(grad_ref, hidden_ref, tail_grad_ref[...], tail_ref[...], 3, buffer_ref)
    for copy in copy_halves(core_ref, buffer_ref, send_ref, keep_ref, 0, 3, sem):
        copy.wait()


def second_dx_kernel(grad_ref, tail_grad_ref, weight_ref, taps_ref, tail_taps_ref, first_ref,
                     out_ref, carry_ref, head_ref, even_ref):
    frames = grad_ref.shape[1]
    weights = first_ref[...]
    out_ref[...] = jnp.zeros(out_ref.shape, F32)

    def piece(place, grad):
        rows = taps_ref[place]
        low_grad = bf(grad * gelu_slope(mm(rows, weights)))
        return t_mm(rows, low_grad)

    def write(index, size, even, odd):
        @pl.when(index == 0)
        def _():
            even_ref[...] = even[0]

        for item in range(size):
            place = 2 * (index * size + item)
            grad = even[item]
            if item == 0:
                grad = jnp.where(index == 0, 0.0, grad)
            out_ref[...] += piece(place, grad) + piece(place + 1, odd[item])

    def weight_of(tap):
        return stack_rows(weight_ref, tap, 3)

    back = layer_dx(grad_ref, tail_grad_ref[...], 3, weight_of, None, write, carry_ref, head_ref)
    out_ref[...] += piece(0, even_ref[...] + head_ref[...])
    rows = tail_taps_ref[...]
    out_ref[...] += t_mm(rows, bf(back * gelu_slope(mm(rows, weights))))


COUNTS = (32, 16, 8, 4, 2, 1)


def kernel_params():
    return pltpu.CompilerParams(vmem_limit_bytes=LIMIT)


def first_layer(small, taps, frames):
    main, tail = taps
    weights = jnp.pad(bf(small[:10]), ((0, 6), (0, 0)))
    hidden = pl.pallas_call(
        first_kernel,
        grid=(33,),
        in_specs=[
            pl.BlockSpec((2, frames, 16), lambda i: (i, 0, 0)),
            pl.BlockSpec((16, CH), lambda i: (0, 0)),
        ],
        out_specs=pl.BlockSpec((1, 2, frames, CH), lambda i: (i, 0, 0, 0)),
        out_shape=jax.ShapeDtypeStruct((33, 2, frames, CH), BF16),
        name="first_layer",
    )(main, weights)
    return weights, hidden, bf(gelu(mm(tail, weights)))


def encode_fwd(small, stack, hidden, hidden_tail, frames):
    shape = jax.ShapeDtypeStruct
    return pl.pallas_call(
        encode_kernel,
        in_specs=[VMEM] * 4,
        out_specs=[VMEM] * 16,
        out_shape=[shape((count, frames, CH), F32) for count in COUNTS]
        + [shape((count // 2 + 1, 2, frames, CH), BF16) for count in COUNTS[:5]]
        + [
            shape((3, TAIL, CH), F32),
            shape((3, TAIL, CH), BF16),
            shape((frames, CH), BF16),
            shape((frames, CH), F32),
            shape((frames, 128), F32),
        ],
        name="encode",
        compiler_params=kernel_params(),
    )(hidden, hidden_tail, stack, small)


def encode_back(core, outs, small, stack, frames, grad):
    shape = jax.ShapeDtypeStruct
    plane = pltpu.VMEM((frames, CH), F32)
    part = shape((sum(KERNELS), CH // 2, CH), F32)
    return pl.pallas_call(
        encode_back_kernel,
        in_specs=[SMEM] + [VMEM] * 18,
        out_specs=[ANY, ANY, VMEM, VMEM, VMEM],
        out_shape=[
            part,
            part,
            shape((COUNTS[0], frames, CH), BF16),
            shape((TAIL, CH), BF16),
            shape((2, CH), F32),
        ],
        scratch_shapes=[pltpu.VMEM((count, frames, CH), BF16) for count in COUNTS[1:]]
        + [
            pltpu.VMEM((2, 3 * CH, CH), F32),
            plane,
            plane,
            plane,
            pltpu.SemaphoreType.DMA((2,)),
        ],
        name="encode_back",
        compiler_params=kernel_params(),
    )(core, grad, outs[14], outs[15], small, stack, *outs[:13])


def second_dw(core, second, second_tail, hidden, hidden_tail, parts):
    return pl.pallas_call(
        second_dw_kernel,
        in_specs=[SMEM] + [VMEM] * 4 + [ANY, ANY],
        out_specs=[ANY, ANY],
        out_shape=[jax.ShapeDtypeStruct(part.shape, F32) for part in parts],
        scratch_shapes=[pltpu.VMEM((3 * CH, CH), F32), pltpu.SemaphoreType.DMA],
        input_output_aliases={5: 0, 6: 1},
        name="second_dw",
        compiler_params=kernel_params(),
    )(core, second, second_tail, hidden, hidden_tail, *parts)


def second_dx(second, second_tail, stack, taps, weights, frames):
    main, tail = taps
    plane = pltpu.VMEM((frames, CH), F32)
    parts = 3 * stack.shape[0] // sum(KERNELS)
    return pl.pallas_call(
        second_dx_kernel,
        grid=(1,),
        in_specs=[
            VMEM,
            VMEM,
            pl.BlockSpec((parts,) + stack.shape[1:], lambda i: (0, 0, 0)),
            VMEM,
            VMEM,
            VMEM,
        ],
        out_specs=VMEM,
        out_shape=jax.ShapeDtypeStruct((16, CH), F32),
        scratch_shapes=[plane, plane, plane],
        name="second_dx",
        compiler_params=kernel_params(),
    )(second, second_tail, stack, main, tail, weights)


def neighbours(segment):
    frames = segment.shape[0]
    padded = jnp.pad(segment, (REACH, REACH), constant_values=-1)
    return jnp.stack([padded[offset : offset + frames] == segment for offset in range(POS_K)], 0)


def masked_of(starts):
    frames = starts.shape[0]
    padded = jnp.pad(starts, (SPAN - 1, 0))
    return (
        jnp.max(jnp.stack([padded[offset : offset + frames] for offset in range(SPAN)], 0), axis=0)
        > 0
    )


def taps_of(values, near, offset, flip):
    frames = values.shape[0]
    lane = 2 * REACH - offset if flip else offset
    shift = (REACH - lane) % frames
    rolled = values if shift == 0 else pltpu.roll(values, shift, 0)
    return bf(jnp.where(near[:, lane : lane + 1] > 0.0, rolled, 0.0))


def position_sum(values, near, spread_ref, back):
    half = D // 2
    sums = [None, None]
    for offset in range(POS_K):
        taps = taps_of(values, near, offset, back)
        for side in range(2):
            weight = spread_ref[offset, side * half : (side + 1) * half, :]
            piece = taps[:, side * half : (side + 1) * half]
            part = mm_t(piece, weight) if back else mm(piece, weight)
            sums[side] = part if sums[side] is None else sums[side] + part
    return jnp.concatenate(sums, axis=1)


def lane_half(values, upper):
    lanes = lax.broadcasted_iota(jnp.int32, values.shape, 1)
    keep = lanes >= HEAD_DIM if upper else lanes < HEAD_DIM
    return jnp.where(keep, values, 0.0)


def start_copies(place_ref, piece_refs, weight_ref, sems):
    if len(piece_refs) == 1 and len(piece_refs[0].shape) == 5:
        n_dp, n_narrow, unused, rows, cols = piece_refs[0].shape
        copies = []
        for matrix in range(3):
            for d in range(n_dp):
                for n in range(n_narrow):
                    copy = pltpu.make_async_copy(
                        piece_refs[0].at[d, n, matrix],
                        weight_ref.at[
                            matrix, pl.ds(d * rows, rows), pl.ds(n * cols, cols)
                        ],
                        sems.at[matrix],
                    )
                    copy.start()
                    copies.append(copy)
        return copies
    if len(piece_refs) == 1:
        copies = [
            pltpu.make_async_copy(piece_refs[0].at[m], weight_ref.at[m], sems.at[m])
            for m in range(3)
        ]
        for copy in copies:
            copy.start()
        return copies
    line, unused, rows, lanes = piece_refs[0].shape
    x, y, c = place_ref[0], place_ref[1], place_ref[2]
    copies = []
    for matrix in range(3):
        for number, ref in enumerate(piece_refs):
            half, dx, dy, dc = number // 8, number // 4 % 2, number // 2 % 2, number % 2
            narrow = (y ^ dy) * 2 + (c ^ dc)
            col = pl.multiple_of((narrow * 2 + half) * lanes, 128)
            for z in range(line):
                row = pl.multiple_of((2 * z + (x ^ dx)) * rows, 16)
                copy = pltpu.make_async_copy(
                    ref.at[z, matrix],
                    weight_ref.at[matrix, pl.ds(row, rows), pl.ds(col, lanes)],
                    sems.at[matrix],
                )
                copy.start()
                copies.append(copy)
    return copies


def await_copies(copies, matrix):
    count = len(copies) // 3
    for copy in copies[matrix * count : (matrix + 1) * count]:
        copy.wait()


def run_block(values, near, attend, spread_ref, weight_ref, vec_ref, copies, keep):
    vec = lambda row: vec_ref[row : row + 1, :]
    frames = values.shape[0]
    mixed = position_sum(bf(values).astype(F32), near, spread_ref, False) + vec(7)
    hidden, norm_one = norm_fwd(values + gelu(mixed), vec(0), vec(1))
    hidden_low = bf(hidden)
    await_copies(copies, 0)
    triple = bf(mm(hidden_low, weight_ref[0, :, : 3 * D]))
    outs = []
    for pair in range(HEADS // 2):
        lo = pair * 2 * HEAD_DIM
        hi = lo + 2 * HEAD_DIM
        query = triple[:, lo:hi].astype(F32)
        key = triple[:, D + lo : D + hi]
        value = triple[:, 2 * D + lo : 2 * D + hi]
        both = []
        for upper in range(2):
            scores = mm_t(bf(lane_half(query, upper)), key) * (1.0 / math.sqrt(HEAD_DIM))
            scores = jnp.where(attend, scores, -1e30)
            raised = jnp.exp(scores - jnp.max(scores, axis=-1, keepdims=True))
            chances = raised / jnp.sum(raised, axis=-1, keepdims=True)
            if keep is not None:
                keep["chances"][2 * pair + upper] = chances
            both.append(lane_half(mm(bf(chances), value), upper))
        outs.append(bf(both[0] + both[1]))
    outs = jnp.concatenate(outs, axis=1)
    second, norm_two = norm_fwd(hidden + mm(outs, weight_ref[0, :, 3 * D :]), vec(2), vec(3))
    second_low = bf(second)
    await_copies(copies, 1)
    await_copies(copies, 2)
    total = second
    step = D
    for start in range(0, weight_ref.shape[2], step):
        wide = mm(second_low, weight_ref[1, :, start : start + step])
        inner = bf(gelu(wide))
        if keep is not None:
            keep["wide"][:, start : start + step] = wide
            keep["right"][2, :, start : start + step] = inner
        total = total + mm_t(inner, weight_ref[2, :, start : start + step])
    result, norm_three = norm_fwd(total, vec(4), vec(5))
    if keep is not None:
        keep["triple"][...] = triple
        keep["mixed"][...] = mixed
        keep["left"][0] = hidden_low
        keep["left"][1] = outs
        keep["left"][2] = second_low
        for index, kept in enumerate((norm_one, norm_two, norm_three)):
            keep["units"][index] = kept[0]
            keep["scales"][index] = jnp.broadcast_to(kept[1], (frames, 128))
    return result


def teacher_kernel(place_ref, feat_ref, near_ref, col_ref, row_ref, spread_ref, vec_ref, *refs):
    piece_refs, (target_ref, weight_ref, sems) = refs[:-3], refs[-3:]
    copies = start_copies(place_ref, piece_refs, weight_ref, sems)
    attend = col_ref[...] == row_ref[...]
    output = run_block(feat_ref[...], near_ref[...], attend, spread_ref, weight_ref, vec_ref,
                       copies, None)
    member = attend.astype(F32)
    clip_size = jnp.sum(member, axis=1, keepdims=True)
    average = jnp.dot(member, output, precision=HIGHEST, preferred_element_type=F32) / clip_size
    center = output - average
    spread = jnp.dot(
        member, center * center, precision=HIGHEST, preferred_element_type=F32
    ) / clip_size
    target_ref[...] = center * lax.rsqrt(jnp.maximum(spread, VAR_FLOOR))


def student_kernel(place_ref, feat_ref, near_ref, col_ref, row_ref, mask_ref, weight_one_ref,
                   spread_ref, vec_ref, target_ref, normed_ref, project_ref, head_ref, *refs):
    piece_refs, refs = refs[:-14], refs[-14:]
    (left_ref, right_ref, side_ref, vector_ref, normed_grad_ref, loss_ref,
     weight_ref, chance_ref, wide_ref, triple_ref, mixed_ref, unit_ref, scale_ref,
     sems) = refs
    copies = start_copies(place_ref, piece_refs, weight_ref, sems)
    vec = lambda row: vec_ref[row : row + 1, :]
    total_sum = lambda values: jnp.sum(values, axis=0, keepdims=True)
    attend = col_ref[...] == row_ref[...]
    near = near_ref[...]
    chosen = mask_ref[...] > 0.0
    values = jnp.where(chosen, vec(9), feat_ref[...])
    keep = {
        "chances": chance_ref, "wide": wide_ref, "right": right_ref, "triple": triple_ref,
        "mixed": mixed_ref, "left": left_ref, "units": unit_ref, "scales": scale_ref,
    }
    result = run_block(values, near, attend, spread_ref, weight_ref, vec_ref, copies, keep)
    kept = lambda index: (unit_ref[index], scale_ref[index, :, :1])
    student_low = bf(result)
    scale = weight_one_ref[0:1, 0:1]
    error = jnp.where(chosen, mm(student_low, head_ref[...]) + vec(8) - target_ref[...], 0.0)
    loss_ref[...] = jnp.broadcast_to(
        jnp.sum(total_sum(error * error), axis=1, keepdims=True) * scale, loss_ref.shape
    )
    predict_grad = error * (2.0 * scale)
    vector_ref[8:9, :] = total_sum(predict_grad)
    predict_low = bf(predict_grad)
    reach_end = CH + POS_K * WIDTH

    def put_side(first, values, group=slice(0, D)):
        if len(side_ref.shape) == 2:
            side_ref[group, first : first + values.shape[1]] = values
            return
        rows, width = side_ref.shape[2:]
        owners = slice(group.start // rows, group.stop // rows)
        for n in range(side_ref.shape[1]):
            low_end = max(first, n * width)
            high_end = min(first + values.shape[1], (n + 1) * width)
            if low_end < high_end:
                part = values[:, low_end - first : high_end - first]
                side_ref[owners, n, :, low_end - n * width : high_end - n * width] = part.reshape(
                    owners.stop - owners.start, rows, high_end - low_end
                )

    put_side(reach_end, t_mm(student_low, predict_low))
    grad = mm_t(predict_low, head_ref[...])

    def norm_step(grad, index):
        back, gain, shift = norm_bwd(kept(index), vec(2 * index), grad)
        vector_ref[2 * index : 2 * index + 1, :] = gain[None]
        vector_ref[2 * index + 1 : 2 * index + 2, :] = shift[None]
        return back

    grad = norm_step(grad, 2)
    down = bf(grad)
    left_ref[3] = down
    for start in range(0, weight_ref.shape[2], D):
        cols = slice(start, start + D)
        wide_grad = bf(mm(down, weight_ref[2, :, cols]) * gelu_slope(wide_ref[:, cols]))
        right_ref[1, :, cols] = wide_grad
        grad = grad + mm_t(wide_grad, weight_ref[1, :, cols])
    grad = norm_step(grad, 1)
    down = bf(grad)
    right_ref[0, :, 3 * D :] = down
    outs_grad = mm_t(down, weight_ref[0, :, 3 * D :])
    for pair in range(HEADS // 2):
        lo = pair * 2 * HEAD_DIM
        hi = lo + 2 * HEAD_DIM
        query = triple_ref[:, lo:hi]
        key = triple_ref[:, D + lo : D + hi]
        value = triple_ref[:, 2 * D + lo : 2 * D + hi]
        sums = [None, None, None]
        for upper in range(2):
            out_low = bf(lane_half(outs_grad[:, lo:hi], upper))
            chances = chance_ref[2 * pair + upper]
            chance_grad = mm_t(out_low, value)
            score_grad = chances * (
                chance_grad - jnp.sum(chance_grad * chances, axis=-1, keepdims=True)
            )
            score_grad = bf(score_grad * (1.0 / math.sqrt(HEAD_DIM)))
            parts = (
                lane_half(mm(score_grad, key), upper),
                lane_half(t_mm(score_grad, query), upper),
                t_mm(bf(chances), out_low),
            )
            for index in range(3):
                sums[index] = parts[index] if upper == 0 else sums[index] + parts[index]
        for index in range(3):
            right_ref[0, :, index * D + lo : index * D + hi] = bf(sums[index])
    grad = grad + mm_t(right_ref[0, :, : 3 * D], weight_ref[0, :, : 3 * D])
    grad = norm_step(grad, 0)
    mixed_grad = grad * gelu_slope(mixed_ref[...])
    vector_ref[7:8, :] = total_sum(mixed_grad)
    mixed_low = bf(mixed_grad)
    grad = grad + position_sum(mixed_low.astype(F32), near, spread_ref, True)
    shifted = bf(values).astype(F32)
    half = D // 2
    for offset in range(POS_K):
        taps = taps_of(shifted, near, offset, False)
        for part in range(2):
            cols = slice(part * half, (part + 1) * half)
            full = t_mm(taps[:, cols], mixed_low[:, cols])
            pieces = [
                full[g * WIDTH : (g + 1) * WIDTH, g * WIDTH : (g + 1) * WIDTH]
                for g in range(half // WIDTH)
            ]
            put_side(CH + offset * WIDTH, jnp.concatenate(pieces, axis=0), cols)
    vector_ref[9:10, :] = total_sum(jnp.where(chosen, grad, 0.0))
    grad = jnp.where(chosen, 0.0, grad)
    vector_ref[6:7, :] = total_sum(grad)
    feat_low = bf(grad)
    put_side(0, t_mm(feat_low, normed_ref[...]))
    normed_grad_ref[...] = mm(feat_low, project_ref[...])


def spread_kernel(side_ref, tile_ref, spread_ref):
    half = D // 2
    rows = lax.broadcasted_iota(jnp.int32, (half, half), 0) // WIDTH
    cols = lax.broadcasted_iota(jnp.int32, (half, half), 1) // WIDTH
    same = rows == cols
    for offset in range(POS_K):
        piece = side_ref[:, offset * WIDTH : (offset + 1) * WIDTH]
        for part in range(2):
            wide = mm(piece[part * half : (part + 1) * half], tile_ref[...])
            spread_ref[offset, part * half : (part + 1) * half, :] = bf(
                jnp.where(same, wide, 0.0)
            )


def block_grad_kernel(place_ref, left_ref, left_two_ref, right_ref, right_two_ref,
                      send_top_ref, keep_top_ref, send_low_ref, keep_low_ref, full_ref):
    line, unused, unused_two, half, cols = keep_top_ref.shape
    x = place_ref[0]
    far = pl.program_id(1)
    full_ref[...] = t_mm(left_ref[0], right_ref[0]) + t_mm(left_two_ref[0], right_two_ref[0])
    for z in range(line):
        start = lambda index: pl.multiple_of((2 * z + index) * 2 * half, 8)
        keep_top_ref[z, 0, 0] = full_ref[pl.ds(start(x), half), :]
        send_top_ref[z, 0, 0] = bf(full_ref[pl.ds(start(1 - x), half), :])

    @pl.when(far == 0)
    def _():
        for z in range(line):
            for index in range(2):
                row = (2 * z + index) * 2 * half + half
                keep_low_ref[z, index, 0] = full_ref[row : row + half, :]

    @pl.when(far == 1)
    def _():
        for z in range(line):
            for index in range(2):
                row = (2 * z + index) * 2 * half + half
                send_low_ref[z, index, 0] = bf(full_ref[row : row + half, :])


def block_grads(left, left_two, right, right_two, place, n_dp, n_narrow):
    frames = left.shape[1]
    cols = right.shape[2] // n_narrow
    half = D // n_dp // 2
    line = n_dp // 2
    shape = jax.ShapeDtypeStruct

    def narrow(far, place):
        return 2 * (place[1] ^ far) + place[2]

    def left_index(matrix, far, place):
        is_out = (narrow(far, place) + 1) * cols > 3 * D
        return (jnp.where(matrix == 0, jnp.where(is_out, 1, 0), matrix + 1), 0, 0)

    left_spec = pl.BlockSpec((1, frames, D), left_index)
    right_spec = pl.BlockSpec(
        (1, frames, cols), lambda matrix, far, place: (matrix, 0, narrow(far, place))
    )
    top_spec = pl.BlockSpec(
        (line, 1, 1, half, cols), lambda matrix, far, place: (0, place[1] ^ far, matrix, 0, 0)
    )
    low_spec = pl.BlockSpec(
        (line, 2, 1, half, cols), lambda matrix, far, place: (0, 0, matrix, 0, 0)
    )
    whole = (line, 2, 3, half, cols)
    return pl.pallas_call(
        block_grad_kernel,
        grid_spec=pltpu.PrefetchScalarGridSpec(
            num_scalar_prefetch=1,
            grid=(3, 2),
            in_specs=[left_spec, left_spec, right_spec, right_spec],
            out_specs=[top_spec, top_spec, low_spec, low_spec],
            scratch_shapes=[pltpu.VMEM((D, cols), F32)],
        ),
        out_shape=[shape(whole, BF16), shape(whole, F32), shape(whole, BF16), shape(whole, F32)],
        name="block_grads",
    )(place, left, left_two, right, right_two)


def plain_weight_grads(left, right, n_dp, n_narrow):
    full = [
        jnp.concatenate(
            [t_mm(left[0], right[0, :, : 3 * D]), t_mm(left[1], right[0, :, 3 * D :])], axis=1
        ),
        t_mm(left[2], right[1]),
        t_mm(left[3], right[2]),
    ]
    full = jnp.stack(full, 0)
    full = full.reshape(3, n_dp, D // n_dp, n_narrow, full.shape[2] // n_narrow)
    return full.transpose(1, 3, 0, 2, 4)


def spread_kernels(side_conv):
    tile = np.zeros((WIDTH, D // 2), np.float32)
    for column in range(D // 2):
        tile[column % WIDTH, column] = 1.0
    return pl.pallas_call(
        spread_kernel,
        in_specs=[VMEM, VMEM],
        out_specs=VMEM,
        out_shape=jax.ShapeDtypeStruct((POS_K, D, D // 2), BF16),
        name="spread",
        compiler_params=pltpu.CompilerParams(vmem_limit_bytes=LIMIT),
    )(side_conv, jnp.asarray(tile, BF16))


def flat_pieces(pieces):
    if not isinstance(pieces, list):
        return [pieces], pieces.shape[-1] * (pieces.shape[1] if pieces.ndim == 5 else 1)
    flat = [piece for half in pieces for row in half for column in row for piece in column]
    return flat, flat[0].shape[-1] * 8


def teacher_target(feats, near, col, row, spread, vec, pieces, place):
    pieces, width = flat_pieces(pieces)
    return pl.pallas_call(
        teacher_kernel,
        in_specs=[SMEM] + [VMEM] * 6 + [ANY] * len(pieces),
        out_specs=VMEM,
        out_shape=jax.ShapeDtypeStruct(feats.shape, F32),
        scratch_shapes=[pltpu.VMEM((3, D, width), BF16), pltpu.SemaphoreType.DMA((3,))],
        name="teacher",
        compiler_params=pltpu.CompilerParams(vmem_limit_bytes=LIMIT),
    )(place, feats, near, col, row, spread, vec, *pieces)


def student_step(feats, near, col, row, mask, weight, spread, vec, target, normed, project, head,
                 pieces, place, side_shape):
    pieces, width = flat_pieces(pieces)
    frames = feats.shape[0]
    shape = jax.ShapeDtypeStruct
    return pl.pallas_call(
        student_kernel,
        in_specs=[SMEM] + [VMEM] * 12 + [ANY] * len(pieces),
        out_specs=[VMEM] * 6,
        out_shape=[
            shape((4, frames, D), BF16),
            shape((3, frames, width), BF16),
            shape(side_shape, F32),
            shape((10, D), F32),
            shape((frames, CH), F32),
            shape((8, 128), F32),
        ],
        scratch_shapes=[
            pltpu.VMEM((3, D, width), BF16),
            pltpu.VMEM((HEADS, frames, frames), F32),
            pltpu.VMEM((frames, width), F32),
            pltpu.VMEM((frames, 3 * D), BF16),
            pltpu.VMEM((frames, D), F32),
            pltpu.VMEM((3, frames, D), F32),
            pltpu.VMEM((3, frames, 128), F32),
            pltpu.SemaphoreType.DMA((3,)),
        ],
        name="student",
        compiler_params=pltpu.CompilerParams(vmem_limit_bytes=LIMIT),
    )(
        place, feats, near, col, row, mask, weight, spread, vec, target, normed, project, head,
        *pieces,
    )


class Links:
    def __init__(self, n_dp, n_narrow):
        self.n_dp, self.n_narrow = n_dp, n_narrow
        self.line = n_dp // 2
        self.direct = n_narrow == 4 and n_dp % 2 == 0 and self.line <= 4 and D % (16 * n_dp) == 0
        dp, narrow = lax.axis_index("dp"), lax.axis_index("narrow")
        self.z, self.x, self.y, self.c = dp // 2, dp % 2, narrow // 2, narrow % 2

    def swap_c(self, values):
        return self.flip(values, "narrow", 1)

    def swap_y(self, values):
        return self.flip(values, "narrow", 2)

    def swap_x(self, values):
        return self.flip(values, "dp", 1)

    def flip(self, values, axis, bit):
        size = self.n_dp if axis == "dp" else self.n_narrow
        return lax.ppermute(values, axis, [(i, i ^ bit) for i in range(size)])

    def step_z(self, values, up, senders):
        move = 1 if up else -1
        pairs = [(2 * z + x, 2 * (z + move) + x) for z in senders for x in range(2)]
        return lax.ppermute(values, "dp", pairs)

    def total(self, values, axes=("narrow", "dp")):
        for axis in axes:
            size = self.n_dp if axis == "dp" else self.n_narrow
            if size & (size - 1):
                values = lax.psum(values, axis)
                continue
            bit = 1
            while bit < size:
                values = values + self.flip(values, axis, bit)
                bit *= 2
        return values

    def go(self, requests):
        results = []
        for request in requests:
            kind, values = request[0], request[1]
            if kind == "c":
                results.append(self.flip(values, "narrow", 1))
            elif kind == "y":
                results.append(self.flip(values, "narrow", 2))
            elif kind == "x":
                results.append(self.flip(values, "dp", 1))
            else:
                results.append(self.step_z(values, kind == "up", request[2]))
        return results

    def gather_steps(self, values):
        last = self.line - 1
        ups, downs = [], []
        up = down = values
        for hop in range(1, self.line):
            up, down = yield [
                ("up", up, range(hop - 1, last)),
                ("down", down, range(1, self.line - hop + 1)),
            ]
            ups.append(up)
            downs.append(down)
        stacked = jnp.stack(ups[::-1] + [values] + downs, 0)
        column = lax.dynamic_slice_in_dim(stacked, last - self.z, self.line, 0)
        lanes = values.shape[-1] // 2
        one, two = column[..., :lanes], column[..., lanes:]
        one_y, two_x, one_x, two_y, one_c, two_c = yield [
            ("y", one), ("x", two), ("x", one), ("y", two), ("c", one), ("c", two)
        ]
        one_xy, two_xy, one_yc, two_xc, one_xc, two_yc = yield [
            ("x", one_y), ("y", two_x), ("c", one_y), ("c", two_x), ("c", one_x), ("c", two_y)
        ]
        one_xyc, two_xyc = yield [("c", one_xy), ("c", two_xy)]
        return [
            [[[one, one_c], [one_y, one_yc]], [[one_x, one_xc], [one_xy, one_xyc]]],
            [[[two, two_c], [two_y, two_yc]], [[two_x, two_xc], [two_xy, two_xyc]]],
        ]

    def gather_whole(self, values):
        if not self.direct:
            whole = lax.all_gather(values, "narrow", axis=2, tiled=True)
            return lax.all_gather(whole, "dp", axis=1, tiled=True)
        whole = lax.all_gather(values, ("dp", "narrow"), axis=0)
        return whole.reshape((self.n_dp, self.n_narrow) + values.shape)

    def split(self, values):
        values = values.reshape((self.line, 2, 2, 2) + values.shape[1:])
        pick = lambda index: lax.dynamic_index_in_dim(values, index, 3, False)
        return pick(1 - self.c), pick(self.c)

    def scatter_steps(self, parts, coarse):
        send, keep = parts
        half = send.shape[-2] // 2
        pick = lambda array, axis, index: lax.dynamic_index_in_dim(array, index, axis, False)
        short = bf if coarse else lambda array: array
        (got,) = yield [("c", send)]

        def both(rows, axis, index):
            return pick(keep[..., rows, :], axis, index) + pick(got[..., rows, :], axis, index)

        top, low_rows = slice(0, half), slice(half, None)
        ends = yield [
            ("x", short(both(top, 1, 1 - self.x))), ("y", short(both(low_rows, 2, 1 - self.y)))
        ]

        def all_three(rows, first, at_first, second, at_second, end):
            mine = [
                pick(pick(array[..., rows, :], first, at_first), second, at_second)
                for array in (keep, got)
            ]
            return mine[0] + mine[1] + pick(end, second, at_second).astype(F32)

        top_of = lambda index: all_three(top, 1, self.x, 1, index, ends[0])
        low_of = lambda index: all_three(low_rows, 2, self.y, 1, index, ends[1])
        more = yield [("y", top_of(1 - self.y)), ("x", low_of(1 - self.x))]
        one = top_of(self.y) + more[0]
        two = low_of(self.x) + more[1]
        return (yield from self.line_steps(jnp.concatenate([one, two], axis=-2)))

    def half_steps(self, send_top, keep_top, send_low, keep_low):
        pick = lambda array, index: lax.dynamic_index_in_dim(array, index, 1, False)
        top, lower = yield [("x", send_top), ("y", send_low)]
        top_of = lambda index: pick(keep_top, index) + pick(top, index).astype(F32)
        low_of = lambda index: pick(keep_low, index) + pick(lower, index).astype(F32)
        more = yield [("y", top_of(1 - self.y)), ("x", low_of(1 - self.x))]
        one, two = top_of(self.y) + more[0], low_of(self.x) + more[1]
        return (yield from self.line_steps(jnp.concatenate([one, two], axis=-2)))

    def line_steps(self, column):
        pick = lambda array, axis, index: lax.dynamic_index_in_dim(array, index, axis, False)
        last = self.line - 1
        at = lambda offset: pick(column, 0, (self.z + offset) % self.line)
        up = down = None
        for hop in range(last, 0, -1):
            send_up = at(hop) if up is None else at(hop) + up
            send_down = at(-hop) if down is None else at(-hop) + down
            up, down = yield [
                ("up", send_up, range(0, last - hop + 1)),
                ("down", send_down, range(hop, self.line)),
            ]
        own = at(0)
        return own if up is None else own + up + down


class Stages:
    def __init__(self, links, steps):
        self.links, self.steps = links, list(steps)
        self.requests = [next(one) for one in self.steps]
        self.results = [None] * len(self.steps)

    def tie(self, *others):
        arrays = [[request[1] for request in one] for one in self.requests]
        arrays, others = lax.optimization_barrier((arrays, others))
        self.requests = [
            [(request[0], array) + tuple(request[2:]) for request, array in zip(one, part)]
            for one, part in zip(self.requests, arrays)
        ]
        return others if len(others) != 1 else others[0]

    def add(self, one):
        self.steps.append(one)
        self.requests.append(next(one))
        self.results.append(None)

    def advance(self, after=()):
        got = [self.links.go(one) for one in self.requests]
        if after:
            got, after = lax.optimization_barrier((got, tuple(after)))
        for index, one in enumerate(self.steps):
            if not self.requests[index]:
                continue
            try:
                self.requests[index] = one.send(got[index])
            except StopIteration as stop:
                self.requests[index] = []
                self.results[index] = stop.value
        return after if len(after) != 1 else after[0]

    def finish(self):
        while any(self.requests):
            self.advance()
        return self.results


def adamw(weight, grad, first, second, power):
    first = DECAY * first + (1.0 - DECAY) * grad
    second = DECAY * second + (1.0 - DECAY) * grad * grad
    unbias = 1.0 - power
    step_size = first / unbias / (jnp.sqrt(second / unbias) + 1e-08)
    return (weight - LR_ADAM * (step_size + WEIGHT_DECAY * weight), first, second)


def exact(left, right):
    return jnp.einsum("brs,bst->brt", left, right, precision=HIGHEST)


def orthogonal(blocks, gram_total):
    gram = gram_total(jnp.einsum("brc,bsc->brs", blocks, blocks, precision=HIGHEST))
    scales = 1.0 / (jnp.sqrt(jnp.trace(gram, axis1=1, axis2=2)) + 1e-07)
    gram = gram * (scales * scales)[:, None, None]
    eye = jnp.eye(gram.shape[1], dtype=F32)[None]
    whole = None
    for iteration in range(5):
        square = exact(gram, gram)
        step = COEFF_A * eye + COEFF_B * gram + COEFF_C * square
        whole = step if whole is None else exact(step, whole)
        if iteration < 4:
            gram = exact(exact(step, gram), step)
            gram = 0.5 * (gram + gram.transpose(0, 2, 1))
    return exact(whole * scales[:, None, None], blocks)


def per_device(
    wave,
    clip_ids,
    span_starts,
    step_count,
    conv_small,
    conv_stack,
    side,
    vectors,
    block,
    teacher_block,
    teacher_vectors,
    small_mean,
    small_square,
    stack_mean,
    stack_square,
    side_mean,
    side_square,
    vector_mean,
    vector_square,
    block_momentum,
    n_dp,
    n_narrow,
):
    everyone = ("dp", "narrow")
    frames = clip_ids.shape[0]
    rows_here, cols_here = block.shape[1:]
    side_rows, side_cols = side.shape
    links = Links(n_dp, n_narrow)
    place = jnp.stack([links.x, links.y, links.c]).astype(jnp.int32)
    stack_rows_here = conv_stack.shape[0]
    side_size = side_rows * side_cols
    side_lines = -(-side_size // CH)
    lines = -(-(stack_rows_here + side_lines) // 16) * 16
    side_flat = jnp.pad(bf(side).reshape(-1), (0, side_lines * CH - side_size))
    send = jnp.concatenate(
        [
            bf(conv_stack),
            side_flat.reshape(side_lines, CH),
            jnp.zeros((lines - stack_rows_here - side_lines, CH), BF16),
        ],
        axis=0,
    )
    stack = lax.all_gather(send, everyone, axis=0)
    teacher_pieces = links.gather_whole(bf(teacher_block))
    masked = masked_of(span_starts)
    masked_here = jnp.full((1, 128), jnp.sum(masked.astype(F32)), F32)
    total = jnp.maximum(links.total(masked_here)[0, 0], 1.0)
    small_low = low(conv_small)
    vector_low = low(vectors)
    taps = first_taps(wave, frames)
    first_weights, hidden, hidden_tail = first_layer(small_low, taps, frames)
    whole_side = stack[:, stack_rows_here : stack_rows_here + side_lines].reshape(
        n_dp * n_narrow, side_lines * CH
    )[:, :side_size]
    whole_side = (
        whole_side.reshape(n_dp, n_narrow, side_rows, side_cols)
        .transpose(0, 2, 1, 3)
        .reshape(n_dp * side_rows, n_narrow * side_cols)
    )
    spread_of = lambda: spread_kernels(whole_side[:, CH : CH + POS_K * WIDTH])
    if links.direct:
        exchange = Stages(links, [links.gather_steps(bf(block))])
        hidden = exchange.advance((hidden,))
        for unused in range(links.line - 2):
            exchange.advance()
        hidden = exchange.tie(hidden)
        outs = encode_fwd(small_low, stack, hidden, hidden_tail, frames)
        outs = list(outs)
        outs[13] = exchange.advance((outs[13],))
        whole_side = exchange.tie(whole_side)
        spread = spread_of()
    else:
        student_pieces = links.gather_whole(bf(block))
        outs = encode_fwd(small_low, stack, hidden, hidden_tail, frames)
        spread = spread_of()
    normed = outs[13]
    project = whole_side[:, :CH]
    head = whole_side[:, CH + POS_K * WIDTH :]
    near = jnp.pad(neighbours(clip_ids).astype(F32).T, ((0, 0), (0, 32 - POS_K)))
    col, row = clip_ids[:, None], clip_ids[None, :]
    feats = mm_t(normed, project) + vector_low[6]
    target = teacher_target(
        feats, near, col, row, spread, low(teacher_vectors), teacher_pieces, place
    )
    if links.direct:
        target = exchange.advance((target,))
        (student_pieces,) = exchange.finish()
    weight = jnp.full((8, 128), 1.0 / (total * math.sqrt(D)), F32)
    left, right, side_grad, vector_grad, normed_grad, loss_tile = student_step(
        feats,
        near,
        col,
        row,
        masked.astype(F32)[:, None],
        weight,
        spread,
        vector_low,
        target,
        normed,
        project,
        head,
        student_pieces,
        place,
        (n_dp, n_narrow, side_rows, side_cols)
        if links.direct
        else (n_dp * side_rows, n_narrow * side_cols),
    )
    loss_part = loss_tile[0, 0]
    devices = n_dp * n_narrow
    if links.direct:
        core = links.c.astype(jnp.int32).reshape(1)
        others = [links.swap_c(left), links.swap_c(right)]
        parts = links.split(side_grad.reshape(devices, side_rows, side_cols))
        others, parts = lax.optimization_barrier((others, parts))
        grads = block_grads(left, others[0], right, others[1], place, n_dp, n_narrow)
        feed = Stages(links, [links.half_steps(*grads)])
        normed_grad = feed.tie(normed_grad)
        *parts_two, second, second_tail, norm_grad = encode_back(
            core, outs, small_low, stack, frames, normed_grad
        )
        second = feed.advance((second,))
        second = feed.tie(second)
        parts_two = second_dw(core, second, second_tail, hidden, hidden_tail, parts_two)
        shape = (links.line, 2, 2) + conv_stack.shape
        last = Stages(
            links, [links.scatter_steps([part.reshape(shape) for part in parts_two], False)]
        )
        second = last.tie(second)
        parts, second = lax.optimization_barrier((parts, second))
        rest = Stages(links, [links.scatter_steps(parts, False)])
        tap_grad = second_dx(second, second_tail, stack, taps, first_weights, frames)
        tap_grad = last.advance((tap_grad,))
        tap_grad = last.tie(tap_grad)
        tap_grad = feed.advance((tap_grad,))
        tap_grad = rest.advance((tap_grad,))
        (stack_piece,) = last.finish()
        (block_piece,) = feed.finish()
        (side_piece,) = rest.finish()
    else:
        sums = lambda values: lax.psum_scatter(
            values.reshape((-1,) + values.shape[-1:]), everyone, scatter_dimension=0, tiled=True
        )
        block_piece = sums(plain_weight_grads(left, right, n_dp, n_narrow))
        block_piece = block_piece.reshape(3, rows_here, cols_here)
        side_grad = side_grad.reshape(n_dp, side_rows, n_narrow, side_cols)
        side_piece = sums(side_grad.transpose(0, 2, 1, 3))
        core = jnp.zeros((1,), jnp.int32)
        *parts, second, second_tail, norm_grad = encode_back(
            core, outs, small_low, stack, frames, normed_grad
        )
        parts = second_dw(core, second, second_tail, hidden, hidden_tail, parts)
        tap_grad = second_dx(second, second_tail, stack, taps, first_weights, frames)
        stack_piece = sums(jnp.stack([parts[1], parts[0]], 1).reshape(sum(KERNELS) * CH, CH))
    small_grad = jnp.concatenate([tap_grad[:10], norm_grad], axis=0)
    packed = jnp.concatenate(
        [
            vector_grad,
            small_grad.reshape(-1, D),
            jnp.full((1, D), loss_part, F32),
        ],
        axis=0,
    )
    packed = links.total(packed)
    vector_total = packed[:10]
    small_total = packed[10:-1].reshape(small_grad.shape)
    loss_value = packed[-1, 0]
    shard_squares = (
        jnp.sum(block_piece * block_piece)
        + jnp.sum(side_piece * side_piece)
        + jnp.sum(stack_piece * stack_piece)
    )
    grad_norm = jnp.sqrt(
        links.total(jnp.full((1, 128), shard_squares, F32))[0, 0]
        + jnp.sum(small_total * small_total)
        + jnp.sum(vector_total * vector_total)
    )
    factor = jnp.minimum(1.0, CLIP_LIMIT / (grad_norm + 1e-06))
    power = jnp.power(DECAY, step_count[0].astype(F32))
    small_next = adamw(conv_small, factor * small_total, small_mean, small_square, power)
    stack_next = adamw(conv_stack, factor * stack_piece, stack_mean, stack_square, power)
    side_next = adamw(side, factor * side_piece, side_mean, side_square, power)
    vector_next = adamw(vectors, factor * vector_total, vector_mean, vector_square, power)
    momentum = DECAY * block_momentum + factor * block_piece
    ortho = orthogonal(momentum, lambda gram: links.total(gram, ("narrow",)))
    block_next = block * (1.0 - LR_MUON * WEIGHT_DECAY) - LR_MUON * ortho
    teacher_next = EMA_RATE * teacher_block + (1.0 - EMA_RATE) * block_next
    teacher_vec_next = EMA_RATE * teacher_vectors + (1.0 - EMA_RATE) * vector_next[0]
    return (
        (loss_value, grad_norm)
        + small_next
        + stack_next
        + side_next
        + vector_next
        + (block_next, momentum, teacher_next, teacher_vec_next, bf(block_next))
    )


def solution(mesh):
    n_dp, n_narrow = mesh.shape["dp"], mesh.shape["narrow"]

    def step(*arguments):
        return per_device(*arguments, n_dp, n_narrow)

    rows = P(("dp", "narrow"), None)
    flat = P(("dp", "narrow"))
    grid = P("dp", "narrow")
    cube = P(None, "dp", "narrow")
    one = P()
    in_specs = (
        (flat, flat, flat, one, one, rows, grid, one, cube, cube, one, one, one)
        + (rows, rows, grid, grid, one, one, cube)
    )
    out_specs = (
        (one, one, one, one, one, rows, rows, rows, grid, grid, grid, one, one, one)
        + (cube, cube, cube, one, cube)
    )
    return jax.shard_map(
        step, mesh=mesh, in_specs=in_specs, out_specs=out_specs, check_vma=False
    )
```

```python
import math

import jax
import jax.numpy as jnp
import numpy as np
from jax import lax
from jax.experimental import pallas as pl
from jax.experimental.pallas import tpu as pltpu
from jax.sharding import Mesh
from jax.sharding import PartitionSpec as P

D = 768
HEADS = 12
HEAD_DIM = 64
CH = 512
GROUPS = 16
WIDTH = D // GROUPS
POS_K = 19
REACH = POS_K // 2
SPAN = 10
TAIL = 16

EPS = 1e-05
VAR_FLOOR = 0.1
CLIP_LIMIT = 0.01
LR_ADAM = 0.03
LR_MUON = 2.0
DECAY = 0.5
WEIGHT_DECAY = 0.01
EMA_RATE = 0.5
KERNELS = (3, 3, 3, 3, 2, 2)
COEFF_A = 3.4445
COEFF_B = -4.775
COEFF_C = 2.0315
HIGHEST = lax.Precision.HIGHEST
F32 = jnp.float32
BF16 = jnp.bfloat16
LIMIT = 60 * 1024 * 1024
ROOT_HALF = math.sqrt(0.5)
ROOT_TAU = 1.0 / math.sqrt(2.0 * math.pi)


VMEM = pl.BlockSpec(memory_space=pltpu.VMEM)
ANY = pl.BlockSpec(memory_space=pl.ANY)
SMEM = pl.BlockSpec(memory_space=pltpu.SMEM)


def bf(values):
    return values.astype(BF16)


def low(values):
    return lax.optimization_barrier(values.astype(BF16)).astype(F32)


def dot(left, right, contract, batch=((), ())):
    return lax.dot_general(left, right, (contract, batch), preferred_element_type=F32)


def mm(left, right):
    return dot(left, right, ((1,), (0,)))


def mm_t(left, right):
    return dot(left, right, ((1,), (1,)))


def t_mm(left, right):
    return dot(left, right, ((0,), (0,)))


def gelu(values):
    return 0.5 * values * (1.0 + lax.erf(values * ROOT_HALF))


def gelu_slope(values):
    return 0.5 * (1.0 + lax.erf(values * ROOT_HALF)) + values * (
        ROOT_TAU * jnp.exp(-0.5 * values * values)
    )


def gelu_both(values):
    chance = 0.5 * (1.0 + lax.erf(values * ROOT_HALF))
    return values * chance, chance + values * (ROOT_TAU * jnp.exp(-0.5 * values * values))


def norm_fwd(values, gain, shift):
    center = values - jnp.mean(values, axis=-1, keepdims=True)
    scale = lax.rsqrt(jnp.mean(center * center, axis=-1, keepdims=True) + EPS)
    unit = center * scale
    return unit * gain + shift, (unit, scale)


def norm_bwd(kept, gain, grad):
    unit, scale = kept
    inner = grad * gain
    back = scale * (
        inner
        - jnp.mean(inner, axis=-1, keepdims=True)
        - unit * jnp.mean(inner * unit, axis=-1, keepdims=True)
    )
    return back, jnp.sum(grad * unit, axis=0), jnp.sum(grad, axis=0)


def first_taps(wave, frames):
    padded = jnp.pad(bf(wave), (0, 320 * (frames + 2) - wave.shape[0])).reshape(frames + 2, 320)
    rows = jnp.concatenate([padded[: frames + 1], padded[1:, :16]], axis=1)
    pick = np.zeros((336, 65 * 16), np.float32)
    for phase in range(64):
        for tap in range(10):
            pick[5 * phase + tap, 16 * phase + tap] = 1.0
    taps = bf(mm(rows, jnp.asarray(pick[:, : 64 * 16], BF16)))
    taps = taps.reshape(frames + 1, 64, 16).transpose(1, 0, 2)
    main = jnp.concatenate(
        [taps[:, :frames], taps[:1, 1:], jnp.zeros((1, frames, 16), BF16)], axis=0
    )
    return main, taps[:TAIL, frames]


def chooser(delta, rows_last=True):
    rows = lax.broadcasted_iota(jnp.int32, (TAIL, TAIL), 0)
    cols = lax.broadcasted_iota(jnp.int32, (TAIL, TAIL), 1)
    hit = cols == 2 * rows + delta if rows_last else rows == 2 * cols + delta
    return jnp.where(hit, 1.0, 0.0)


def stack_rows(ref, tap, taps=sum(KERNELS)):
    count = ref.shape[0] // taps
    rows = CH // count
    return ref[tap * count : (tap + 1) * count, :rows, :].reshape(CH, CH)


def first_kernel(taps_ref, weight_ref, out_ref):
    frames = taps_ref.shape[1]
    rows = taps_ref[...].reshape(2 * frames, taps_ref.shape[2])
    out_ref[...] = bf(gelu(mm(rows, weight_ref[...]))).reshape(out_ref.shape)


def encode_kernel(hidden_ref, tail_ref, stack_ref, small_ref, *refs):
    value_refs, hidden_refs = refs[:6], (hidden_ref,) + refs[6:11]
    value_tail_ref, hidden_tail_ref, normed_ref, unit_ref, scale_ref = refs[11:]
    frames = hidden_ref.shape[2]
    offset = 0
    tail = tail_ref[...]
    for layer, kernel in enumerate(KERNELS):
        source, values = hidden_refs[layer], value_refs[layer]
        count = values.shape[0]
        size = min(4, count)
        target = hidden_refs[layer + 1] if layer < 5 else None

        def product(index, offset=offset, kernel=kernel, source=source, size=size):
            total = None
            for tap in range(kernel):
                piece = source[pl.ds(index * size + tap // 2, size), tap % 2]
                part = mm(
                    piece.reshape(size * frames, CH),
                    stack_rows(stack_ref, offset // CH + tap),
                )
                total = part if total is None else total + part
            return total

        def step(index, carry, values=values, target=target, size=size, product=product):
            total = product(index)
            active, slope = gelu_both(total)
            values[pl.ds(index * size, size)] = slope.reshape(size, frames, CH)
            target[pl.ds(index * (size // 2), size // 2)] = bf(active).reshape(
                size // 2, 2, frames, CH
            )
            return carry

        if layer < 5:
            if count == size:
                step(0, 0)
            else:
                lax.fori_loop(0, count // size, step, 0)
        else:
            total = product(0)
            encoded, slope = gelu_both(total)
            values[...] = slope.reshape(values.shape)
            normed, kept = norm_fwd(encoded, small_ref[10:11, :], small_ref[11:12, :])
            normed_ref[...] = bf(normed)
            unit_ref[...] = kept[0]
            scale_ref[...] = jnp.broadcast_to(kept[1], scale_ref.shape)
        if layer < 3:
            total = None
            for tap in range(kernel):
                part = mm(
                    bf(mm(bf(chooser(tap)), tail)),
                    stack_rows(stack_ref, offset // CH + tap),
                )
                total = part if total is None else total + part
            active, slope = gelu_both(total)
            value_tail_ref[layer] = slope
            tail = bf(active)
            hidden_tail_ref[layer] = tail
            head = target[0, 0].astype(F32)
            rows = lax.broadcasted_iota(jnp.int32, (frames, CH), 0)
            moved = jnp.where(
                rows == frames - 1, active[0:1].astype(BF16).astype(F32),
                pltpu.roll(head, frames - 1, 0),
            )
            target[count // 2, 0] = bf(moved)
            target[count // 2, 1] = jnp.zeros((frames, CH), BF16)
        offset += kernel * CH


def layer_dw(grad_ref, source_ref, tail_grad, source_tail, kernel, out_ref):
    count, frames = grad_ref.shape[:2]
    size = min(8, count)
    for tap in range(kernel):
        rows = slice(tap * CH, (tap + 1) * CH)
        if tail_grad is None:
            out_ref[rows, :] = jnp.zeros((CH, CH), F32)
        else:
            out_ref[rows, :] = t_mm(bf(mm(bf(chooser(tap)), source_tail)), tail_grad)

        def step(index, carry, tap=tap, rows=rows):
            piece = source_ref[pl.ds(index * size + tap // 2, size), tap % 2]
            grad = grad_ref[pl.ds(index * size, size)]
            out_ref[rows, :] += t_mm(
                piece.reshape(size * frames, CH), grad.reshape(size * frames, CH)
            )
            return carry

        if count == size:
            step(0, 0)
        else:
            lax.fori_loop(0, count // size, step, 0)


def layer_dx(grad_ref, tail_grad, kernel, weight_of, slope, write, carry_ref, head_ref):
    count, frames = grad_ref.shape[:2]
    size = min(4, count)
    carry_ref[...] = jnp.zeros((frames, CH), F32)

    def step(index, unused):
        grad = grad_ref[pl.ds(index * size, size)].reshape(size * frames, CH)
        even = mm_t(grad, weight_of(0)).reshape(size, frames, CH)
        odd = mm_t(grad, weight_of(1)).reshape(size, frames, CH)
        if kernel == 3:
            late = mm_t(grad, weight_of(2)).reshape(size, frames, CH)
            before = carry_ref[...][None]
            if size > 1:
                before = jnp.concatenate([before, late[:-1]], axis=0)
            even = even + before
            carry_ref[...] = late[-1]
        write(index, size, even, odd)
        return unused

    if count == size:
        step(0, 0)
    else:
        lax.fori_loop(0, count // size, step, 0)
    if kernel != 3:
        return None
    wrap = carry_ref[...]
    rows = lax.broadcasted_iota(jnp.int32, (frames, CH), 0)
    head_ref[...] = jnp.where(rows == 0, 0.0, pltpu.roll(wrap, 1, 0))
    first = lax.broadcasted_iota(jnp.int32, (TAIL, CH), 0) == 0
    back = jnp.where(first, wrap[frames - 1 : frames, :], 0.0)
    if tail_grad is not None:
        for tap in range(3):
            back = back + jnp.dot(
                chooser(tap, False), mm_t(tail_grad, weight_of(tap)),
                precision=HIGHEST, preferred_element_type=F32,
            )
    return back


def copy_halves(order, core_ref, held, send_ref, keep_ref, first, taps, sem):
    half = CH // 2
    core = core_ref[0]
    copies = []
    for tap in range(taps):
        for target, index in ((send_ref, 1 - core), (keep_ref, core)):
            start = pl.multiple_of(tap * CH + index * half, half)
            place = order[first + tap]
            copies.append(
                pltpu.make_async_copy(held.at[pl.ds(start, half)], target.at[place], sem)
            )
            copies[-1].start()
    return copies


def encode_back_kernel(order, core_ref, grad_ref, unit_ref, scale_ref, small_ref, stack_ref, *refs):
    value_refs, hidden_refs = refs[:6], refs[6:11]
    value_tail_ref, hidden_tail_ref = refs[11:13]
    send_ref, keep_ref, second_ref, second_tail_ref, norm_ref = refs[13:18]
    grad_refs = (second_ref,) + refs[18:23]
    buffer_ref, carry_ref, head_ref, even_ref, sems = refs[23:]
    frames = grad_ref.shape[0]
    grad, gain, shift = norm_bwd(
        (unit_ref[...], scale_ref[:, :1]), small_ref[10:11, :], grad_ref[...]
    )
    norm_ref[0:1, :] = gain[None]
    norm_ref[1:2, :] = shift[None]
    grad_refs[5][0] = bf(grad * value_refs[5][0])
    tail_grad = None
    offset = sum(KERNELS) * CH
    copies = [[], []]
    for layer in range(5, 0, -1):
        kernel = KERNELS[layer]
        offset -= kernel * CH
        slot = layer % 2
        for copy in copies[slot]:
            copy.wait()
        held = buffer_ref.at[slot, 0 : kernel * CH]
        tail_source = None if tail_grad is None else hidden_tail_ref[layer - 1]
        layer_dw(grad_refs[layer], hidden_refs[layer - 1], tail_grad, tail_source, kernel, held)
        copies[slot] = copy_halves(
            order, core_ref, held, send_ref, keep_ref, offset // CH, kernel, sems.at[slot]
        )
        values, target = value_refs[layer - 1], grad_refs[layer - 1]

        def weight_of(tap, offset=offset):
            return stack_rows(stack_ref, offset // CH + tap)

        def write(index, size, even, odd, values=values, target=target, kernel=kernel):
            if kernel == 3:
                if not isinstance(index, int):
                    @pl.when(index == 0)
                    def _():
                        even_ref[...] = even[0]
                else:
                    even_ref[...] = even[0]
            for item in range(size):
                place = 2 * (index * size + item)
                target[place] = bf(even[item] * values[place])
                target[place + 1] = bf(odd[item] * values[place + 1])

        back = layer_dx(grad_refs[layer], tail_grad, kernel, weight_of, None, write,
                        carry_ref, head_ref)
        tail_grad = None
        if kernel == 3:
            target[0] = bf((even_ref[...] + head_ref[...]) * values[0])
            tail_grad = bf(back * value_tail_ref[layer - 1])
    second_tail_ref[...] = tail_grad
    for copy in copies[0] + copies[1]:
        copy.wait()


def second_dw_kernel(order, core_ref, grad_ref, tail_grad_ref, hidden_ref, tail_ref, old_send_ref,
                     old_keep_ref, send_ref, keep_ref, buffer_ref, sem):
    layer_dw(grad_ref, hidden_ref, tail_grad_ref[...], tail_ref[...], 3, buffer_ref)
    for copy in copy_halves(
        order, core_ref, buffer_ref, send_ref, keep_ref, 0, 3, sem
    ):
        copy.wait()


def second_dx_kernel(grad_ref, tail_grad_ref, weight_ref, taps_ref, tail_taps_ref, first_ref,
                     out_ref, carry_ref, head_ref, even_ref):
    frames = grad_ref.shape[1]
    weights = first_ref[...]
    out_ref[...] = jnp.zeros(out_ref.shape, F32)

    def piece(place, grad):
        rows = taps_ref[place]
        low_grad = bf(grad * gelu_slope(mm(rows, weights)))
        return t_mm(rows, low_grad)

    def write(index, size, even, odd):
        @pl.when(index == 0)
        def _():
            even_ref[...] = even[0]

        for item in range(size):
            place = 2 * (index * size + item)
            grad = even[item]
            if item == 0:
                grad = jnp.where(index == 0, 0.0, grad)
            out_ref[...] += piece(place, grad) + piece(place + 1, odd[item])

    def weight_of(tap):
        return stack_rows(weight_ref, tap, 3)

    back = layer_dx(grad_ref, tail_grad_ref[...], 3, weight_of, None, write, carry_ref, head_ref)
    out_ref[...] += piece(0, even_ref[...] + head_ref[...])
    rows = tail_taps_ref[...]
    out_ref[...] += t_mm(rows, bf(back * gelu_slope(mm(rows, weights))))


COUNTS = (32, 16, 8, 4, 2, 1)


def kernel_params():
    return pltpu.CompilerParams(vmem_limit_bytes=LIMIT)


def first_layer(small, taps, frames):
    main, tail = taps
    weights = jnp.pad(bf(small[:10]), ((0, 6), (0, 0)))
    hidden = pl.pallas_call(
        first_kernel,
        grid=(33,),
        in_specs=[
            pl.BlockSpec((2, frames, 16), lambda i: (i, 0, 0)),
            pl.BlockSpec((16, CH), lambda i: (0, 0)),
        ],
        out_specs=pl.BlockSpec((1, 2, frames, CH), lambda i: (i, 0, 0, 0)),
        out_shape=jax.ShapeDtypeStruct((33, 2, frames, CH), BF16),
        name="first_layer",
    )(main, weights)
    return weights, hidden, bf(gelu(mm(tail, weights)))


def encode_fwd(small, stack, hidden, hidden_tail, frames):
    shape = jax.ShapeDtypeStruct
    return pl.pallas_call(
        encode_kernel,
        in_specs=[VMEM] * 4,
        out_specs=[VMEM] * 16,
        out_shape=[shape((count, frames, CH), F32) for count in COUNTS]
        + [shape((count // 2 + 1, 2, frames, CH), BF16) for count in COUNTS[:5]]
        + [
            shape((3, TAIL, CH), F32),
            shape((3, TAIL, CH), BF16),
            shape((frames, CH), BF16),
            shape((frames, CH), F32),
            shape((frames, 128), F32),
        ],
        name="encode",
        compiler_params=kernel_params(),
    )(hidden, hidden_tail, stack, small)


def encode_back(order, core, outs, small, stack, frames, grad):
    shape = jax.ShapeDtypeStruct
    plane = pltpu.VMEM((frames, CH), F32)
    part = shape((sum(KERNELS), CH // 2, CH), F32)
    return pl.pallas_call(
        lambda *refs: encode_back_kernel(order, *refs),
        in_specs=[SMEM] + [VMEM] * 18,
        out_specs=[ANY, ANY, VMEM, VMEM, VMEM],
        out_shape=[
            part,
            part,
            shape((COUNTS[0], frames, CH), BF16),
            shape((TAIL, CH), BF16),
            shape((2, CH), F32),
        ],
        scratch_shapes=[pltpu.VMEM((count, frames, CH), BF16) for count in COUNTS[1:]]
        + [
            pltpu.VMEM((2, 3 * CH, CH), F32),
            plane,
            plane,
            plane,
            pltpu.SemaphoreType.DMA((2,)),
        ],
        name="encode_back",
        compiler_params=kernel_params(),
    )(core, grad, outs[14], outs[15], small, stack, *outs[:13])


def second_dw(order, core, second, second_tail, hidden, hidden_tail, parts):
    return pl.pallas_call(
        lambda *refs: second_dw_kernel(order, *refs),
        in_specs=[SMEM] + [VMEM] * 4 + [ANY, ANY],
        out_specs=[ANY, ANY],
        out_shape=[jax.ShapeDtypeStruct(part.shape, F32) for part in parts],
        scratch_shapes=[pltpu.VMEM((3 * CH, CH), F32), pltpu.SemaphoreType.DMA],
        input_output_aliases={5: 0, 6: 1},
        name="second_dw",
        compiler_params=kernel_params(),
    )(core, second, second_tail, hidden, hidden_tail, *parts)


def second_dx(second, second_tail, stack, taps, weights, frames):
    main, tail = taps
    plane = pltpu.VMEM((frames, CH), F32)
    parts = 3 * stack.shape[0] // sum(KERNELS)
    return pl.pallas_call(
        second_dx_kernel,
        grid=(1,),
        in_specs=[
            VMEM,
            VMEM,
            pl.BlockSpec((parts,) + stack.shape[1:], lambda i: (0, 0, 0)),
            VMEM,
            VMEM,
            VMEM,
        ],
        out_specs=VMEM,
        out_shape=jax.ShapeDtypeStruct((16, CH), F32),
        scratch_shapes=[plane, plane, plane],
        name="second_dx",
        compiler_params=kernel_params(),
    )(second, second_tail, stack, main, tail, weights)


def neighbours(segment):
    frames = segment.shape[0]
    padded = jnp.pad(segment, (REACH, REACH), constant_values=-1)
    return jnp.stack([padded[offset : offset + frames] == segment for offset in range(POS_K)], 0)


def masked_of(starts):
    frames = starts.shape[0]
    padded = jnp.pad(starts, (SPAN - 1, 0))
    return (
        jnp.max(jnp.stack([padded[offset : offset + frames] for offset in range(SPAN)], 0), axis=0)
        > 0
    )


def taps_of(values, near, offset, flip):
    frames = values.shape[0]
    lane = 2 * REACH - offset if flip else offset
    shift = (REACH - lane) % frames
    rolled = values if shift == 0 else pltpu.roll(values, shift, 0)
    return bf(jnp.where(near[:, lane : lane + 1] > 0.0, rolled, 0.0))


def position_sum(values, near, spread_ref, back):
    half = D // 2
    sums = [None, None]
    for offset in range(POS_K):
        taps = taps_of(values, near, offset, back)
        for side in range(2):
            weight = spread_ref[offset, side * half : (side + 1) * half, :]
            piece = taps[:, side * half : (side + 1) * half]
            part = mm_t(piece, weight) if back else mm(piece, weight)
            sums[side] = part if sums[side] is None else sums[side] + part
    return jnp.concatenate(sums, axis=1)


def lane_half(values, upper):
    lanes = lax.broadcasted_iota(jnp.int32, values.shape, 1)
    keep = lanes >= HEAD_DIM if upper else lanes < HEAD_DIM
    return jnp.where(keep, values, 0.0)


def start_copies(place_ref, piece_refs, weight_ref, sems):
    if len(piece_refs) == 1 and len(piece_refs[0].shape) == 5:
        n_dp, n_narrow, unused, rows, cols = piece_refs[0].shape
        copies = []
        for matrix in range(3):
            for d in range(n_dp):
                for n in range(n_narrow):
                    copy = pltpu.make_async_copy(
                        piece_refs[0].at[d, n, matrix],
                        weight_ref.at[
                            matrix, pl.ds(d * rows, rows), pl.ds(n * cols, cols)
                        ],
                        sems.at[matrix],
                    )
                    copy.start()
                    copies.append(copy)
        return copies
    if len(piece_refs) == 1:
        copies = [
            pltpu.make_async_copy(piece_refs[0].at[m], weight_ref.at[m], sems.at[m])
            for m in range(3)
        ]
        for copy in copies:
            copy.start()
        return copies
    line, unused, rows, cols = piece_refs[0].shape
    lanes = cols // 2
    x, y, c = place_ref[0], place_ref[1], place_ref[2]
    column, one_y, two_x, one_x, two_y, one_xy, two_xy, column_c, next_c, far_c = piece_refs
    pieces = [
        (column, None, None, 0, 0, 0), (column_c, None, None, 0, 0, 1),
        (one_y, None, 0, 0, 1, 0), (two_x, None, 1, 1, 0, 0),
        (one_x, None, 0, 1, 0, 0), (two_y, None, 1, 0, 1, 0),
        (next_c, 0, 0, 0, 1, 1), (next_c, 1, 1, 1, 0, 1),
        (next_c, 2, 0, 1, 0, 1), (next_c, 3, 1, 0, 1, 1),
        (one_xy, None, 0, 1, 1, 0), (two_xy, None, 1, 1, 1, 0),
        (far_c, 0, 0, 1, 1, 1), (far_c, 1, 1, 1, 1, 1),
    ]
    copies = []
    for matrix in range(3):
        for ref, index, half, dx, dy, dc in pieces:
            width = cols if half is None else lanes
            narrow = (y ^ dy) * 2 + (c ^ dc)
            col = pl.multiple_of(narrow * cols + (half or 0) * lanes, 128)
            for z in range(line):
                row = pl.multiple_of((2 * z + (x ^ dx)) * rows, 16)
                source = ref.at[z, matrix] if index is None else ref.at[index, z, matrix]
                copy = pltpu.make_async_copy(
                    source,
                    weight_ref.at[matrix, pl.ds(row, rows), pl.ds(col, width)],
                    sems.at[matrix],
                )
                copy.start()
                copies.append(copy)
    return copies


def await_copies(copies, matrix):
    count = len(copies) // 3
    for copy in copies[matrix * count : (matrix + 1) * count]:
        copy.wait()


def run_block(values, near, attend, spread_ref, weight_ref, vec_ref, copies, keep):
    vec = lambda row: vec_ref[row : row + 1, :]
    frames = values.shape[0]
    mixed = position_sum(bf(values).astype(F32), near, spread_ref, False) + vec(7)
    hidden, norm_one = norm_fwd(values + gelu(mixed), vec(0), vec(1))
    hidden_low = bf(hidden)
    await_copies(copies, 0)
    triple = bf(mm(hidden_low, weight_ref[0, :, : 3 * D]))
    outs = []
    for pair in range(HEADS // 2):
        lo = pair * 2 * HEAD_DIM
        hi = lo + 2 * HEAD_DIM
        query = triple[:, lo:hi].astype(F32)
        key = triple[:, D + lo : D + hi]
        value = triple[:, 2 * D + lo : 2 * D + hi]
        both = []
        for upper in range(2):
            scores = mm_t(bf(lane_half(query, upper)), key) * (1.0 / math.sqrt(HEAD_DIM))
            scores = jnp.where(attend, scores, -1e30)
            raised = jnp.exp(scores - jnp.max(scores, axis=-1, keepdims=True))
            chances = raised / jnp.sum(raised, axis=-1, keepdims=True)
            if keep is not None:
                keep["chances"][2 * pair + upper] = chances
            both.append(lane_half(mm(bf(chances), value), upper))
        outs.append(bf(both[0] + both[1]))
    outs = jnp.concatenate(outs, axis=1)
    second, norm_two = norm_fwd(hidden + mm(outs, weight_ref[0, :, 3 * D :]), vec(2), vec(3))
    second_low = bf(second)
    await_copies(copies, 1)
    await_copies(copies, 2)
    total = second
    step = D
    for start in range(0, weight_ref.shape[2], step):
        wide = mm(second_low, weight_ref[1, :, start : start + step])
        inner = bf(gelu(wide))
        if keep is not None:
            keep["wide"][:, start : start + step] = wide
            keep["right"][2, :, start : start + step] = inner
        total = total + mm_t(inner, weight_ref[2, :, start : start + step])
    result, norm_three = norm_fwd(total, vec(4), vec(5))
    if keep is not None:
        keep["triple"][...] = triple
        keep["mixed"][...] = mixed
        keep["left"][0] = hidden_low
        keep["left"][1] = outs
        keep["left"][2] = second_low
        for index, kept in enumerate((norm_one, norm_two, norm_three)):
            keep["units"][index] = kept[0]
            keep["scales"][index] = jnp.broadcast_to(kept[1], (frames, 128))
    return result


def teacher_kernel(place_ref, feat_ref, near_ref, col_ref, row_ref, spread_ref, vec_ref, *refs):
    piece_refs, (target_ref, weight_ref, sems) = refs[:-3], refs[-3:]
    copies = start_copies(place_ref, piece_refs, weight_ref, sems)
    attend = col_ref[...] == row_ref[...]
    output = run_block(feat_ref[...], near_ref[...], attend, spread_ref, weight_ref, vec_ref,
                       copies, None)
    member = attend.astype(F32)
    clip_size = jnp.sum(member, axis=1, keepdims=True)
    average = jnp.dot(member, output, precision=HIGHEST, preferred_element_type=F32) / clip_size
    center = output - average
    spread = jnp.dot(
        member, center * center, precision=HIGHEST, preferred_element_type=F32
    ) / clip_size
    target_ref[...] = center * lax.rsqrt(jnp.maximum(spread, VAR_FLOOR))


def student_kernel(place_ref, feat_ref, near_ref, col_ref, row_ref, mask_ref, weight_one_ref,
                   spread_ref, vec_ref, target_ref, normed_ref, project_ref, head_ref, *refs):
    piece_refs, refs = refs[:-14], refs[-14:]
    (left_ref, right_ref, side_ref, vector_ref, normed_grad_ref, loss_ref,
     weight_ref, chance_ref, wide_ref, triple_ref, mixed_ref, unit_ref, scale_ref,
     sems) = refs
    copies = start_copies(place_ref, piece_refs, weight_ref, sems)
    vec = lambda row: vec_ref[row : row + 1, :]
    total_sum = lambda values: jnp.sum(values, axis=0, keepdims=True)
    attend = col_ref[...] == row_ref[...]
    near = near_ref[...]
    chosen = mask_ref[...] > 0.0
    values = jnp.where(chosen, vec(9), feat_ref[...])
    keep = {
        "chances": chance_ref, "wide": wide_ref, "right": right_ref, "triple": triple_ref,
        "mixed": mixed_ref, "left": left_ref, "units": unit_ref, "scales": scale_ref,
    }
    result = run_block(values, near, attend, spread_ref, weight_ref, vec_ref, copies, keep)
    kept = lambda index: (unit_ref[index], scale_ref[index, :, :1])
    student_low = bf(result)
    scale = weight_one_ref[0:1, 0:1]
    error = jnp.where(chosen, mm(student_low, head_ref[...]) + vec(8) - target_ref[...], 0.0)
    loss_ref[...] = jnp.broadcast_to(
        jnp.sum(total_sum(error * error), axis=1, keepdims=True) * scale, loss_ref.shape
    )
    predict_grad = error * (2.0 * scale)
    vector_ref[8:9, :] = total_sum(predict_grad)
    predict_low = bf(predict_grad)
    reach_end = CH + POS_K * WIDTH

    def put_side(first, values, group=slice(0, D)):
        if len(side_ref.shape) == 2:
            side_ref[group, first : first + values.shape[1]] = values
            return
        rows, width = side_ref.shape[2:]
        owners = slice(group.start // rows, group.stop // rows)
        for n in range(side_ref.shape[1]):
            low_end = max(first, n * width)
            high_end = min(first + values.shape[1], (n + 1) * width)
            if low_end < high_end:
                part = values[:, low_end - first : high_end - first]
                side_ref[owners, n, :, low_end - n * width : high_end - n * width] = part.reshape(
                    owners.stop - owners.start, rows, high_end - low_end
                )

    put_side(reach_end, t_mm(student_low, predict_low))
    grad = mm_t(predict_low, head_ref[...])

    def norm_step(grad, index):
        back, gain, shift = norm_bwd(kept(index), vec(2 * index), grad)
        vector_ref[2 * index : 2 * index + 1, :] = gain[None]
        vector_ref[2 * index + 1 : 2 * index + 2, :] = shift[None]
        return back

    grad = norm_step(grad, 2)
    down = bf(grad)
    left_ref[3] = down
    for start in range(0, weight_ref.shape[2], D):
        cols = slice(start, start + D)
        wide_grad = bf(mm(down, weight_ref[2, :, cols]) * gelu_slope(wide_ref[:, cols]))
        right_ref[1, :, cols] = wide_grad
        grad = grad + mm_t(wide_grad, weight_ref[1, :, cols])
    grad = norm_step(grad, 1)
    down = bf(grad)
    right_ref[0, :, 3 * D :] = down
    outs_grad = mm_t(down, weight_ref[0, :, 3 * D :])
    for pair in range(HEADS // 2):
        lo = pair * 2 * HEAD_DIM
        hi = lo + 2 * HEAD_DIM
        query = triple_ref[:, lo:hi]
        key = triple_ref[:, D + lo : D + hi]
        value = triple_ref[:, 2 * D + lo : 2 * D + hi]
        sums = [None, None, None]
        for upper in range(2):
            out_low = bf(lane_half(outs_grad[:, lo:hi], upper))
            chances = chance_ref[2 * pair + upper]
            chance_grad = mm_t(out_low, value)
            score_grad = chances * (
                chance_grad - jnp.sum(chance_grad * chances, axis=-1, keepdims=True)
            )
            score_grad = bf(score_grad * (1.0 / math.sqrt(HEAD_DIM)))
            parts = (
                lane_half(mm(score_grad, key), upper),
                lane_half(t_mm(score_grad, query), upper),
                t_mm(bf(chances), out_low),
            )
            for index in range(3):
                sums[index] = parts[index] if upper == 0 else sums[index] + parts[index]
        for index in range(3):
            right_ref[0, :, index * D + lo : index * D + hi] = bf(sums[index])
    grad = grad + mm_t(right_ref[0, :, : 3 * D], weight_ref[0, :, : 3 * D])
    grad = norm_step(grad, 0)
    mixed_grad = grad * gelu_slope(mixed_ref[...])
    vector_ref[7:8, :] = total_sum(mixed_grad)
    mixed_low = bf(mixed_grad)
    grad = grad + position_sum(mixed_low.astype(F32), near, spread_ref, True)
    shifted = bf(values).astype(F32)
    half = D // 2
    for offset in range(POS_K):
        taps = taps_of(shifted, near, offset, False)
        for part in range(2):
            cols = slice(part * half, (part + 1) * half)
            full = t_mm(taps[:, cols], mixed_low[:, cols])
            pieces = [
                full[g * WIDTH : (g + 1) * WIDTH, g * WIDTH : (g + 1) * WIDTH]
                for g in range(half // WIDTH)
            ]
            put_side(CH + offset * WIDTH, jnp.concatenate(pieces, axis=0), cols)
    vector_ref[9:10, :] = total_sum(jnp.where(chosen, grad, 0.0))
    grad = jnp.where(chosen, 0.0, grad)
    vector_ref[6:7, :] = total_sum(grad)
    feat_low = bf(grad)
    put_side(0, t_mm(feat_low, normed_ref[...]))
    normed_grad_ref[...] = mm(feat_low, project_ref[...])


def spread_kernel(side_ref, tile_ref, spread_ref):
    half = D // 2
    rows = lax.broadcasted_iota(jnp.int32, (half, half), 0) // WIDTH
    cols = lax.broadcasted_iota(jnp.int32, (half, half), 1) // WIDTH
    same = rows == cols
    for offset in range(POS_K):
        piece = side_ref[:, offset * WIDTH : (offset + 1) * WIDTH]
        for part in range(2):
            wide = mm(piece[part * half : (part + 1) * half], tile_ref[...])
            spread_ref[offset, part * half : (part + 1) * half, :] = bf(
                jnp.where(same, wide, 0.0)
            )


def block_grad_kernel(place_ref, left_ref, left_two_ref, right_ref, right_two_ref,
                      send_top_ref, keep_top_ref, send_low_ref, keep_low_ref, full_ref):
    unused, line, unused_two, half, cols = keep_top_ref.shape
    x = place_ref[0]
    far = pl.program_id(1)
    full_ref[...] = t_mm(left_ref[0], right_ref[0]) + t_mm(left_two_ref[0], right_two_ref[0])
    for z in range(line):
        start = lambda index: pl.multiple_of((2 * z + index) * 2 * half, 8)
        keep_top_ref[0, z, 0] = full_ref[pl.ds(start(x), half), :]
        send_top_ref[0, z, 0] = bf(full_ref[pl.ds(start(1 - x), half), :])

    @pl.when(far == 0)
    def _():
        for z in range(line):
            for index in range(2):
                row = (2 * z + index) * 2 * half + half
                keep_low_ref[index, z, 0] = full_ref[row : row + half, :]

    @pl.when(far == 1)
    def _():
        for z in range(line):
            for index in range(2):
                row = (2 * z + index) * 2 * half + half
                send_low_ref[index, z, 0] = bf(full_ref[row : row + half, :])


def block_grads(left, left_two, right, right_two, place, n_dp, n_narrow):
    frames = left.shape[1]
    cols = right.shape[2] // n_narrow
    half = D // n_dp // 2
    line = n_dp // 2
    shape = jax.ShapeDtypeStruct

    def narrow(far, place):
        return 2 * (place[1] ^ far) + place[2]

    def left_index(matrix, far, place):
        is_out = (narrow(far, place) + 1) * cols > 3 * D
        return (jnp.where(matrix == 0, jnp.where(is_out, 1, 0), matrix + 1), 0, 0)

    left_spec = pl.BlockSpec((1, frames, D), left_index)
    right_spec = pl.BlockSpec(
        (1, frames, cols), lambda matrix, far, place: (matrix, 0, narrow(far, place))
    )
    top_spec = pl.BlockSpec(
        (1, line, 1, half, cols), lambda matrix, far, place: (place[1] ^ far, 0, matrix, 0, 0)
    )
    low_spec = pl.BlockSpec(
        (2, line, 1, half, cols), lambda matrix, far, place: (0, 0, matrix, 0, 0)
    )
    whole = (2, line, 3, half, cols)
    return pl.pallas_call(
        block_grad_kernel,
        grid_spec=pltpu.PrefetchScalarGridSpec(
            num_scalar_prefetch=1,
            grid=(3, 2),
            in_specs=[left_spec, left_spec, right_spec, right_spec],
            out_specs=[top_spec, top_spec, low_spec, low_spec],
            scratch_shapes=[pltpu.VMEM((D, cols), F32)],
        ),
        out_shape=[shape(whole, BF16), shape(whole, F32), shape(whole, BF16), shape(whole, F32)],
        name="block_grads",
    )(place, left, left_two, right, right_two)


def plain_weight_grads(left, right, n_dp, n_narrow):
    full = [
        jnp.concatenate(
            [t_mm(left[0], right[0, :, : 3 * D]), t_mm(left[1], right[0, :, 3 * D :])], axis=1
        ),
        t_mm(left[2], right[1]),
        t_mm(left[3], right[2]),
    ]
    full = jnp.stack(full, 0)
    full = full.reshape(3, n_dp, D // n_dp, n_narrow, full.shape[2] // n_narrow)
    return full.transpose(1, 3, 0, 2, 4)


def spread_kernels(side_conv):
    tile = np.zeros((WIDTH, D // 2), np.float32)
    for column in range(D // 2):
        tile[column % WIDTH, column] = 1.0
    return pl.pallas_call(
        spread_kernel,
        in_specs=[VMEM, VMEM],
        out_specs=VMEM,
        out_shape=jax.ShapeDtypeStruct((POS_K, D, D // 2), BF16),
        name="spread",
        compiler_params=pltpu.CompilerParams(vmem_limit_bytes=LIMIT),
    )(side_conv, jnp.asarray(tile, BF16))


def flat_pieces(pieces):
    if isinstance(pieces, list):
        return pieces, pieces[0].shape[-1] * 4
    return [pieces], pieces.shape[-1] * (pieces.shape[1] if pieces.ndim == 5 else 1)


def teacher_target(feats, near, col, row, spread, vec, pieces, place):
    pieces, width = flat_pieces(pieces)
    return pl.pallas_call(
        teacher_kernel,
        in_specs=[SMEM] + [VMEM] * 6 + [ANY] * len(pieces),
        out_specs=VMEM,
        out_shape=jax.ShapeDtypeStruct(feats.shape, F32),
        scratch_shapes=[pltpu.VMEM((3, D, width), BF16), pltpu.SemaphoreType.DMA((3,))],
        name="teacher",
        compiler_params=pltpu.CompilerParams(vmem_limit_bytes=LIMIT),
    )(place, feats, near, col, row, spread, vec, *pieces)


def student_step(feats, near, col, row, mask, weight, spread, vec, target, normed, project, head,
                 pieces, place, side_shape):
    pieces, width = flat_pieces(pieces)
    frames = feats.shape[0]
    shape = jax.ShapeDtypeStruct
    return pl.pallas_call(
        student_kernel,
        in_specs=[SMEM] + [VMEM] * 12 + [ANY] * len(pieces),
        out_specs=[VMEM] * 6,
        out_shape=[
            shape((4, frames, D), BF16),
            shape((3, frames, width), BF16),
            shape(side_shape, F32),
            shape((10, D), F32),
            shape((frames, CH), F32),
            shape((8, 128), F32),
        ],
        scratch_shapes=[
            pltpu.VMEM((3, D, width), BF16),
            pltpu.VMEM((HEADS, frames, frames), F32),
            pltpu.VMEM((frames, width), F32),
            pltpu.VMEM((frames, 3 * D), BF16),
            pltpu.VMEM((frames, D), F32),
            pltpu.VMEM((3, frames, D), F32),
            pltpu.VMEM((3, frames, 128), F32),
            pltpu.SemaphoreType.DMA((3,)),
        ],
        name="student",
        compiler_params=pltpu.CompilerParams(vmem_limit_bytes=LIMIT),
    )(
        place, feats, near, col, row, mask, weight, spread, vec, target, normed, project, head,
        *pieces,
    )


class Links:
    def __init__(self, n_dp, n_narrow):
        self.n_dp, self.n_narrow = n_dp, n_narrow
        self.line = n_dp // 2
        self.direct = n_narrow == 4 and n_dp % 2 == 0 and 4 * self.line == sum(KERNELS)
        dp, narrow = lax.axis_index("dp"), lax.axis_index("narrow")
        self.z, self.x, self.y, self.c = dp // 2, dp % 2, narrow // 2, narrow % 2

    def swap_c(self, values):
        return self.flip(values, "narrow", 1)

    def swap_y(self, values):
        return self.flip(values, "narrow", 2)

    def swap_x(self, values):
        return self.flip(values, "dp", 1)

    def flip(self, values, axis, bit):
        size = self.n_dp if axis == "dp" else self.n_narrow
        return lax.ppermute(values, axis, [(i, i ^ bit) for i in range(size)])

    def step_z(self, values, up, senders):
        move = 1 if up else -1
        pairs = [(2 * z + x, 2 * (z + move) + x) for z in senders for x in range(2)]
        return lax.ppermute(values, "dp", pairs)

    def total(self, values, axes=("narrow", "dp")):
        for axis in axes:
            size = self.n_dp if axis == "dp" else self.n_narrow
            if size & (size - 1):
                values = lax.psum(values, axis)
                continue
            bit = 1
            while bit < size:
                values = values + self.flip(values, axis, bit)
                bit *= 2
        return values

    def go(self, requests):
        results = []
        for request in requests:
            kind, values = request[0], request[1]
            if kind == "c":
                results.append(self.flip(values, "narrow", 1))
            elif kind == "y":
                results.append(self.flip(values, "narrow", 2))
            elif kind == "x":
                results.append(self.flip(values, "dp", 1))
            else:
                results.append(self.step_z(values, kind == "up", request[2]))
        return results

    def gather_steps(self, values):
        last = self.line - 1
        ups, downs = [], []
        up = down = values
        for hop in range(1, self.line):
            up, down = yield [
                ("up", up, range(hop - 1, last)),
                ("down", down, range(1, self.line - hop + 1)),
            ]
            ups.append(up)
            downs.append(down)
        stacked = jnp.stack(ups[::-1] + [values] + downs, 0)
        column = lax.dynamic_slice_in_dim(stacked, last - self.z, self.line, 0)
        lanes = values.shape[-1] // 2
        one, two = column[..., :lanes], column[..., lanes:]
        one_y, two_x, one_x, two_y, column_c = yield [
            ("y", one), ("x", two), ("x", one), ("y", two), ("c", column)
        ]
        next_c = jnp.stack([one_y, two_x, one_x, two_y], 0)
        one_xy, two_xy, next_c = yield [("x", one_y), ("y", two_x), ("c", next_c)]
        (far_c,) = yield [("c", jnp.stack([one_xy, two_xy], 0))]
        return [column, one_y, two_x, one_x, two_y, one_xy, two_xy, column_c, next_c, far_c]

    def gather_whole(self, values):
        if not self.direct:
            whole = lax.all_gather(values, "narrow", axis=2, tiled=True)
            return lax.all_gather(whole, "dp", axis=1, tiled=True)
        whole = lax.all_gather(values, ("dp", "narrow"), axis=0)
        return whole.reshape((self.n_dp, self.n_narrow) + values.shape)

    def scatter_steps(self, parts):
        send, keep = parts
        half = send.shape[-2] // 2
        pick = lambda array, axis, index: lax.dynamic_index_in_dim(array, index, axis, False)
        (got,) = yield [("c", send)]

        def both(rows, axis, index):
            return pick(keep[..., rows, :], axis, index) + pick(got[..., rows, :], axis, index)

        top, low_rows = slice(0, half), slice(half, None)
        ends = yield [
            ("x", both(top, 0, 1 - self.x)), ("y", both(low_rows, 1, 1 - self.y))
        ]

        def all_three(rows, first, at_first, second, at_second, end):
            mine = [
                pick(pick(array[..., rows, :], first, at_first), second, at_second)
                for array in (keep, got)
            ]
            return mine[0] + mine[1] + pick(end, second, at_second)

        top_of = lambda index: all_three(top, 0, self.x, 0, index, ends[0])
        low_of = lambda index: all_three(low_rows, 1, self.y, 0, index, ends[1])
        more = yield [("y", top_of(1 - self.y)), ("x", low_of(1 - self.x))]
        one = top_of(self.y) + more[0]
        two = low_of(self.x) + more[1]
        return (yield from self.line_steps(jnp.concatenate([one, two], axis=-2)))

    def half_steps(self, send_top, keep_top, send_low, keep_low):
        pick = lambda array, index: lax.dynamic_index_in_dim(array, index, 0, False)
        top, lower = yield [("x", send_top), ("y", send_low)]
        top_of = lambda index: pick(keep_top, index) + pick(top, index).astype(F32)
        low_of = lambda index: pick(keep_low, index) + pick(lower, index).astype(F32)
        more = yield [("y", top_of(1 - self.y)), ("x", low_of(1 - self.x))]
        one, two = top_of(self.y) + more[0], low_of(self.x) + more[1]
        return (yield from self.line_steps(jnp.concatenate([one, two], axis=-2)))

    def line_steps(self, column):
        pick = lambda array, axis, index: lax.dynamic_index_in_dim(array, index, axis, False)
        last = self.line - 1
        at = lambda offset: pick(column, 0, (self.z + offset) % self.line)
        up = down = None
        for hop in range(last, 0, -1):
            send_up = at(hop) if up is None else at(hop) + up
            send_down = at(-hop) if down is None else at(-hop) + down
            up, down = yield [
                ("up", send_up, range(0, last - hop + 1)),
                ("down", send_down, range(hop, self.line)),
            ]
        own = at(0)
        return own if up is None else own + up + down


class Stages:
    def __init__(self, links, steps):
        self.links, self.steps = links, list(steps)
        self.requests = [next(one) for one in self.steps]
        self.results = [None] * len(self.steps)

    def tie(self, *others):
        arrays = [[request[1] for request in one] for one in self.requests]
        arrays, others = lax.optimization_barrier((arrays, others))
        self.requests = [
            [(request[0], array) + tuple(request[2:]) for request, array in zip(one, part)]
            for one, part in zip(self.requests, arrays)
        ]
        return others if len(others) != 1 else others[0]

    def add(self, one):
        self.steps.append(one)
        self.requests.append(next(one))
        self.results.append(None)

    def advance(self, after=()):
        got = [self.links.go(one) for one in self.requests]
        if after:
            got, after = lax.optimization_barrier((got, tuple(after)))
        for index, one in enumerate(self.steps):
            if not self.requests[index]:
                continue
            try:
                self.requests[index] = one.send(got[index])
            except StopIteration as stop:
                self.requests[index] = []
                self.results[index] = stop.value
        return after if len(after) != 1 else after[0]

    def finish(self):
        while any(self.requests):
            self.advance()
        return self.results


def adamw(weight, grad, first, second, power):
    first = DECAY * first + (1.0 - DECAY) * grad
    second = DECAY * second + (1.0 - DECAY) * grad * grad
    unbias = 1.0 - power
    step_size = first / unbias / (jnp.sqrt(second / unbias) + 1e-08)
    return (weight - LR_ADAM * (step_size + WEIGHT_DECAY * weight), first, second)


def exact(left, right):
    return jnp.einsum("brs,bst->brt", left, right, precision=HIGHEST)


def orthogonal(blocks, gram_total):
    gram = gram_total(jnp.einsum("brc,bsc->brs", blocks, blocks, precision=HIGHEST))
    scales = 1.0 / (jnp.sqrt(jnp.trace(gram, axis1=1, axis2=2)) + 1e-07)
    gram = gram * (scales * scales)[:, None, None]
    eye = jnp.eye(gram.shape[1], dtype=F32)[None]
    whole = None
    for iteration in range(5):
        square = exact(gram, gram)
        step = COEFF_A * eye + COEFF_B * gram + COEFF_C * square
        whole = step if whole is None else exact(step, whole)
        if iteration < 4:
            gram = exact(exact(step, gram), step)
            gram = 0.5 * (gram + gram.transpose(0, 2, 1))
    return exact(whole * scales[:, None, None], blocks)


def per_device(
    wave,
    clip_ids,
    span_starts,
    step_count,
    conv_small,
    conv_stack,
    side,
    vectors,
    block,
    teacher_block,
    teacher_vectors,
    small_mean,
    small_square,
    stack_mean,
    stack_square,
    side_mean,
    side_square,
    vector_mean,
    vector_square,
    block_momentum,
    n_dp,
    n_narrow,
):
    everyone = ("dp", "narrow")
    frames = clip_ids.shape[0]
    rows_here, cols_here = block.shape[1:]
    side_rows, side_cols = side.shape
    links = Links(n_dp, n_narrow)
    place = jnp.stack([links.x, links.y, links.c]).astype(jnp.int32)
    stack_rows_here = conv_stack.shape[0]
    side_size = side_rows * side_cols
    side_lines = -(-side_size // CH)
    lines = -(-(stack_rows_here + side_lines) // 16) * 16
    side_flat = jnp.pad(bf(side).reshape(-1), (0, side_lines * CH - side_size))
    send = jnp.concatenate(
        [
            bf(conv_stack),
            side_flat.reshape(side_lines, CH),
            jnp.zeros((lines - stack_rows_here - side_lines, CH), BF16),
        ],
        axis=0,
    )
    stack = lax.all_gather(send, everyone, axis=0)
    teacher_pieces = links.gather_whole(bf(teacher_block))
    masked = masked_of(span_starts)
    masked_here = jnp.full((1, 128), jnp.sum(masked.astype(F32)), F32)
    masked_all = links.total(masked_here)
    small_low = low(conv_small)
    vector_low = low(vectors)
    taps = first_taps(wave, frames)
    first_weights, hidden, hidden_tail = first_layer(small_low, taps, frames)
    whole_side = stack[:, stack_rows_here : stack_rows_here + side_lines].reshape(
        n_dp * n_narrow, side_lines * CH
    )[:, :side_size]
    whole_side = (
        whole_side.reshape(n_dp, n_narrow, side_rows, side_cols)
        .transpose(0, 2, 1, 3)
        .reshape(n_dp * side_rows, n_narrow * side_cols)
    )
    spread_of = lambda: spread_kernels(whole_side[:, CH : CH + POS_K * WIDTH])
    if links.direct:
        exchange = Stages(links, [links.gather_steps(bf(block))])
        hidden = exchange.advance((hidden,))
        for unused in range(links.line - 2):
            exchange.advance()
        hidden = exchange.tie(hidden)
        hidden, masked_all = lax.optimization_barrier((hidden, masked_all))
        outs = encode_fwd(small_low, stack, hidden, hidden_tail, frames)
        outs = list(outs)
        outs[13] = exchange.advance((outs[13],))
        whole_side = exchange.tie(whole_side)
        spread = spread_of()
    else:
        student_pieces = links.gather_whole(bf(block))
        outs = encode_fwd(small_low, stack, hidden, hidden_tail, frames)
        spread = spread_of()
    normed = outs[13]
    project = whole_side[:, :CH]
    head = whole_side[:, CH + POS_K * WIDTH :]
    near = jnp.pad(neighbours(clip_ids).astype(F32).T, ((0, 0), (0, 32 - POS_K)))
    col, row = clip_ids[:, None], clip_ids[None, :]
    feats = mm_t(normed, project) + vector_low[6]
    target = teacher_target(
        feats, near, col, row, spread, low(teacher_vectors), teacher_pieces, place
    )
    if links.direct:
        target = exchange.advance((target,))
        (student_pieces,) = exchange.finish()
    total = jnp.maximum(masked_all[0, 0], 1.0)
    weight = jnp.full((8, 128), 1.0 / (total * math.sqrt(D)), F32)
    left, right, side_grad, vector_grad, normed_grad, loss_tile = student_step(
        feats,
        near,
        col,
        row,
        masked.astype(F32)[:, None],
        weight,
        spread,
        vector_low,
        target,
        normed,
        project,
        head,
        student_pieces,
        place,
        (n_dp, n_narrow, side_rows, side_cols)
        if links.direct
        else (n_dp * side_rows, n_narrow * side_cols),
    )
    loss_part = loss_tile[0, 0]
    devices = n_dp * n_narrow
    if links.direct:
        core = links.c.astype(jnp.int32).reshape(1)
        order = [tap // 2 % 2 * 8 + tap % 2 * 4 + tap // 4 for tap in range(sum(KERNELS))]
        others = [links.swap_c(left), links.swap_c(right)]
        side_piece = lax.psum_scatter(
            side_grad.reshape(devices * side_rows, side_cols),
            everyone,
            scatter_dimension=0,
            tiled=True,
        )
        grads = block_grads(left, others[0], right, others[1], place, n_dp, n_narrow)
        feed = Stages(links, [links.half_steps(*grads)])
        normed_grad = feed.tie(normed_grad)
        *parts, second, second_tail, norm_grad = encode_back(
            order, core, outs, small_low, stack, frames, normed_grad
        )
        parts = second_dw(order, core, second, second_tail, hidden, hidden_tail, parts)
        parts = feed.advance(tuple(parts))
        second = feed.tie(second)
        shape = (2, 2, links.line) + conv_stack.shape
        last = Stages(links, [links.scatter_steps([part.reshape(shape) for part in parts])])
        second = last.tie(second)
        second = last.advance((second,))
        second = last.tie(second)
        second = feed.advance((second,))
        second = feed.tie(second)
        tap_grad = second_dx(second, second_tail, stack, taps, first_weights, frames)
        for one in (feed, last, feed, last):
            tap_grad = one.advance((tap_grad,))
            tap_grad = one.tie(tap_grad)
        (block_piece,) = feed.finish()
        (stack_piece,) = last.finish()
    else:
        sums = lambda values: lax.psum_scatter(
            values.reshape((-1,) + values.shape[-1:]), everyone, scatter_dimension=0, tiled=True
        )
        block_piece = sums(plain_weight_grads(left, right, n_dp, n_narrow))
        block_piece = block_piece.reshape(3, rows_here, cols_here)
        side_grad = side_grad.reshape(n_dp, side_rows, n_narrow, side_cols)
        side_piece = sums(side_grad.transpose(0, 2, 1, 3))
        core = jnp.zeros((1,), jnp.int32)
        order = list(range(sum(KERNELS)))
        *parts, second, second_tail, norm_grad = encode_back(
            order, core, outs, small_low, stack, frames, normed_grad
        )
        parts = second_dw(order, core, second, second_tail, hidden, hidden_tail, parts)
        tap_grad = second_dx(second, second_tail, stack, taps, first_weights, frames)
        stack_piece = sums(jnp.stack([parts[1], parts[0]], 1).reshape(sum(KERNELS) * CH, CH))
    small_grad = jnp.concatenate([tap_grad[:10], norm_grad], axis=0)
    packed = jnp.concatenate(
        [
            vector_grad,
            small_grad.reshape(-1, D),
            jnp.full((1, D), loss_part, F32),
        ],
        axis=0,
    )
    packed = links.total(packed)
    vector_total = packed[:10]
    small_total = packed[10:-1].reshape(small_grad.shape)
    loss_value = packed[-1, 0]
    shard_squares = (
        jnp.sum(block_piece * block_piece)
        + jnp.sum(side_piece * side_piece)
        + jnp.sum(stack_piece * stack_piece)
    )
    grad_norm = jnp.sqrt(
        links.total(jnp.full((1, 128), shard_squares, F32))[0, 0]
        + jnp.sum(small_total * small_total)
        + jnp.sum(vector_total * vector_total)
    )
    factor = jnp.minimum(1.0, CLIP_LIMIT / (grad_norm + 1e-06))
    power = jnp.power(DECAY, step_count[0].astype(F32))
    small_next = adamw(conv_small, factor * small_total, small_mean, small_square, power)
    stack_next = adamw(conv_stack, factor * stack_piece, stack_mean, stack_square, power)
    side_next = adamw(side, factor * side_piece, side_mean, side_square, power)
    vector_next = adamw(vectors, factor * vector_total, vector_mean, vector_square, power)
    momentum = DECAY * block_momentum + factor * block_piece
    ortho = orthogonal(momentum, lambda gram: links.total(gram, ("narrow",)))
    block_next = block * (1.0 - LR_MUON * WEIGHT_DECAY) - LR_MUON * ortho
    teacher_next = EMA_RATE * teacher_block + (1.0 - EMA_RATE) * block_next
    teacher_vec_next = EMA_RATE * teacher_vectors + (1.0 - EMA_RATE) * vector_next[0]
    return (
        (loss_value, grad_norm)
        + small_next
        + stack_next
        + side_next
        + vector_next
        + (block_next, momentum, teacher_next, teacher_vec_next, bf(block_next))
    )


def solution(mesh):
    n_dp, n_narrow = mesh.shape["dp"], mesh.shape["narrow"]

    def step(*arguments):
        return per_device(*arguments, n_dp, n_narrow)

    rows = P(("dp", "narrow"), None)
    flat = P(("dp", "narrow"))
    grid = P("dp", "narrow")
    cube = P(None, "dp", "narrow")
    one = P()
    in_specs = (
        (flat, flat, flat, one, one, rows, grid, one, cube, cube, one, one, one)
        + (rows, rows, grid, grid, one, one, cube)
    )
    out_specs = (
        (one, one, one, one, one, rows, rows, rows, grid, grid, grid, one, one, one)
        + (cube, cube, cube, one, cube)
    )
    return jax.shard_map(
        step, mesh=mesh, in_specs=in_specs, out_specs=out_specs, check_vma=False
    )
```

```python
import math

import jax
import jax.numpy as jnp
import numpy as np
from jax import lax
from jax.experimental import pallas as pl
from jax.experimental.pallas import tpu as pltpu
from jax.sharding import Mesh
from jax.sharding import PartitionSpec as P

D = 768
HEADS = 12
HEAD_DIM = 64
CH = 512
GROUPS = 16
WIDTH = D // GROUPS
POS_K = 19
REACH = POS_K // 2
SPAN = 10
TAIL = 16

EPS = 1e-05
VAR_FLOOR = 0.1
CLIP_LIMIT = 0.01
LR_ADAM = 0.03
LR_MUON = 2.0
DECAY = 0.5
WEIGHT_DECAY = 0.01
EMA_RATE = 0.5
KERNELS = (3, 3, 3, 3, 2, 2)
COEFF_A = 3.4445
COEFF_B = -4.775
COEFF_C = 2.0315
HIGHEST = lax.Precision.HIGHEST
F32 = jnp.float32
BF16 = jnp.bfloat16
LIMIT = 60 * 1024 * 1024
ROOT_HALF = math.sqrt(0.5)
ROOT_TAU = 1.0 / math.sqrt(2.0 * math.pi)


VMEM = pl.BlockSpec(memory_space=pltpu.VMEM)
ANY = pl.BlockSpec(memory_space=pl.ANY)
SMEM = pl.BlockSpec(memory_space=pltpu.SMEM)


def bf(values):
    return values.astype(BF16)


def low(values):
    return lax.optimization_barrier(values.astype(BF16)).astype(F32)


def dot(left, right, contract, batch=((), ())):
    return lax.dot_general(left, right, (contract, batch), preferred_element_type=F32)


def mm(left, right):
    return dot(left, right, ((1,), (0,)))


def mm_t(left, right):
    return dot(left, right, ((1,), (1,)))


def t_mm(left, right):
    return dot(left, right, ((0,), (0,)))


def gelu(values):
    return 0.5 * values * (1.0 + lax.erf(values * ROOT_HALF))


def gelu_slope(values):
    return 0.5 * (1.0 + lax.erf(values * ROOT_HALF)) + values * (
        ROOT_TAU * jnp.exp(-0.5 * values * values)
    )


def gelu_both(values):
    chance = 0.5 * (1.0 + lax.erf(values * ROOT_HALF))
    return values * chance, chance + values * (ROOT_TAU * jnp.exp(-0.5 * values * values))


def norm_fwd(values, gain, shift):
    center = values - jnp.mean(values, axis=-1, keepdims=True)
    scale = lax.rsqrt(jnp.mean(center * center, axis=-1, keepdims=True) + EPS)
    unit = center * scale
    return unit * gain + shift, (unit, scale)


def norm_bwd(kept, gain, grad):
    unit, scale = kept
    inner = grad * gain
    back = scale * (
        inner
        - jnp.mean(inner, axis=-1, keepdims=True)
        - unit * jnp.mean(inner * unit, axis=-1, keepdims=True)
    )
    return back, jnp.sum(grad * unit, axis=0), jnp.sum(grad, axis=0)


def first_taps(wave, frames):
    padded = jnp.pad(bf(wave), (0, 320 * (frames + 2) - wave.shape[0])).reshape(frames + 2, 320)
    rows = jnp.concatenate([padded[: frames + 1], padded[1:, :16]], axis=1)
    pick = np.zeros((336, 65 * 16), np.float32)
    for phase in range(64):
        for tap in range(10):
            pick[5 * phase + tap, 16 * phase + tap] = 1.0
    taps = bf(mm(rows, jnp.asarray(pick[:, : 64 * 16], BF16)))
    taps = taps.reshape(frames + 1, 64, 16).transpose(1, 0, 2)
    main = jnp.concatenate(
        [taps[:, :frames], taps[:1, 1:], jnp.zeros((1, frames, 16), BF16)], axis=0
    )
    return main, taps[:TAIL, frames]


def chooser(delta, rows_last=True):
    rows = lax.broadcasted_iota(jnp.int32, (TAIL, TAIL), 0)
    cols = lax.broadcasted_iota(jnp.int32, (TAIL, TAIL), 1)
    hit = cols == 2 * rows + delta if rows_last else rows == 2 * cols + delta
    return jnp.where(hit, 1.0, 0.0)


def stack_rows(ref, tap, taps=sum(KERNELS)):
    count = ref.shape[0] // taps
    rows = CH // count
    return ref[tap * count : (tap + 1) * count, :rows, :].reshape(CH, CH)


def first_kernel(taps_ref, weight_ref, out_ref):
    frames = taps_ref.shape[1]
    rows = taps_ref[...].reshape(2 * frames, taps_ref.shape[2])
    out_ref[...] = bf(gelu(mm(rows, weight_ref[...]))).reshape(out_ref.shape)


def encode_kernel(hidden_ref, tail_ref, stack_ref, small_ref, *refs):
    value_refs, hidden_refs = refs[:6], (hidden_ref,) + refs[6:11]
    value_tail_ref, hidden_tail_ref, normed_ref, unit_ref, scale_ref = refs[11:]
    frames = hidden_ref.shape[2]
    offset = 0
    tail = tail_ref[...]
    for layer, kernel in enumerate(KERNELS):
        source, values = hidden_refs[layer], value_refs[layer]
        count = values.shape[0]
        size = min(4, count)
        target = hidden_refs[layer + 1] if layer < 5 else None

        def product(index, offset=offset, kernel=kernel, source=source, size=size):
            total = None
            for tap in range(kernel):
                piece = source[pl.ds(index * size + tap // 2, size), tap % 2]
                part = mm(
                    piece.reshape(size * frames, CH),
                    stack_rows(stack_ref, offset // CH + tap),
                )
                total = part if total is None else total + part
            return total

        def step(index, carry, values=values, target=target, size=size, product=product):
            total = product(index)
            active, slope = gelu_both(total)
            values[pl.ds(index * size, size)] = slope.reshape(size, frames, CH)
            target[pl.ds(index * (size // 2), size // 2)] = bf(active).reshape(
                size // 2, 2, frames, CH
            )
            return carry

        if layer < 5:
            if count == size:
                step(0, 0)
            else:
                lax.fori_loop(0, count // size, step, 0)
        else:
            total = product(0)
            encoded, slope = gelu_both(total)
            values[...] = slope.reshape(values.shape)
            normed, kept = norm_fwd(encoded, small_ref[10:11, :], small_ref[11:12, :])
            normed_ref[...] = bf(normed)
            unit_ref[...] = kept[0]
            scale_ref[...] = jnp.broadcast_to(kept[1], scale_ref.shape)
        if layer < 3:
            total = None
            for tap in range(kernel):
                part = mm(
                    bf(mm(bf(chooser(tap)), tail)),
                    stack_rows(stack_ref, offset // CH + tap),
                )
                total = part if total is None else total + part
            active, slope = gelu_both(total)
            value_tail_ref[layer] = slope
            tail = bf(active)
            hidden_tail_ref[layer] = tail
            head = target[0, 0].astype(F32)
            rows = lax.broadcasted_iota(jnp.int32, (frames, CH), 0)
            moved = jnp.where(
                rows == frames - 1, active[0:1].astype(BF16).astype(F32),
                pltpu.roll(head, frames - 1, 0),
            )
            target[count // 2, 0] = bf(moved)
            target[count // 2, 1] = jnp.zeros((frames, CH), BF16)
        offset += kernel * CH


def layer_dw(grad_ref, source_ref, tail_grad, source_tail, kernel, out_ref):
    count, frames = grad_ref.shape[:2]
    size = min(8, count)
    for tap in range(kernel):
        rows = slice(tap * CH, (tap + 1) * CH)
        if tail_grad is None:
            out_ref[rows, :] = jnp.zeros((CH, CH), F32)
        else:
            out_ref[rows, :] = t_mm(bf(mm(bf(chooser(tap)), source_tail)), tail_grad)

        def step(index, carry, tap=tap, rows=rows):
            piece = source_ref[pl.ds(index * size + tap // 2, size), tap % 2]
            grad = grad_ref[pl.ds(index * size, size)]
            out_ref[rows, :] += t_mm(
                piece.reshape(size * frames, CH), grad.reshape(size * frames, CH)
            )
            return carry

        if count == size:
            step(0, 0)
        else:
            lax.fori_loop(0, count // size, step, 0)


def layer_dx(grad_ref, tail_grad, kernel, weight_of, slope, write, carry_ref, head_ref):
    count, frames = grad_ref.shape[:2]
    size = min(4, count)
    carry_ref[...] = jnp.zeros((frames, CH), F32)

    def step(index, unused):
        grad = grad_ref[pl.ds(index * size, size)].reshape(size * frames, CH)
        even = mm_t(grad, weight_of(0)).reshape(size, frames, CH)
        odd = mm_t(grad, weight_of(1)).reshape(size, frames, CH)
        if kernel == 3:
            late = mm_t(grad, weight_of(2)).reshape(size, frames, CH)
            before = carry_ref[...][None]
            if size > 1:
                before = jnp.concatenate([before, late[:-1]], axis=0)
            even = even + before
            carry_ref[...] = late[-1]
        write(index, size, even, odd)
        return unused

    if count == size:
        step(0, 0)
    else:
        lax.fori_loop(0, count // size, step, 0)
    if kernel != 3:
        return None
    wrap = carry_ref[...]
    rows = lax.broadcasted_iota(jnp.int32, (frames, CH), 0)
    head_ref[...] = jnp.where(rows == 0, 0.0, pltpu.roll(wrap, 1, 0))
    first = lax.broadcasted_iota(jnp.int32, (TAIL, CH), 0) == 0
    back = jnp.where(first, wrap[frames - 1 : frames, :], 0.0)
    if tail_grad is not None:
        for tap in range(3):
            back = back + jnp.dot(
                chooser(tap, False), mm_t(tail_grad, weight_of(tap)),
                precision=HIGHEST, preferred_element_type=F32,
            )
    return back


def copy_halves(order, core_ref, held, send_ref, keep_ref, first, taps, sem):
    half = CH // 2
    core = core_ref[0]
    copies = []
    for tap in range(taps):
        for target, index in ((send_ref, 1 - core), (keep_ref, core)):
            start = pl.multiple_of(tap * CH + index * half, half)
            place = order[first + tap]
            copies.append(
                pltpu.make_async_copy(held.at[pl.ds(start, half)], target.at[place], sem)
            )
            copies[-1].start()
    return copies


def encode_back_kernel(order, core_ref, grad_ref, unit_ref, scale_ref, small_ref, stack_ref, *refs):
    value_sources, hidden_sources = refs[:6], refs[6:11]
    value_tail_ref, hidden_tail_ref = refs[11:13]
    send_ref, keep_ref, second_ref, second_tail_ref, norm_ref = refs[13:18]
    grad_refs = (second_ref,) + refs[18:23]
    buffer_ref, carry_ref, head_ref, even_ref, sems = refs[23:28]
    value_refs = refs[28:33] + (value_sources[5],)
    hidden_refs, stack_copy, in_sems = refs[33:38], refs[38], refs[39]
    each = stack_ref.shape[0] // sum(KERNELS)
    fetches = [None] * 6
    first_tap = sum(KERNELS)
    for layer in range(5, 0, -1):
        first_tap -= KERNELS[layer]
        owners = slice(first_tap * each, (first_tap + KERNELS[layer]) * each)
        fetches[layer] = [
            pltpu.make_async_copy(source, target, in_sems.at[layer - 1])
            for source, target in (
                (stack_ref.at[owners, : CH // each], stack_copy.at[owners]),
                (hidden_sources[layer - 1], hidden_refs[layer - 1]),
                (value_sources[layer - 1], value_refs[layer - 1]),
            )
        ]
        for fetch in fetches[layer]:
            fetch.start()
    frames = grad_ref.shape[0]
    grad, gain, shift = norm_bwd(
        (unit_ref[...], scale_ref[:, :1]), small_ref[10:11, :], grad_ref[...]
    )
    norm_ref[0:1, :] = gain[None]
    norm_ref[1:2, :] = shift[None]
    grad_refs[5][0] = bf(grad * value_refs[5][0])
    tail_grad = None
    offset = sum(KERNELS) * CH
    copies = [[], []]
    for layer in range(5, 0, -1):
        kernel = KERNELS[layer]
        offset -= kernel * CH
        slot = layer % 2
        for copy in fetches[layer] + copies[slot]:
            copy.wait()
        held = buffer_ref.at[slot, 0 : kernel * CH]
        tail_source = None if tail_grad is None else hidden_tail_ref[layer - 1]
        layer_dw(grad_refs[layer], hidden_refs[layer - 1], tail_grad, tail_source, kernel, held)
        copies[slot] = copy_halves(
            order, core_ref, held, send_ref, keep_ref, offset // CH, kernel, sems.at[slot]
        )
        values, target = value_refs[layer - 1], grad_refs[layer - 1]

        def weight_of(tap, offset=offset):
            return stack_rows(stack_copy, offset // CH + tap)

        def write(index, size, even, odd, values=values, target=target, kernel=kernel):
            if kernel == 3:
                if not isinstance(index, int):
                    @pl.when(index == 0)
                    def _():
                        even_ref[...] = even[0]
                else:
                    even_ref[...] = even[0]
            for item in range(size):
                place = 2 * (index * size + item)
                target[place] = bf(even[item] * values[place])
                target[place + 1] = bf(odd[item] * values[place + 1])

        back = layer_dx(grad_refs[layer], tail_grad, kernel, weight_of, None, write,
                        carry_ref, head_ref)
        tail_grad = None
        if kernel == 3:
            target[0] = bf((even_ref[...] + head_ref[...]) * values[0])
            tail_grad = bf(back * value_tail_ref[layer - 1])
    second_tail_ref[...] = tail_grad
    for copy in copies[0] + copies[1]:
        copy.wait()


def second_dw_kernel(order, core_ref, grad_ref, tail_grad_ref, hidden_ref, tail_ref, old_send_ref,
                     old_keep_ref, send_ref, keep_ref, buffer_ref, sem):
    layer_dw(grad_ref, hidden_ref, tail_grad_ref[...], tail_ref[...], 3, buffer_ref)
    for copy in copy_halves(
        order, core_ref, buffer_ref, send_ref, keep_ref, 0, 3, sem
    ):
        copy.wait()


def second_dx_kernel(grad_ref, tail_grad_ref, weight_ref, taps_ref, tail_taps_ref, first_ref,
                     out_ref, carry_ref, head_ref, even_ref):
    frames = grad_ref.shape[1]
    weights = first_ref[...]
    out_ref[...] = jnp.zeros(out_ref.shape, F32)

    def piece(place, grad):
        rows = taps_ref[place]
        low_grad = bf(grad * gelu_slope(mm(rows, weights)))
        return t_mm(rows, low_grad)

    def write(index, size, even, odd):
        @pl.when(index == 0)
        def _():
            even_ref[...] = even[0]

        for item in range(size):
            place = 2 * (index * size + item)
            grad = even[item]
            if item == 0:
                grad = jnp.where(index == 0, 0.0, grad)
            out_ref[...] += piece(place, grad) + piece(place + 1, odd[item])

    def weight_of(tap):
        return stack_rows(weight_ref, tap, 3)

    back = layer_dx(grad_ref, tail_grad_ref[...], 3, weight_of, None, write, carry_ref, head_ref)
    out_ref[...] += piece(0, even_ref[...] + head_ref[...])
    rows = tail_taps_ref[...]
    out_ref[...] += t_mm(rows, bf(back * gelu_slope(mm(rows, weights))))


COUNTS = (32, 16, 8, 4, 2, 1)


def kernel_params():
    return pltpu.CompilerParams(vmem_limit_bytes=LIMIT)


def first_layer(small, taps, frames):
    main, tail = taps
    weights = jnp.pad(bf(small[:10]), ((0, 6), (0, 0)))
    hidden = pl.pallas_call(
        first_kernel,
        grid=(33,),
        in_specs=[
            pl.BlockSpec((2, frames, 16), lambda i: (i, 0, 0)),
            pl.BlockSpec((16, CH), lambda i: (0, 0)),
        ],
        out_specs=pl.BlockSpec((1, 2, frames, CH), lambda i: (i, 0, 0, 0)),
        out_shape=jax.ShapeDtypeStruct((33, 2, frames, CH), BF16),
        name="first_layer",
    )(main, weights)
    return weights, hidden, bf(gelu(mm(tail, weights)))


def encode_fwd(small, stack, hidden, hidden_tail, frames):
    shape = jax.ShapeDtypeStruct
    return pl.pallas_call(
        encode_kernel,
        in_specs=[VMEM] * 4,
        out_specs=[VMEM] * 16,
        out_shape=[shape((count, frames, CH), F32) for count in COUNTS]
        + [shape((count // 2 + 1, 2, frames, CH), BF16) for count in COUNTS[:5]]
        + [
            shape((3, TAIL, CH), F32),
            shape((3, TAIL, CH), BF16),
            shape((frames, CH), BF16),
            shape((frames, CH), F32),
            shape((frames, 128), F32),
        ],
        name="encode",
        compiler_params=kernel_params(),
    )(hidden, hidden_tail, stack, small)


def encode_back(order, core, outs, small, stack, frames, grad):
    shape = jax.ShapeDtypeStruct
    plane = pltpu.VMEM((frames, CH), F32)
    part = shape((sum(KERNELS), CH // 2, CH), F32)
    return pl.pallas_call(
        lambda *refs: encode_back_kernel(order, *refs),
        in_specs=[SMEM] + [VMEM] * 4 + [ANY] * 6 + [VMEM] + [ANY] * 5 + [VMEM] * 2,
        out_specs=[ANY, ANY, VMEM, VMEM, VMEM],
        out_shape=[
            part,
            part,
            shape((COUNTS[0], frames, CH), BF16),
            shape((TAIL, CH), BF16),
            shape((2, CH), F32),
        ],
        scratch_shapes=[pltpu.VMEM((count, frames, CH), BF16) for count in COUNTS[1:]]
        + [
            pltpu.VMEM((2, 3 * CH, CH), F32),
            plane,
            plane,
            plane,
            pltpu.SemaphoreType.DMA((2,)),
        ]
        + [pltpu.VMEM(array.shape, array.dtype) for array in outs[:5] + outs[6:11]]
        + [
            pltpu.VMEM(
                (stack.shape[0], sum(KERNELS) * CH // stack.shape[0], CH), BF16
            ),
            pltpu.SemaphoreType.DMA((5,)),
        ],
        name="encode_back",
        compiler_params=kernel_params(),
    )(core, grad, outs[14], outs[15], small, stack, *outs[:13])


def second_dw(order, core, second, second_tail, hidden, hidden_tail, parts):
    return pl.pallas_call(
        lambda *refs: second_dw_kernel(order, *refs),
        in_specs=[SMEM] + [VMEM] * 4 + [ANY, ANY],
        out_specs=[ANY, ANY],
        out_shape=[jax.ShapeDtypeStruct(part.shape, F32) for part in parts],
        scratch_shapes=[pltpu.VMEM((3 * CH, CH), F32), pltpu.SemaphoreType.DMA],
        input_output_aliases={5: 0, 6: 1},
        name="second_dw",
        compiler_params=kernel_params(),
    )(core, second, second_tail, hidden, hidden_tail, *parts)


def second_dx(second, second_tail, stack, taps, weights, frames):
    main, tail = taps
    plane = pltpu.VMEM((frames, CH), F32)
    parts = 3 * stack.shape[0] // sum(KERNELS)
    return pl.pallas_call(
        second_dx_kernel,
        grid=(1,),
        in_specs=[
            VMEM,
            VMEM,
            pl.BlockSpec((parts,) + stack.shape[1:], lambda i: (0, 0, 0)),
            VMEM,
            VMEM,
            VMEM,
        ],
        out_specs=VMEM,
        out_shape=jax.ShapeDtypeStruct((16, CH), F32),
        scratch_shapes=[plane, plane, plane],
        name="second_dx",
        compiler_params=kernel_params(),
    )(second, second_tail, stack, main, tail, weights)


def neighbours(segment):
    frames = segment.shape[0]
    padded = jnp.pad(segment, (REACH, REACH), constant_values=-1)
    return jnp.stack([padded[offset : offset + frames] == segment for offset in range(POS_K)], 0)


def masked_of(starts):
    frames = starts.shape[0]
    padded = jnp.pad(starts, (SPAN - 1, 0))
    return (
        jnp.max(jnp.stack([padded[offset : offset + frames] for offset in range(SPAN)], 0), axis=0)
        > 0
    )


def taps_of(values, near, offset, flip):
    frames = values.shape[0]
    lane = 2 * REACH - offset if flip else offset
    shift = (REACH - lane) % frames
    rolled = values if shift == 0 else pltpu.roll(values, shift, 0)
    return bf(jnp.where(near[:, lane : lane + 1] > 0.0, rolled, 0.0))


def position_sum(values, near, spread_ref, back):
    half = D // 2
    sums = [None, None]
    for offset in range(POS_K):
        taps = taps_of(values, near, offset, back)
        for side in range(2):
            weight = spread_ref[offset, side * half : (side + 1) * half, :]
            piece = taps[:, side * half : (side + 1) * half]
            part = mm_t(piece, weight) if back else mm(piece, weight)
            sums[side] = part if sums[side] is None else sums[side] + part
    return jnp.concatenate(sums, axis=1)


def lane_half(values, upper):
    lanes = lax.broadcasted_iota(jnp.int32, values.shape, 1)
    keep = lanes >= HEAD_DIM if upper else lanes < HEAD_DIM
    return jnp.where(keep, values, 0.0)


def start_copies(place_ref, piece_refs, weight_ref, sems):
    if len(piece_refs) == 1 and len(piece_refs[0].shape) == 5:
        n_dp, n_narrow, unused, rows, cols = piece_refs[0].shape
        copies = []
        for matrix in range(3):
            for d in range(n_dp):
                for n in range(n_narrow):
                    copy = pltpu.make_async_copy(
                        piece_refs[0].at[d, n, matrix],
                        weight_ref.at[
                            matrix, pl.ds(d * rows, rows), pl.ds(n * cols, cols)
                        ],
                        sems.at[matrix],
                    )
                    copy.start()
                    copies.append(copy)
        return copies
    if len(piece_refs) == 1:
        copies = [
            pltpu.make_async_copy(piece_refs[0].at[m], weight_ref.at[m], sems.at[m])
            for m in range(3)
        ]
        for copy in copies:
            copy.start()
        return copies
    line, unused, rows, cols = piece_refs[0].shape
    lanes = cols // 2
    x, y, c = place_ref[0], place_ref[1], place_ref[2]
    column, one_y, two_x, one_x, two_y, one_xy, two_xy, column_c, next_c, far_c = piece_refs
    pieces = [
        (column, None, None, 0, 0, 0), (column_c, None, None, 0, 0, 1),
        (one_y, None, 0, 0, 1, 0), (two_x, None, 1, 1, 0, 0),
        (one_x, None, 0, 1, 0, 0), (two_y, None, 1, 0, 1, 0),
        (next_c, 0, 0, 0, 1, 1), (next_c, 1, 1, 1, 0, 1),
        (next_c, 2, 0, 1, 0, 1), (next_c, 3, 1, 0, 1, 1),
        (one_xy, None, 0, 1, 1, 0), (two_xy, None, 1, 1, 1, 0),
        (far_c, 0, 0, 1, 1, 1), (far_c, 1, 1, 1, 1, 1),
    ]
    copies = []
    for matrix in range(3):
        for ref, index, half, dx, dy, dc in pieces:
            width = cols if half is None else lanes
            narrow = (y ^ dy) * 2 + (c ^ dc)
            col = pl.multiple_of(narrow * cols + (half or 0) * lanes, 128)
            for z in range(line):
                row = pl.multiple_of((2 * z + (x ^ dx)) * rows, 16)
                source = ref.at[z, matrix] if index is None else ref.at[index, z, matrix]
                copy = pltpu.make_async_copy(
                    source,
                    weight_ref.at[matrix, pl.ds(row, rows), pl.ds(col, width)],
                    sems.at[matrix],
                )
                copy.start()
                copies.append(copy)
    return copies


def await_copies(copies, matrix):
    count = len(copies) // 3
    for copy in copies[matrix * count : (matrix + 1) * count]:
        copy.wait()


def run_block(values, near, attend, spread_ref, weight_ref, vec_ref, copies, keep):
    vec = lambda row: vec_ref[row : row + 1, :]
    frames = values.shape[0]
    mixed = position_sum(bf(values).astype(F32), near, spread_ref, False) + vec(7)
    hidden, norm_one = norm_fwd(values + gelu(mixed), vec(0), vec(1))
    hidden_low = bf(hidden)
    await_copies(copies, 0)
    triple = bf(mm(hidden_low, weight_ref[0, :, : 3 * D]))
    outs = []
    for pair in range(HEADS // 2):
        lo = pair * 2 * HEAD_DIM
        hi = lo + 2 * HEAD_DIM
        query = triple[:, lo:hi].astype(F32)
        key = triple[:, D + lo : D + hi]
        value = triple[:, 2 * D + lo : 2 * D + hi]
        both = []
        for upper in range(2):
            scores = mm_t(bf(lane_half(query, upper)), key) * (1.0 / math.sqrt(HEAD_DIM))
            scores = jnp.where(attend, scores, -1e30)
            raised = jnp.exp(scores - jnp.max(scores, axis=-1, keepdims=True))
            chances = raised / jnp.sum(raised, axis=-1, keepdims=True)
            if keep is not None:
                keep["chances"][2 * pair + upper] = chances
            both.append(lane_half(mm(bf(chances), value), upper))
        outs.append(bf(both[0] + both[1]))
    outs = jnp.concatenate(outs, axis=1)
    second, norm_two = norm_fwd(hidden + mm(outs, weight_ref[0, :, 3 * D :]), vec(2), vec(3))
    second_low = bf(second)
    await_copies(copies, 1)
    await_copies(copies, 2)
    total = second
    step = D
    for start in range(0, weight_ref.shape[2], step):
        wide = mm(second_low, weight_ref[1, :, start : start + step])
        inner = bf(gelu(wide))
        if keep is not None:
            keep["wide"][:, start : start + step] = wide
            keep["right"][2, :, start : start + step] = inner
        total = total + mm_t(inner, weight_ref[2, :, start : start + step])
    result, norm_three = norm_fwd(total, vec(4), vec(5))
    if keep is not None:
        keep["triple"][...] = triple
        keep["mixed"][...] = mixed
        keep["left"][0] = hidden_low
        keep["left"][1] = outs
        keep["left"][2] = second_low
        for index, kept in enumerate((norm_one, norm_two, norm_three)):
            keep["units"][index] = kept[0]
            keep["scales"][index] = jnp.broadcast_to(kept[1], (frames, 128))
    return result


def teacher_kernel(place_ref, feat_ref, near_ref, col_ref, row_ref, spread_ref, vec_ref, *refs):
    piece_refs, (target_ref, weight_ref, sems) = refs[:-3], refs[-3:]
    copies = start_copies(place_ref, piece_refs, weight_ref, sems)
    attend = col_ref[...] == row_ref[...]
    output = run_block(feat_ref[...], near_ref[...], attend, spread_ref, weight_ref, vec_ref,
                       copies, None)
    member = attend.astype(F32)
    clip_size = jnp.sum(member, axis=1, keepdims=True)
    average = jnp.dot(member, output, precision=HIGHEST, preferred_element_type=F32) / clip_size
    center = output - average
    spread = jnp.dot(
        member, center * center, precision=HIGHEST, preferred_element_type=F32
    ) / clip_size
    target_ref[...] = center * lax.rsqrt(jnp.maximum(spread, VAR_FLOOR))


def student_kernel(place_ref, feat_ref, near_ref, col_ref, row_ref, mask_ref, weight_one_ref,
                   spread_ref, vec_ref, target_ref, normed_ref, project_ref, head_ref, *refs):
    piece_refs, refs = refs[:-14], refs[-14:]
    (left_ref, right_ref, side_ref, vector_ref, normed_grad_ref, loss_ref,
     weight_ref, chance_ref, wide_ref, triple_ref, mixed_ref, unit_ref, scale_ref,
     sems) = refs
    copies = start_copies(place_ref, piece_refs, weight_ref, sems)
    vec = lambda row: vec_ref[row : row + 1, :]
    total_sum = lambda values: jnp.sum(values, axis=0, keepdims=True)
    attend = col_ref[...] == row_ref[...]
    near = near_ref[...]
    chosen = mask_ref[...] > 0.0
    values = jnp.where(chosen, vec(9), feat_ref[...])
    keep = {
        "chances": chance_ref, "wide": wide_ref, "right": right_ref, "triple": triple_ref,
        "mixed": mixed_ref, "left": left_ref, "units": unit_ref, "scales": scale_ref,
    }
    result = run_block(values, near, attend, spread_ref, weight_ref, vec_ref, copies, keep)
    kept = lambda index: (unit_ref[index], scale_ref[index, :, :1])
    student_low = bf(result)
    scale = weight_one_ref[0:1, 0:1]
    error = jnp.where(chosen, mm(student_low, head_ref[...]) + vec(8) - target_ref[...], 0.0)
    loss_ref[...] = jnp.broadcast_to(
        jnp.sum(total_sum(error * error), axis=1, keepdims=True) * scale, loss_ref.shape
    )
    predict_grad = error * (2.0 * scale)
    vector_ref[8:9, :] = total_sum(predict_grad)
    predict_low = bf(predict_grad)
    reach_end = CH + POS_K * WIDTH

    def put_side(first, values, group=slice(0, D)):
        if len(side_ref.shape) == 2:
            side_ref[group, first : first + values.shape[1]] = values
            return
        rows, width = side_ref.shape[2:]
        owners = slice(group.start // rows, group.stop // rows)
        for n in range(side_ref.shape[1]):
            low_end = max(first, n * width)
            high_end = min(first + values.shape[1], (n + 1) * width)
            if low_end < high_end:
                part = values[:, low_end - first : high_end - first]
                side_ref[owners, n, :, low_end - n * width : high_end - n * width] = part.reshape(
                    owners.stop - owners.start, rows, high_end - low_end
                )

    put_side(reach_end, t_mm(student_low, predict_low))
    grad = mm_t(predict_low, head_ref[...])

    def norm_step(grad, index):
        back, gain, shift = norm_bwd(kept(index), vec(2 * index), grad)
        vector_ref[2 * index : 2 * index + 1, :] = gain[None]
        vector_ref[2 * index + 1 : 2 * index + 2, :] = shift[None]
        return back

    grad = norm_step(grad, 2)
    down = bf(grad)
    left_ref[3] = down
    for start in range(0, weight_ref.shape[2], D):
        cols = slice(start, start + D)
        wide_grad = bf(mm(down, weight_ref[2, :, cols]) * gelu_slope(wide_ref[:, cols]))
        right_ref[1, :, cols] = wide_grad
        grad = grad + mm_t(wide_grad, weight_ref[1, :, cols])
    grad = norm_step(grad, 1)
    down = bf(grad)
    right_ref[0, :, 3 * D :] = down
    outs_grad = mm_t(down, weight_ref[0, :, 3 * D :])
    for pair in range(HEADS // 2):
        lo = pair * 2 * HEAD_DIM
        hi = lo + 2 * HEAD_DIM
        query = triple_ref[:, lo:hi]
        key = triple_ref[:, D + lo : D + hi]
        value = triple_ref[:, 2 * D + lo : 2 * D + hi]
        sums = [None, None, None]
        for upper in range(2):
            out_low = bf(lane_half(outs_grad[:, lo:hi], upper))
            chances = chance_ref[2 * pair + upper]
            chance_grad = mm_t(out_low, value)
            score_grad = chances * (
                chance_grad - jnp.sum(chance_grad * chances, axis=-1, keepdims=True)
            )
            score_grad = bf(score_grad * (1.0 / math.sqrt(HEAD_DIM)))
            parts = (
                lane_half(mm(score_grad, key), upper),
                lane_half(t_mm(score_grad, query), upper),
                t_mm(bf(chances), out_low),
            )
            for index in range(3):
                sums[index] = parts[index] if upper == 0 else sums[index] + parts[index]
        for index in range(3):
            right_ref[0, :, index * D + lo : index * D + hi] = bf(sums[index])
    grad = grad + mm_t(right_ref[0, :, : 3 * D], weight_ref[0, :, : 3 * D])
    grad = norm_step(grad, 0)
    mixed_grad = grad * gelu_slope(mixed_ref[...])
    vector_ref[7:8, :] = total_sum(mixed_grad)
    mixed_low = bf(mixed_grad)
    grad = grad + position_sum(mixed_low.astype(F32), near, spread_ref, True)
    shifted = bf(values).astype(F32)
    half = D // 2
    for offset in range(POS_K):
        taps = taps_of(shifted, near, offset, False)
        for part in range(2):
            cols = slice(part * half, (part + 1) * half)
            full = t_mm(taps[:, cols], mixed_low[:, cols])
            pieces = [
                full[g * WIDTH : (g + 1) * WIDTH, g * WIDTH : (g + 1) * WIDTH]
                for g in range(half // WIDTH)
            ]
            put_side(CH + offset * WIDTH, jnp.concatenate(pieces, axis=0), cols)
    vector_ref[9:10, :] = total_sum(jnp.where(chosen, grad, 0.0))
    grad = jnp.where(chosen, 0.0, grad)
    vector_ref[6:7, :] = total_sum(grad)
    feat_low = bf(grad)
    put_side(0, t_mm(feat_low, normed_ref[...]))
    normed_grad_ref[...] = mm(feat_low, project_ref[...])


def spread_kernel(side_ref, tile_ref, spread_ref):
    half = D // 2
    rows = lax.broadcasted_iota(jnp.int32, (half, half), 0) // WIDTH
    cols = lax.broadcasted_iota(jnp.int32, (half, half), 1) // WIDTH
    same = rows == cols
    for offset in range(POS_K):
        piece = side_ref[:, offset * WIDTH : (offset + 1) * WIDTH]
        for part in range(2):
            wide = mm(piece[part * half : (part + 1) * half], tile_ref[...])
            spread_ref[offset, part * half : (part + 1) * half, :] = bf(
                jnp.where(same, wide, 0.0)
            )


def block_grad_kernel(place_ref, left_ref, left_two_ref, right_ref, right_two_ref,
                      send_top_ref, keep_top_ref, send_low_ref, keep_low_ref, full_ref):
    unused, line, unused_two, half, cols = keep_top_ref.shape
    x = place_ref[0]
    far = pl.program_id(1)
    full_ref[...] = t_mm(left_ref[0], right_ref[0]) + t_mm(left_two_ref[0], right_two_ref[0])
    for z in range(line):
        start = lambda index: pl.multiple_of((2 * z + index) * 2 * half, 8)
        keep_top_ref[0, z, 0] = full_ref[pl.ds(start(x), half), :]
        send_top_ref[0, z, 0] = bf(full_ref[pl.ds(start(1 - x), half), :])

    @pl.when(far == 0)
    def _():
        for z in range(line):
            for index in range(2):
                row = (2 * z + index) * 2 * half + half
                keep_low_ref[index, z, 0] = full_ref[row : row + half, :]

    @pl.when(far == 1)
    def _():
        for z in range(line):
            for index in range(2):
                row = (2 * z + index) * 2 * half + half
                send_low_ref[index, z, 0] = bf(full_ref[row : row + half, :])


def block_grads(left, left_two, right, right_two, place, n_dp, n_narrow):
    frames = left.shape[1]
    cols = right.shape[2] // n_narrow
    half = D // n_dp // 2
    line = n_dp // 2
    shape = jax.ShapeDtypeStruct

    def narrow(far, place):
        return 2 * (place[1] ^ far) + place[2]

    def left_index(matrix, far, place):
        is_out = (narrow(far, place) + 1) * cols > 3 * D
        return (jnp.where(matrix == 0, jnp.where(is_out, 1, 0), matrix + 1), 0, 0)

    left_spec = pl.BlockSpec((1, frames, D), left_index)
    right_spec = pl.BlockSpec(
        (1, frames, cols), lambda matrix, far, place: (matrix, 0, narrow(far, place))
    )
    top_spec = pl.BlockSpec(
        (1, line, 1, half, cols), lambda matrix, far, place: (place[1] ^ far, 0, matrix, 0, 0)
    )
    low_spec = pl.BlockSpec(
        (2, line, 1, half, cols), lambda matrix, far, place: (0, 0, matrix, 0, 0)
    )
    whole = (2, line, 3, half, cols)
    return pl.pallas_call(
        block_grad_kernel,
        grid_spec=pltpu.PrefetchScalarGridSpec(
            num_scalar_prefetch=1,
            grid=(3, 2),
            in_specs=[left_spec, left_spec, right_spec, right_spec],
            out_specs=[top_spec, top_spec, low_spec, low_spec],
            scratch_shapes=[pltpu.VMEM((D, cols), F32)],
        ),
        out_shape=[shape(whole, BF16), shape(whole, F32), shape(whole, BF16), shape(whole, F32)],
        name="block_grads",
    )(place, left, left_two, right, right_two)


def plain_weight_grads(left, right, n_dp, n_narrow):
    full = [
        jnp.concatenate(
            [t_mm(left[0], right[0, :, : 3 * D]), t_mm(left[1], right[0, :, 3 * D :])], axis=1
        ),
        t_mm(left[2], right[1]),
        t_mm(left[3], right[2]),
    ]
    full = jnp.stack(full, 0)
    full = full.reshape(3, n_dp, D // n_dp, n_narrow, full.shape[2] // n_narrow)
    return full.transpose(1, 3, 0, 2, 4)


def spread_kernels(side_conv):
    tile = np.zeros((WIDTH, D // 2), np.float32)
    for column in range(D // 2):
        tile[column % WIDTH, column] = 1.0
    return pl.pallas_call(
        spread_kernel,
        in_specs=[VMEM, VMEM],
        out_specs=VMEM,
        out_shape=jax.ShapeDtypeStruct((POS_K, D, D // 2), BF16),
        name="spread",
        compiler_params=pltpu.CompilerParams(vmem_limit_bytes=LIMIT),
    )(side_conv, jnp.asarray(tile, BF16))


def flat_pieces(pieces):
    if isinstance(pieces, list):
        return pieces, pieces[0].shape[-1] * 4
    return [pieces], pieces.shape[-1] * (pieces.shape[1] if pieces.ndim == 5 else 1)


def teacher_target(feats, near, col, row, spread, vec, pieces, place):
    pieces, width = flat_pieces(pieces)
    return pl.pallas_call(
        teacher_kernel,
        in_specs=[SMEM] + [VMEM] * 6 + [ANY] * len(pieces),
        out_specs=VMEM,
        out_shape=jax.ShapeDtypeStruct(feats.shape, F32),
        scratch_shapes=[pltpu.VMEM((3, D, width), BF16), pltpu.SemaphoreType.DMA((3,))],
        name="teacher",
        compiler_params=pltpu.CompilerParams(vmem_limit_bytes=LIMIT),
    )(place, feats, near, col, row, spread, vec, *pieces)


def student_step(feats, near, col, row, mask, weight, spread, vec, target, normed, project, head,
                 pieces, place, side_shape):
    pieces, width = flat_pieces(pieces)
    frames = feats.shape[0]
    shape = jax.ShapeDtypeStruct
    return pl.pallas_call(
        student_kernel,
        in_specs=[SMEM] + [VMEM] * 12 + [ANY] * len(pieces),
        out_specs=[VMEM] * 6,
        out_shape=[
            shape((4, frames, D), BF16),
            shape((3, frames, width), BF16),
            shape(side_shape, F32),
            shape((10, D), F32),
            shape((frames, CH), F32),
            shape((8, 128), F32),
        ],
        scratch_shapes=[
            pltpu.VMEM((3, D, width), BF16),
            pltpu.VMEM((HEADS, frames, frames), F32),
            pltpu.VMEM((frames, width), F32),
            pltpu.VMEM((frames, 3 * D), BF16),
            pltpu.VMEM((frames, D), F32),
            pltpu.VMEM((3, frames, D), F32),
            pltpu.VMEM((3, frames, 128), F32),
            pltpu.SemaphoreType.DMA((3,)),
        ],
        name="student",
        compiler_params=pltpu.CompilerParams(vmem_limit_bytes=LIMIT),
    )(
        place, feats, near, col, row, mask, weight, spread, vec, target, normed, project, head,
        *pieces,
    )


class Links:
    def __init__(self, n_dp, n_narrow):
        self.n_dp, self.n_narrow = n_dp, n_narrow
        self.line = n_dp // 2
        self.direct = n_narrow == 4 and n_dp % 2 == 0 and 4 * self.line == sum(KERNELS)
        dp, narrow = lax.axis_index("dp"), lax.axis_index("narrow")
        self.z, self.x, self.y, self.c = dp // 2, dp % 2, narrow // 2, narrow % 2

    def swap_c(self, values):
        return self.flip(values, "narrow", 1)

    def swap_y(self, values):
        return self.flip(values, "narrow", 2)

    def swap_x(self, values):
        return self.flip(values, "dp", 1)

    def flip(self, values, axis, bit):
        size = self.n_dp if axis == "dp" else self.n_narrow
        return lax.ppermute(values, axis, [(i, i ^ bit) for i in range(size)])

    def step_z(self, values, up, senders):
        move = 1 if up else -1
        pairs = [(2 * z + x, 2 * (z + move) + x) for z in senders for x in range(2)]
        return lax.ppermute(values, "dp", pairs)

    def total(self, values, axes=("narrow", "dp")):
        for axis in axes:
            size = self.n_dp if axis == "dp" else self.n_narrow
            if size & (size - 1):
                values = lax.psum(values, axis)
                continue
            bit = 1
            if (size.bit_length() - 1) % 2:
                values = values + self.flip(values, axis, bit)
                bit = 2
            while bit < size:
                near, far, both = (self.flip(values, axis, bit * k) for k in (1, 2, 3))
                values = (values + near) + (far + both)
                bit *= 4
        return values

    def go(self, requests):
        results = []
        for request in requests:
            kind, values = request[0], request[1]
            if kind == "c":
                results.append(self.flip(values, "narrow", 1))
            elif kind == "y":
                results.append(self.flip(values, "narrow", 2))
            elif kind == "x":
                results.append(self.flip(values, "dp", 1))
            else:
                results.append(self.step_z(values, kind == "up", request[2]))
        return results

    def gather_steps(self, values):
        last = self.line - 1
        ups, downs = [], []
        up = down = values
        for hop in range(1, self.line):
            up, down = yield [
                ("up", up, range(hop - 1, last)),
                ("down", down, range(1, self.line - hop + 1)),
            ]
            ups.append(up)
            downs.append(down)
        stacked = jnp.stack(ups[::-1] + [values] + downs, 0)
        column = lax.dynamic_slice_in_dim(stacked, last - self.z, self.line, 0)
        lanes = values.shape[-1] // 2
        one, two = column[..., :lanes], column[..., lanes:]
        one_y, two_x, one_x, two_y, column_c = yield [
            ("y", one), ("x", two), ("x", one), ("y", two), ("c", column)
        ]
        next_c = jnp.stack([one_y, two_x, one_x, two_y], 0)
        one_xy, two_xy, next_c = yield [("x", one_y), ("y", two_x), ("c", next_c)]
        (far_c,) = yield [("c", jnp.stack([one_xy, two_xy], 0))]
        return [column, one_y, two_x, one_x, two_y, one_xy, two_xy, column_c, next_c, far_c]

    def gather_whole(self, values):
        if not self.direct:
            whole = lax.all_gather(values, "narrow", axis=2, tiled=True)
            return lax.all_gather(whole, "dp", axis=1, tiled=True)
        whole = lax.all_gather(values, ("dp", "narrow"), axis=0)
        return whole.reshape((self.n_dp, self.n_narrow) + values.shape)

    def scatter_steps(self, parts):
        send, keep = parts
        half = send.shape[-2] // 2
        pick = lambda array, axis, index: lax.dynamic_index_in_dim(array, index, axis, False)
        (got,) = yield [("c", send)]

        def both(rows, axis, index):
            return pick(keep[..., rows, :], axis, index) + pick(got[..., rows, :], axis, index)

        top, low_rows = slice(0, half), slice(half, None)
        ends = yield [
            ("x", both(top, 0, 1 - self.x)), ("y", both(low_rows, 1, 1 - self.y))
        ]

        def all_three(rows, first, at_first, second, at_second, end):
            mine = [
                pick(pick(array[..., rows, :], first, at_first), second, at_second)
                for array in (keep, got)
            ]
            return mine[0] + mine[1] + pick(end, second, at_second)

        top_of = lambda index: all_three(top, 0, self.x, 0, index, ends[0])
        low_of = lambda index: all_three(low_rows, 1, self.y, 0, index, ends[1])
        more = yield [("y", top_of(1 - self.y)), ("x", low_of(1 - self.x))]
        one = top_of(self.y) + more[0]
        two = low_of(self.x) + more[1]
        return (yield from self.line_steps(jnp.concatenate([one, two], axis=-2)))

    def half_steps(self, send_top, keep_top, send_low, keep_low):
        pick = lambda array, index: lax.dynamic_index_in_dim(array, index, 0, False)
        top, lower = yield [("x", send_top), ("y", send_low)]
        top_of = lambda index: pick(keep_top, index) + pick(top, index).astype(F32)
        low_of = lambda index: pick(keep_low, index) + pick(lower, index).astype(F32)
        more = yield [("y", top_of(1 - self.y)), ("x", low_of(1 - self.x))]
        one, two = top_of(self.y) + more[0], low_of(self.x) + more[1]
        return (yield from self.line_steps(jnp.concatenate([one, two], axis=-2)))

    def line_steps(self, column):
        pick = lambda array, axis, index: lax.dynamic_index_in_dim(array, index, axis, False)
        last = self.line - 1
        at = lambda offset: pick(column, 0, (self.z + offset) % self.line)
        up = down = None
        for hop in range(last, 0, -1):
            send_up = at(hop) if up is None else at(hop) + up
            send_down = at(-hop) if down is None else at(-hop) + down
            up, down = yield [
                ("up", send_up, range(0, last - hop + 1)),
                ("down", send_down, range(hop, self.line)),
            ]
        own = at(0)
        return own if up is None else own + up + down


class Stages:
    def __init__(self, links, steps):
        self.links, self.steps = links, list(steps)
        self.requests = [next(one) for one in self.steps]
        self.results = [None] * len(self.steps)

    def tie(self, *others):
        arrays = [[request[1] for request in one] for one in self.requests]
        arrays, others = lax.optimization_barrier((arrays, others))
        self.requests = [
            [(request[0], array) + tuple(request[2:]) for request, array in zip(one, part)]
            for one, part in zip(self.requests, arrays)
        ]
        return others if len(others) != 1 else others[0]

    def add(self, one):
        self.steps.append(one)
        self.requests.append(next(one))
        self.results.append(None)

    def advance(self, after=()):
        got = [self.links.go(one) for one in self.requests]
        if after:
            got, after = lax.optimization_barrier((got, tuple(after)))
        for index, one in enumerate(self.steps):
            if not self.requests[index]:
                continue
            try:
                self.requests[index] = one.send(got[index])
            except StopIteration as stop:
                self.requests[index] = []
                self.results[index] = stop.value
        return after if len(after) != 1 else after[0]

    def finish(self):
        while any(self.requests):
            self.advance()
        return self.results


def adamw(weight, grad, first, second, power):
    first = DECAY * first + (1.0 - DECAY) * grad
    second = DECAY * second + (1.0 - DECAY) * grad * grad
    unbias = 1.0 - power
    step_size = first / unbias / (jnp.sqrt(second / unbias) + 1e-08)
    return (weight - LR_ADAM * (step_size + WEIGHT_DECAY * weight), first, second)


def exact(left, right):
    return jnp.einsum("brs,bst->brt", left, right, precision=HIGHEST)


def orthogonal(blocks, gram_total):
    gram = gram_total(jnp.einsum("brc,bsc->brs", blocks, blocks, precision=HIGHEST))
    scales = 1.0 / (jnp.sqrt(jnp.trace(gram, axis1=1, axis2=2)) + 1e-07)
    gram = gram * (scales * scales)[:, None, None]
    eye = jnp.eye(gram.shape[1], dtype=F32)[None]
    whole = None
    for iteration in range(5):
        square = exact(gram, gram)
        step = COEFF_A * eye + COEFF_B * gram + COEFF_C * square
        whole = step if whole is None else exact(step, whole)
        if iteration < 4:
            gram = exact(exact(step, gram), step)
            gram = 0.5 * (gram + gram.transpose(0, 2, 1))
    return exact(whole * scales[:, None, None], blocks)


def per_device(
    wave,
    clip_ids,
    span_starts,
    step_count,
    conv_small,
    conv_stack,
    side,
    vectors,
    block,
    teacher_block,
    teacher_vectors,
    small_mean,
    small_square,
    stack_mean,
    stack_square,
    side_mean,
    side_square,
    vector_mean,
    vector_square,
    block_momentum,
    n_dp,
    n_narrow,
):
    everyone = ("dp", "narrow")
    frames = clip_ids.shape[0]
    rows_here, cols_here = block.shape[1:]
    side_rows, side_cols = side.shape
    links = Links(n_dp, n_narrow)
    place = jnp.stack([links.x, links.y, links.c]).astype(jnp.int32)
    stack_rows_here = conv_stack.shape[0]
    side_size = side_rows * side_cols
    side_lines = -(-side_size // CH)
    lines = -(-(stack_rows_here + side_lines) // 16) * 16
    side_flat = jnp.pad(bf(side).reshape(-1), (0, side_lines * CH - side_size))
    send = jnp.concatenate(
        [
            bf(conv_stack),
            side_flat.reshape(side_lines, CH),
            jnp.zeros((lines - stack_rows_here - side_lines, CH), BF16),
        ],
        axis=0,
    )
    stack = lax.all_gather(send, everyone, axis=0)
    teacher_pieces = links.gather_whole(bf(teacher_block))
    masked = masked_of(span_starts)
    masked_here = jnp.full((1, 128), jnp.sum(masked.astype(F32)), F32)
    masked_all = links.total(masked_here)
    small_low = low(conv_small)
    vector_low = low(vectors)
    taps = first_taps(wave, frames)
    first_weights, hidden, hidden_tail = first_layer(small_low, taps, frames)
    whole_side = stack[:, stack_rows_here : stack_rows_here + side_lines].reshape(
        n_dp * n_narrow, side_lines * CH
    )[:, :side_size]
    whole_side = (
        whole_side.reshape(n_dp, n_narrow, side_rows, side_cols)
        .transpose(0, 2, 1, 3)
        .reshape(n_dp * side_rows, n_narrow * side_cols)
    )
    spread_of = lambda: spread_kernels(whole_side[:, CH : CH + POS_K * WIDTH])
    if links.direct:
        exchange = Stages(links, [links.gather_steps(bf(block))])
        hidden = exchange.advance((hidden,))
        for unused in range(links.line - 2):
            exchange.advance()
        hidden = exchange.tie(hidden)
        hidden, masked_all = lax.optimization_barrier((hidden, masked_all))
        outs = encode_fwd(small_low, stack, hidden, hidden_tail, frames)
        outs = list(outs)
        outs[13] = exchange.advance((outs[13],))
        whole_side = exchange.tie(whole_side)
        spread = spread_of()
    else:
        student_pieces = links.gather_whole(bf(block))
        outs = encode_fwd(small_low, stack, hidden, hidden_tail, frames)
        spread = spread_of()
    normed = outs[13]
    project = whole_side[:, :CH]
    head = whole_side[:, CH + POS_K * WIDTH :]
    near = jnp.pad(neighbours(clip_ids).astype(F32).T, ((0, 0), (0, 32 - POS_K)))
    col, row = clip_ids[:, None], clip_ids[None, :]
    feats = mm_t(normed, project) + vector_low[6]
    target = teacher_target(
        feats, near, col, row, spread, low(teacher_vectors), teacher_pieces, place
    )
    if links.direct:
        target = exchange.advance((target,))
        (student_pieces,) = exchange.finish()
    total = jnp.maximum(masked_all[0, 0], 1.0)
    weight = jnp.full((8, 128), 1.0 / (total * math.sqrt(D)), F32)
    left, right, side_grad, vector_grad, normed_grad, loss_tile = student_step(
        feats,
        near,
        col,
        row,
        masked.astype(F32)[:, None],
        weight,
        spread,
        vector_low,
        target,
        normed,
        project,
        head,
        student_pieces,
        place,
        (n_dp, n_narrow, side_rows, side_cols)
        if links.direct
        else (n_dp * side_rows, n_narrow * side_cols),
    )
    loss_part = loss_tile[0, 0]
    devices = n_dp * n_narrow
    if links.direct:
        core = links.c.astype(jnp.int32).reshape(1)
        order = [tap // 2 % 2 * 8 + tap % 2 * 4 + tap // 4 for tap in range(sum(KERNELS))]
        others = [links.swap_c(left), links.swap_c(right)]
        side_piece = lax.psum_scatter(
            side_grad.reshape(devices * side_rows, side_cols),
            everyone,
            scatter_dimension=0,
            tiled=True,
        )
        grads = block_grads(left, others[0], right, others[1], place, n_dp, n_narrow)
        feed = Stages(links, [links.half_steps(*grads)])
        normed_grad = feed.tie(normed_grad)
        *parts, second, second_tail, norm_grad = encode_back(
            order, core, list(outs), small_low, stack, frames, normed_grad
        )
        parts = second_dw(order, core, second, second_tail, hidden, hidden_tail, parts)
        parts = feed.advance(tuple(parts))
        second = feed.tie(second)
        shape = (2, 2, links.line) + conv_stack.shape
        last = Stages(links, [links.scatter_steps([part.reshape(shape) for part in parts])])
        second = last.tie(second)
        second = last.advance((second,))
        second = last.tie(second)
        second = feed.advance((second,))
        second = feed.tie(second)
        tap_grad = second_dx(second, second_tail, stack, taps, first_weights, frames)
        for one in (feed, last, feed, last):
            tap_grad = one.advance((tap_grad,))
            tap_grad = one.tie(tap_grad)
        (block_piece,) = feed.finish()
        (stack_piece,) = last.finish()
    else:
        sums = lambda values: lax.psum_scatter(
            values.reshape((-1,) + values.shape[-1:]), everyone, scatter_dimension=0, tiled=True
        )
        block_piece = sums(plain_weight_grads(left, right, n_dp, n_narrow))
        block_piece = block_piece.reshape(3, rows_here, cols_here)
        side_grad = side_grad.reshape(n_dp, side_rows, n_narrow, side_cols)
        side_piece = sums(side_grad.transpose(0, 2, 1, 3))
        core = jnp.zeros((1,), jnp.int32)
        order = list(range(sum(KERNELS)))
        *parts, second, second_tail, norm_grad = encode_back(
            order, core, list(outs), small_low, stack, frames, normed_grad
        )
        parts = second_dw(order, core, second, second_tail, hidden, hidden_tail, parts)
        tap_grad = second_dx(second, second_tail, stack, taps, first_weights, frames)
        stack_piece = sums(jnp.stack([parts[1], parts[0]], 1).reshape(sum(KERNELS) * CH, CH))
    small_grad = jnp.concatenate([tap_grad[:10], norm_grad], axis=0)
    packed = jnp.concatenate(
        [
            vector_grad,
            small_grad.reshape(-1, D),
            jnp.full((1, D), loss_part, F32),
        ],
        axis=0,
    )
    packed = links.total(packed)
    vector_total = packed[:10]
    small_total = packed[10:-1].reshape(small_grad.shape)
    loss_value = packed[-1, 0]
    shard_squares = (
        jnp.sum(block_piece * block_piece)
        + jnp.sum(side_piece * side_piece)
        + jnp.sum(stack_piece * stack_piece)
    )
    grad_norm = jnp.sqrt(
        links.total(jnp.full((1, 128), shard_squares, F32))[0, 0]
        + jnp.sum(small_total * small_total)
        + jnp.sum(vector_total * vector_total)
    )
    factor = jnp.minimum(1.0, CLIP_LIMIT / (grad_norm + 1e-06))
    power = jnp.power(DECAY, step_count[0].astype(F32))
    small_next = adamw(conv_small, factor * small_total, small_mean, small_square, power)
    stack_next = adamw(conv_stack, factor * stack_piece, stack_mean, stack_square, power)
    side_next = adamw(side, factor * side_piece, side_mean, side_square, power)
    vector_next = adamw(vectors, factor * vector_total, vector_mean, vector_square, power)
    momentum = DECAY * block_momentum + factor * block_piece
    ortho = orthogonal(momentum, lambda gram: links.total(gram, ("narrow",)))
    block_next = block * (1.0 - LR_MUON * WEIGHT_DECAY) - LR_MUON * ortho
    teacher_next = EMA_RATE * teacher_block + (1.0 - EMA_RATE) * block_next
    teacher_vec_next = EMA_RATE * teacher_vectors + (1.0 - EMA_RATE) * vector_next[0]
    return (
        (loss_value, grad_norm)
        + small_next
        + stack_next
        + side_next
        + vector_next
        + (block_next, momentum, teacher_next, teacher_vec_next, bf(block_next))
    )


def solution(mesh):
    n_dp, n_narrow = mesh.shape["dp"], mesh.shape["narrow"]

    def step(*arguments):
        return per_device(*arguments, n_dp, n_narrow)

    rows = P(("dp", "narrow"), None)
    flat = P(("dp", "narrow"))
    grid = P("dp", "narrow")
    cube = P(None, "dp", "narrow")
    one = P()
    in_specs = (
        (flat, flat, flat, one, one, rows, grid, one, cube, cube, one, one, one)
        + (rows, rows, grid, grid, one, one, cube)
    )
    out_specs = (
        (one, one, one, one, one, rows, rows, rows, grid, grid, grid, one, one, one)
        + (cube, cube, cube, one, cube)
    )
    return jax.shard_map(
        step, mesh=mesh, in_specs=in_specs, out_specs=out_specs, check_vma=False
    )
```
